32 devices in a mesh: chaos: 8 (over z, x), space: 4 (over y, core).
Axes of the slice: x: 2, y: 2, z: 4, core: 2. Of those that a mesh axis runs over, the one named last changes fastest.
Arguments:
- coeffs: float32 [64, 16, 32, 128], P('chaos', 'space'), may hold values from -6 to 6
- source: float32 [64, 16, 32, 128], P('chaos', 'space'), may hold values from -6 to 6
- mean_field: float32 [16, 32, 128], P('space'), may hold values from 0.5 to 2
- mode_bank: float32 [8, 16, 32, 128], P('chaos', 'space'), may hold values from -2.4 to 2.4
- mode_owner: int32 [2], replicated, may hold values from 0 to 7, as said below
- links: int32 [8, 32, 4], P('chaos'), may hold values from 0 to 63, as said below
Outputs:
- residual: float32 [64, 16, 32, 128], P('chaos', 'space')
- correction: float32 [64, 16, 32, 128], P('chaos', 'space')
The draws below stay inside these ranges and needn't reach their ends.
Inputs may be any that keep to these rules, and one draw needn't show every extreme that they name: `mode_owner`: 2 distinct slots. Entry (s, p, k, L) of links[d]: s a coefficient among device d's 8, p a global destination coefficient, k a mode, L a level from 0 to 3, where level 0 marks a pair that is absent. Every pair appears in both directions with one level. One device's list names coefficients of one destination device at most 5 times, and some device's list does so exactly 5 times with all those entries present.
All inputs are finite; a program needn't handle non-finite values.
Results may differ from the reference program's by a relative error of at most 0.00015.
Values sent between devices are 32-bit elements; how exact they have to be, the bound alone decides.
No kernel may reach another device: no remote copies, remote signals or barrier semaphores. Data moves between devices by JAX's collectives and lax.ppermute only.
A program may use at most 128 MiB of HBM per device.

```python
import math
import jax
import jax.numpy as jnp
from jax import lax

M = 2
COEF_DEV = 8
NX = 32
NY = 128
ITERS = 4
COEFS = 64
NZ = 16
N_CHAOS = 8


def draw_mode_owner(key, part):
    pick_key, order_key = jax.random.split(key, 2)
    others = jax.random.permutation(pick_key, N_CHAOS - 1)[:M - 1]
    owners = jnp.concatenate([others, jnp.full((1,), N_CHAOS - 1, dtype=others.dtype)])
    order = jax.random.permutation(order_key, M)
    return owners[order].astype(jnp.int32)


def draw_links(key, part):
    shift_key, perm_key, low_key, high_key, order_key = jax.random.split(key, 5)
    shift_range = N_CHAOS // 2 - 1
    raise_count = M * COEF_DEV
    other_shifts = jax.random.permutation(shift_key, shift_range) + 1
    link_index = jnp.arange(raise_count)
    cycle_index = (link_index - 1) % shift_range
    shift_flat = jnp.where(link_index == 0, N_CHAOS // 2, other_shifts[cycle_index])
    shift_table = shift_flat.reshape(M, COEF_DEV)
    local_perm = jax.vmap(lambda sub_key: jax.random.permutation(sub_key, COEF_DEV))(jax.random.split(perm_key, M))
    forced = ((link_index == 0) | (cycle_index == 0)).reshape(M, COEF_DEV)
    low_levels = jax.random.randint(low_key, (M, N_CHAOS, COEF_DEV), 0, 4)
    high_levels = jax.random.randint(high_key, (M, N_CHAOS, COEF_DEV), 1, 4)
    levels = jnp.where(forced[:, None, :], high_levels, low_levels)
    full_shape = (N_CHAOS, M, COEF_DEV)
    device_ids = jnp.arange(N_CHAOS)[:, None, None]
    local_ids = jnp.broadcast_to(jnp.arange(COEF_DEV)[None, None, :], full_shape)
    mode_ids = jnp.broadcast_to(jnp.arange(M)[None, :, None], full_shape)
    raise_dst = (device_ids + shift_table[None]) % N_CHAOS * COEF_DEV + local_perm[None]
    raise_level = jnp.transpose(levels, (1, 0, 2))
    anchor = (device_ids - shift_table[None]) % N_CHAOS
    lower_src = jnp.broadcast_to(local_perm[None], full_shape)
    lower_dst = anchor * COEF_DEV + local_ids
    lower_level = levels[mode_ids, anchor, local_ids]
    raise_part = jnp.stack([local_ids, jnp.broadcast_to(raise_dst, full_shape), mode_ids, raise_level], axis=-1)
    lower_part = jnp.stack([lower_src, lower_dst, mode_ids, lower_level], axis=-1)
    entries = jnp.concatenate([raise_part.reshape(N_CHAOS, raise_count, 4), lower_part.reshape(N_CHAOS, raise_count, 4)], axis=1)
    order = jax.vmap(lambda sub_key: jax.random.permutation(sub_key, 2 * raise_count))(jax.random.split(order_key, N_CHAOS))
    entries = jnp.take_along_axis(entries, order[:, :, None], axis=1)
    return entries.astype(jnp.int32)


def block_levels(own_key, shape, cuts, low, high):
    level, own = 1.0, jax.random.fold_in(own_key, 6)
    for dim, shards_of in cuts:
        steps = jnp.exp(jax.random.uniform(jax.random.fold_in(own, dim), (shards_of,), jnp.float32, low / len(cuts), high / len(cuts)))
        level = level * jnp.repeat(steps, shape[dim] // shards_of).reshape([-1 if axis == dim else 1 for axis in range(len(shape))])
    return level


def gaussian(own_key, extent, spread, limit, shards=(), kind=jnp.bfloat16):
    array = spread * jax.random.normal(own_key, extent, jnp.float32)
    if shards:
        array = array * block_levels(own_key, extent, shards, -0.22, 0.18)
    return jnp.clip(array, -limit, limit).astype(kind)


def setup_inputs(seed: int = 0) -> dict:
    splits = jax.random.split(jax.random.key(seed), 7)
    coeffs = gaussian(splits[0], (COEFS, NZ, NX, NY), 1.0, 6.0, ((0, 8), (1, 4)), jnp.float32)
    source = gaussian(splits[1], (COEFS, NZ, NX, NY), 1.0, 6.0, ((0, 8), (1, 4)), jnp.float32)
    mean_field = jnp.clip(jnp.exp(math.log(2.0) - 1.3862944 * jax.random.uniform(splits[2], (NZ, NX, NY), jnp.float32) ** block_levels(splits[2], (NZ, NX, NY), ((0, 4),), -0.2, 0.2)), 0.5, 2.0)
    mode_bank = gaussian(splits[3], (N_CHAOS, NZ, NX, NY), 0.4, 2.4, ((0, 8), (1, 4)), jnp.float32)
    mode_owner = draw_mode_owner(jax.random.fold_in(splits[6], 71), 0)
    links = draw_links(jax.random.fold_in(splits[6], 71), 0)
    return dict(coeffs=coeffs, source=source, mean_field=mean_field, mode_bank=mode_bank, mode_owner=mode_owner, links=links)


REACTION = 0.5
BOUND_LOW = 0.04
BOUND_HIGH = 2.0

def neighbour(values, along_axis, offset):
    along_axis = along_axis % values.ndim
    length = values.shape[along_axis]
    zero_rim = jnp.zeros_like(lax.slice_in_dim(values, 0, 1, axis=along_axis))
    if offset > 0:
        return jnp.concatenate([lax.slice_in_dim(values, 1, length, axis=along_axis), zero_rim], axis=along_axis)
    return jnp.concatenate([zero_rim, lax.slice_in_dim(values, 0, length - 1, axis=along_axis)], axis=along_axis)

def neighbour_pairs(values, diffusion):
    centre = values[..., 1:-1, :, :]
    own_coef = diffusion[..., 1:-1, :, :]
    listing = [(values[..., 2:, :, :], diffusion[..., 2:, :, :]), (values[..., :-2, :, :], diffusion[..., :-2, :, :])]
    for along_axis in (-2, -1):
        for offset in (1, -1):
            listing.append((neighbour(centre, along_axis, offset), neighbour(own_coef, along_axis, offset)))
    return (centre, own_coef, listing)

def stencil(values, diffusion):
    centre, own_coef, listing = neighbour_pairs(values, diffusion)
    running = None
    for other_cell, near_coef in listing:
        term = 0.5 * (own_coef + near_coef) * (centre - other_cell)
        running = term if running is None else running + term
    return running

def face_total(diffusion):
    centre, own_coef, listing = neighbour_pairs(diffusion, diffusion)
    running = None
    for other_cell, near_coef in listing:
        term = 0.5 * (own_coef + near_coef)
        running = term if running is None else running + term
    return running

def pad_depth(values):
    widths = [(0, 0)] * (values.ndim - 3) + [(1, 1), (0, 0), (0, 0)]
    return jnp.pad(values, widths)

def reference(coeffs, source, mean_field, mode_bank, mode_owner, links):
    mode_fields = mode_bank[mode_owner]
    coef_pad = pad_depth(coeffs)
    mean_pad = pad_depth(mean_field)
    mode_pad = pad_depth(mode_fields)
    base_apply = REACTION * coeffs + stencil(coef_pad, mean_pad)
    products = stencil(coef_pad[None], mode_pad[:, None])
    flat_products = products.reshape(M * COEFS, NZ * NX * NY)

    def add_device(device, accumulated):
        entries = lax.dynamic_index_in_dim(links, device, 0, keepdims=False)
        payload_row = entries[:, 2] * COEFS + device * COEF_DEV + entries[:, 0]
        weight = jnp.sqrt(entries[:, 3].astype(jnp.float32))
        return accumulated.at[entries[:, 1]].add(weight[:, None] * flat_products[payload_row])
    coupling = lax.fori_loop(0, N_CHAOS, add_device, jnp.zeros((COEFS, NZ * NX * NY), jnp.float32))
    coupling = coupling.reshape(coeffs.shape)
    residual = source - (base_apply + coupling)
    diagonal = REACTION + face_total(mean_pad)
    midpoint = (BOUND_HIGH + BOUND_LOW) / 2.0
    halfwidth = (BOUND_HIGH - BOUND_LOW) / 2.0
    spread_ratio = midpoint / halfwidth
    update = residual / (midpoint * diagonal)
    ratio_now = 1.0 / spread_ratio
    solution = jnp.zeros_like(residual)
    remainder = residual
    for sweep_index in range(ITERS):
        solution = solution + update
        if sweep_index + 1 < ITERS:
            remainder = remainder - (REACTION * update + stencil(pad_depth(update), mean_pad))
            ratio_next = 1.0 / (2.0 * spread_ratio - ratio_now)
            update = ratio_next * ratio_now * update + 2.0 * ratio_next / halfwidth * remainder / diagonal
            ratio_now = ratio_next
    return (residual, solution)
```

```python
import functools
import math

import jax
import jax.numpy as jnp
from jax import lax
from jax.experimental import pallas as pl
from jax.experimental.pallas import tpu as pltpu
from jax.sharding import PartitionSpec as P

M = 2
ITERS = 4

REACTION = 0.5
BOUND_LOW = 0.04
BOUND_HIGH = 2.0

CHUNKS = 2
TABLE_ROWS = 8


VMEM = pl.BlockSpec(memory_space=pltpu.VMEM)
SMEM = pl.BlockSpec(memory_space=pltpu.SMEM)


def cost(planes, nx, ny, flops):
    return pl.CostEstimate(
        flops=flops * planes * nx * ny, bytes_accessed=8 * planes * nx * ny, transcendentals=0
    )


def shifted(values, axis, step):
    return pltpu.roll(values, step % values.shape[axis], axis)


def faces(below, own, above):
    nx, ny = own.shape
    ix = lax.broadcasted_iota(jnp.int32, (nx, ny), 0)
    iy = lax.broadcasted_iota(jnp.int32, (nx, ny), 1)
    half = 0.5 * own
    zero = jnp.zeros_like(own)
    xm = jnp.where(ix == 0, zero, half + shifted(half, 0, 1))
    xp = jnp.where(ix == nx - 1, zero, half + shifted(half, 0, -1))
    ym = jnp.where(iy == 0, zero, half + shifted(half, 1, 1))
    yp = jnp.where(iy == ny - 1, zero, half + shifted(half, 1, -1))
    up = half + 0.5 * above
    down = half + 0.5 * below
    total = up + down
    total = total + jnp.where(ix == 0, half, xm) + jnp.where(ix == nx - 1, half, xp)
    total = total + jnp.where(iy == 0, half, ym) + jnp.where(iy == ny - 1, half, yp)
    return xm, xp, ym, yp, down, up, total


def lateral(to_xm, to_xp, to_ym, to_yp):
    return (
        shifted(to_xm, 0, -1)
        + shifted(to_xp, 0, 1)
        + shifted(to_ym, 1, -1)
        + shifted(to_yp, 1, 1)
    )


def scan_table(table, block, coef_dev, entries, targets, lists, weights, counts, visit):
    for kind in range(len(targets)):
        counts[block * len(targets) + kind] = 0

    def body(e, carry):
        p = table[1, e].astype(jnp.int32)
        w = table[3, e]
        device = lax.div(p, coef_dev)
        for kind, target_device in enumerate(targets):

            @pl.when((device == target_device) & (w > 0.0))
            def _():
                row = table[0, e].astype(jnp.int32)
                target = lax.rem(p, coef_dev) * M + table[2, e].astype(jnp.int32)
                slot = block * len(targets) + kind
                at = counts[slot]
                lists[slot * entries + at] = row * (coef_dev * M) + target
                weights[slot * entries + at] = w
                counts[slot] = at + 1
                visit(kind, row, target, w)

        return carry

    lax.fori_loop(0, entries, body, 0)


def sum_first_kernel(n_blocks, coef_dev, entries, rows, slot_rows, where_ref, *refs):
    blocks, (own, other, lists, weights, counts), (tables, sems) = (
        refs[:n_blocks],
        refs[n_blocks : n_blocks + 5],
        refs[n_blocks + 5 :],
    )
    targets = coef_dev * M
    table_at = coef_dev * rows + slot_rows
    copies = [
        pltpu.make_async_copy(b.at[pl.ds(table_at, TABLE_ROWS)], tables.at[i], sems.at[i])
        for i, b in enumerate(blocks)
    ]
    for copy in copies:
        copy.start()
    own[...] = jnp.zeros_like(own)
    other[...] = jnp.zeros_like(other)
    outs = (own, other)
    for copy in copies:
        copy.wait()
    wanted = (where_ref[0], where_ref[1])
    for i, b in enumerate(blocks):

        def visit(kind, row, target, w, b=b):
            at = pl.ds(pl.multiple_of(target * rows, rows), rows)
            src = b[pl.ds(pl.multiple_of(row * rows, rows), rows), :]
            outs[kind][at, :] = outs[kind][at, :] + w * src

        scan_table(
            tables.at[i], i, coef_dev, entries, wanted, lists, weights, counts, visit
        )
        for k in range(M):

            @pl.when(where_ref[2 + k] == where_ref[2 + M + i])
            def _(b=b, k=k):
                at = pl.ds(targets * rows + k * slot_rows, slot_rows)
                own[at, :] = own[at, :] + b[pl.ds(coef_dev * rows, slot_rows), :]

    tail = pl.ds(targets * rows, M * slot_rows)
    other[tail, :] = own[tail, :]


def sum_next_kernel(n_blocks, coef_dev, entries, rows, lists, weights, counts, *refs):
    blocks, outs = refs[:n_blocks], refs[n_blocks:]
    targets = coef_dev * M
    for out in outs:
        out[...] = jnp.zeros_like(out)
    for i, b in enumerate(blocks):
        for kind, out in enumerate(outs):
            slot = i * len(outs) + kind

            def body(e, carry, b=b, out=out, slot=slot):
                code = lists[slot * entries + e]
                w = weights[slot * entries + e]
                row, target = lax.div(code, targets), lax.rem(code, targets)
                at = pl.ds(pl.multiple_of(target * rows, rows), rows)
                src = b[pl.ds(pl.multiple_of(row * rows, rows), rows), :]
                out[at, :] = out[at, :] + w * src
                return carry

            lax.fori_loop(0, counts[slot], body, 0)


def exchange_pairs(count, inner, mask, keep=lambda o: True):
    return [
        (o * inner + i, (o ^ mask) * inner + i)
        for o in range(count)
        for i in range(inner)
        if keep(o)
    ]


def line_of_four(block, inner):
    middle = (1, 2)
    near = lax.ppermute(block, "chaos", exchange_pairs(4, inner, 1))
    mid = lax.ppermute(block, "chaos", exchange_pairs(4, inner, 3, lambda o: o in middle))
    far = lax.ppermute(block, "chaos", exchange_pairs(4, inner, 2))
    relay = lax.ppermute(far, "chaos", exchange_pairs(4, inner, 1, lambda o: o in middle))
    return [block, near, far, mid, relay], (0, 1, 2, 3, 3)


def column_sums(blocks, table_block, coef_dev, entries, rows, slot_rows, wanted, owners):
    targets = coef_dev * M

    def sums(block, table, device):
        ids = table[:3, :entries].astype(jnp.int32)
        w = table[3, :entries]
        picked = (ids[0][:, None] == jnp.arange(coef_dev)[None, :]).astype(jnp.float32)
        found = []
        for who in wanted:
            mine = jnp.where(ids[1] // coef_dev == who, w, 0.0)
            target = (ids[1] % coef_dev) * M + ids[2]
            onehot = (jnp.arange(targets)[:, None] == target[None, :]).astype(jnp.float32)
            matrix = jnp.sum(
                (onehot * mine[None, :])[:, :, None] * picked[None, :, :], axis=1
            )
            data = block[: coef_dev * rows].reshape(coef_dev, -1)
            found.append(
                jnp.dot(matrix, data, precision=lax.Precision.HIGHEST).reshape(
                    targets * rows, -1
                )
            )
        if slot_rows:
            slot = block[coef_dev * rows : coef_dev * rows + slot_rows]
            part = jnp.concatenate(
                [jnp.where(owners[k] == device, slot, 0.0) for k in range(M)], axis=0
            )
            found = [jnp.concatenate([f, part], axis=0) for f in found]
        return found

    return sums


def chaos_sums(chunks, coef_dev, entries, rows_of, slot_rows, mode_owner):
    count = lax.axis_size("chaos")
    inner = 2 if count % 2 == 0 else 1
    outer = count // inner
    me = lax.axis_index("chaos")
    my_outer, my_inner = me // inner, me % inner
    neighbour = my_outer * inner + (inner - 1 - my_inner)
    lanes = chunks[0].shape[1]
    targets = coef_dev * M
    found = []
    if outer == 4:
        lists = None
        for number, chunk in enumerate(chunks):
            rows = rows_of[number]
            blocks, masks = line_of_four(chunk, inner)
            n_blocks = len(blocks)
            size = targets * rows
            if lists is None:
                owners_of = [(my_outer ^ mask) * inner + my_inner for mask in masks]
                where = jnp.stack(
                    [me, neighbour]
                    + [mode_owner[k] for k in range(M)]
                    + owners_of
                ).astype(jnp.int32)
                full = jax.ShapeDtypeStruct((size + M * slot_rows, lanes), jnp.float32)
                own, other, *lists = pl.pallas_call(
                    functools.partial(
                        sum_first_kernel, n_blocks, coef_dev, entries, rows, slot_rows
                    ),
                    out_shape=(
                        full,
                        full,
                        jax.ShapeDtypeStruct((n_blocks * 2 * entries,), jnp.int32),
                        jax.ShapeDtypeStruct((n_blocks * 2 * entries,), jnp.float32),
                        jax.ShapeDtypeStruct((n_blocks * 2,), jnp.int32),
                    ),
                    in_specs=[SMEM] + [VMEM] * n_blocks,
                    out_specs=(VMEM, VMEM, SMEM, SMEM, SMEM),
                    scratch_shapes=[
                        pltpu.SMEM((n_blocks, TABLE_ROWS, lanes), jnp.float32),
                        pltpu.SemaphoreType.DMA((n_blocks,)),
                    ],
                    cost_estimate=cost(targets, rows, lanes, 4),
                    name="sum_first",
                )(where, *blocks)
            else:
                part = jax.ShapeDtypeStruct((size, lanes), jnp.float32)
                own, other = pl.pallas_call(
                    functools.partial(sum_next_kernel, n_blocks, coef_dev, entries, rows),
                    out_shape=(part, part),
                    in_specs=[SMEM] * 3 + [VMEM] * n_blocks,
                    out_specs=(VMEM, VMEM),
                    cost_estimate=cost(targets, rows, lanes, 4),
                    name="sum_next",
                )(*lists, *blocks)
            found.append((own, other))
    else:
        ring = [
            (o * inner + i, ((o + 1) % outer) * inner + i)
            for o in range(outer)
            for i in range(inner)
        ]
        table_at = coef_dev * rows_of[0] + slot_rows

        def at_step(step, blocks):
            device = ((my_outer - step) % outer) * inner + my_inner
            table = blocks[0][table_at : table_at + TABLE_ROWS]
            return [
                tuple(
                    column_sums(
                        blocks,
                        table,
                        coef_dev,
                        entries,
                        rows_of[j],
                        slot_rows if j == 0 else 0,
                        (me, neighbour),
                        mode_owner,
                    )(block, table, device)
                )
                for j, block in enumerate(blocks)
            ]

        def body(step, carry):
            blocks, sums = carry
            blocks = [lax.ppermute(b, "chaos", ring) for b in blocks]
            return blocks, jax.tree.map(jnp.add, sums, at_step(step, blocks))

        _, found = lax.fori_loop(1, outer, body, (list(chunks), at_step(0, chunks)))
    if inner == 1:
        return [own for own, _ in found]
    across = [
        (o * inner + i, o * inner + inner - 1 - i) for o in range(outer) for i in range(inner)
    ]
    return [own + lax.ppermute(other, "chaos", across) for own, other in found]


def depth_pair(values):
    count = lax.axis_size("space")
    first = [(i, i ^ 1) for i in range(count) if i ^ 1 < count]
    second = [
        (i, j)
        for i in range(count)
        for j in [i - 1 if i % 2 == 0 else i + 1]
        if 0 <= j < count
    ]
    return lax.ppermute(values, "space", second), lax.ppermute(values, "space", first)


def base_kernel(coef_dev, depth, n_space, space_ref, coeffs, source, mean, *refs):
    other, pair, known, face, coef_ext, mean_ext = refs
    nx, ny = mean.shape[1:]
    index = space_ref[0]
    even = lax.rem(index, 2) == 0
    pair_at = jnp.where(even, 2 * depth, 0)
    other_at = jnp.where(even, 0, 2 * depth)
    total_layers = 3 * depth
    planes = coef_dev * depth

    for at, part in ((pair_at, pair), (other_at, other)):
        for c in range(coef_dev):
            coef_ext[c, pl.ds(at, depth)] = part[c * depth : (c + 1) * depth]
        mean_ext[pl.ds(at, depth)] = part[2 * planes : 2 * planes + depth]
    for c in range(coef_dev):
        coef_ext[c, depth : 2 * depth] = coeffs[c]
    mean_ext[depth : 2 * depth] = mean[...]

    def layer(l, source_of):
        xm, xp, ym, yp, down, up, total = faces(mean_ext[l - 1], mean_ext[l], mean_ext[l + 1])
        diagonal = REACTION + total
        absolute = index * depth + l - depth
        inside = (absolute >= 0) & (absolute < n_space * depth)
        face[0, l], face[1, l], face[2, l], face[3, l] = xm, xp, ym, yp
        face[4, l], face[5, l] = down, up
        face[6, l] = jnp.where(inside, 1.0 / diagonal, 0.0)

        def coefficient(c, carry):
            v = coef_ext[c, l]
            spread = lateral(xm * v, xp * v, ym * v, yp * v)
            spread = spread + down * coef_ext[c, l - 1] + up * coef_ext[c, l + 1]
            known[c, l] = source_of(c) - (diagonal * v - spread)
            return carry

        lax.fori_loop(0, coef_dev, coefficient, 0)

    def from_part(part, at):
        def body(l, carry):
            layer(l, lambda c: part[planes + c * depth + l - at])
            return carry

        lax.fori_loop(jnp.maximum(at, 1), jnp.minimum(at + depth, total_layers - 1), body, 0)

    from_part(pair, pair_at)
    from_part(other, other_at)

    def body(l, carry):
        layer(l, lambda c: source[c, l - depth])
        return carry

    lax.fori_loop(depth, 2 * depth, body, 0)


def sweep_constants():
    midpoint = (BOUND_HIGH + BOUND_LOW) / 2.0
    halfwidth = (BOUND_HIGH - BOUND_LOW) / 2.0
    ratio = midpoint / halfwidth
    now = 1.0 / ratio
    steps = []
    for _ in range(ITERS - 1):
        following = 1.0 / (2.0 * ratio - now)
        steps.append((following * now, 2.0 * following / halfwidth))
        now = following
    return midpoint, steps


def sweep_kernel(coef_dev, depth, layer_counts, space_ref, known, face, *refs):
    n = len(layer_counts)
    parts = [refs[3 * j : 3 * j + 3] for j in range(n)]
    residual, correction, summed, mode_ext, mode_face, scaled, first, second = refs[3 * n :]
    nx, ny = known.shape[2:]
    targets = coef_dev * M
    even = lax.rem(space_ref[0], 2) == 0
    pair_at = jnp.where(even, 2 * depth, 0)
    other_at = jnp.where(even, 0, 2 * depth)
    last = 3 * depth - 1

    start = 0
    for j, (trio, layers) in enumerate(zip(parts, layer_counts)):
        for part, at in zip(trio, (depth, other_at, pair_at)):
            for t in range(targets):
                for l in range(layers):
                    row = (t * layers + l) * nx
                    summed[t, at + start + l] = part[row : row + nx]
            if j == 0:
                for k in range(M):
                    for l in range(depth):
                        row = (targets * layers + k * depth + l) * nx
                        mode_ext[k, at + l] = part[row : row + nx]
        start += layers

    def mode_faces(l, carry):
        for k in range(M):
            got = faces(mode_ext[k, l - 1], mode_ext[k, l], mode_ext[k, l + 1])
            for i, value in enumerate(got):
                mode_face[k, i, l] = value
        return carry

    lax.fori_loop(1, last, mode_faces, 0)
    midpoint, steps = sweep_constants()

    def coupled(l, carry):
        def coefficient(c, carry):
            to = [None] * 4
            rest = known[c, l]
            for k in range(M):
                v = summed[c * M + k, l]
                for i in range(4):
                    term = mode_face[k, i, l] * v
                    to[i] = term if to[i] is None else to[i] + term
                rest = rest - mode_face[k, 6, l] * v
                rest = rest + mode_face[k, 4, l] * summed[c * M + k, l - 1]
                rest = rest + mode_face[k, 5, l] * summed[c * M + k, l + 1]
            rest = rest + lateral(*to)
            w = rest * face[6, l]
            scaled[c, l] = w
            first[c, l] = w * (1.0 / midpoint)

            @pl.when((l >= depth) & (l < 2 * depth))
            def _():
                residual[c, l - depth] = rest
                correction[c, l - depth] = w * (1.0 / midpoint)

            return carry

        lax.fori_loop(0, coef_dev, coefficient, 0)
        return carry

    lax.fori_loop(1, last, coupled, 0)

    now, later = first, second
    for number, (keep, gain) in enumerate(steps):
        low = depth - (len(steps) - 1 - number)

        def swept(l, carry, now=now, later=later, keep=keep, gain=gain, number=number):
            def coefficient(c, carry):
                v = now[c, l]
                spread = lateral(face[0, l] * v, face[1, l] * v, face[2, l] * v, face[3, l] * v)
                spread = spread + face[4, l] * now[c, l - 1] + face[5, l] * now[c, l + 1]
                w = scaled[c, l] - v + face[6, l] * spread
                d = keep * v + gain * w
                if number + 1 < len(steps):
                    scaled[c, l] = w
                    later[c, l] = d

                @pl.when((l >= depth) & (l < 2 * depth))
                def _():
                    correction[c, l - depth] = correction[c, l - depth] + d

                return carry

            lax.fori_loop(0, coef_dev, coefficient, 0)
            return carry

        lax.fori_loop(low, 3 * depth - low, swept, 0)
        now, later = later, now


def per_device(coeffs, source, mean_field, mode_bank, mode_owner, links):
    coef_dev, depth, nx, ny = coeffs.shape
    n_space = lax.axis_size("space")
    entries = links.shape[1]
    slot_rows = depth * nx
    per_chunk = depth // CHUNKS
    layer_counts = [per_chunk] * CHUNKS
    index = lax.axis_index("space").astype(jnp.int32).reshape(1)

    table = links[0].astype(jnp.float32)
    table = jnp.where(jnp.arange(4)[None, :] == 3, jnp.sqrt(table), table)
    table = jnp.pad(table.T, ((0, TABLE_ROWS - 4), (0, ny - entries)))
    chunks, start = [], 0
    for j, layers in enumerate(layer_counts):
        piece = coeffs[:, start : start + layers].reshape(-1, ny)
        if j == 0:
            piece = jnp.concatenate([piece, mode_bank[0].reshape(-1, ny), table], axis=0)
        chunks.append(piece)
        start += layers

    sums = chaos_sums(
        chunks, coef_dev, entries, [layers * nx for layers in layer_counts], slot_rows, mode_owner
    )

    early = jnp.concatenate(
        [coeffs.reshape(-1, nx, ny), source.reshape(-1, nx, ny), mean_field], axis=0
    )
    other, pair = depth_pair(early)
    wide = (coef_dev, 3 * depth, nx, ny)
    known, face = pl.pallas_call(
        functools.partial(base_kernel, coef_dev, depth, n_space),
        out_shape=(
            jax.ShapeDtypeStruct(wide, jnp.float32),
            jax.ShapeDtypeStruct((7, 3 * depth, nx, ny), jnp.float32),
        ),
        in_specs=[SMEM] + [VMEM] * 5,
        out_specs=(VMEM, VMEM),
        scratch_shapes=[
            pltpu.VMEM(wide, jnp.float32),
            pltpu.VMEM((3 * depth, nx, ny), jnp.float32),
        ],
        cost_estimate=cost(3 * depth * coef_dev, nx, ny, 20),
        name="base",
    )(index, coeffs, source, mean_field, other, pair)

    parts = []
    for own in sums:
        parts += [own, *depth_pair(own)]
    out = jax.ShapeDtypeStruct(coeffs.shape, jnp.float32)
    return pl.pallas_call(
        functools.partial(sweep_kernel, coef_dev, depth, layer_counts),
        out_shape=(out, out),
        in_specs=[SMEM] + [VMEM] * (2 + len(parts)),
        out_specs=(VMEM, VMEM),
        scratch_shapes=[
            pltpu.VMEM((coef_dev * M, 3 * depth, nx, ny), jnp.float32),
            pltpu.VMEM((M, 3 * depth, nx, ny), jnp.float32),
            pltpu.VMEM((M, 7, 3 * depth, nx, ny), jnp.float32),
            pltpu.VMEM(wide, jnp.float32),
            pltpu.VMEM(wide, jnp.float32),
            pltpu.VMEM(wide, jnp.float32),
        ],
        cost_estimate=cost(6 * depth * coef_dev, nx, ny, 40),
        name="sweeps",
    )(index, known, face, *parts)


def solution(mesh):
    in_specs = (
        P("chaos", "space", None, None),
        P("chaos", "space", None, None),
        P("space", None, None),
        P("chaos", "space", None, None),
        P(),
        P("chaos", None, None),
    )
    out_specs = (P("chaos", "space", None, None), P("chaos", "space", None, None))
    return jax.shard_map(
        per_device, mesh=mesh, in_specs=in_specs, out_specs=out_specs, check_vma=False
    )
```

```python
import functools

import jax
import jax.numpy as jnp
from jax import lax
from jax.experimental import pallas as pl
from jax.experimental.pallas import tpu as pltpu
from jax.sharding import PartitionSpec as P


M = 2
ITERS = 4

REACTION = 0.5
BOUND_LOW = 0.04
BOUND_HIGH = 2.0

CHUNKS = 2
TABLE_ROWS = 8


VMEM = pl.BlockSpec(memory_space=pltpu.VMEM)
SMEM = pl.BlockSpec(memory_space=pltpu.SMEM)


def cost(planes, nx, ny, flops):
    return pl.CostEstimate(
        flops=flops * planes * nx * ny, bytes_accessed=8 * planes * nx * ny, transcendentals=0
    )


def shifted(values, axis, step):
    return pltpu.roll(values, step % values.shape[axis], axis)


def faces(below, own, above):
    nx, ny = own.shape
    ix = lax.broadcasted_iota(jnp.int32, (nx, ny), 0)
    iy = lax.broadcasted_iota(jnp.int32, (nx, ny), 1)
    half = 0.5 * own
    zero = jnp.zeros_like(own)
    xm = jnp.where(ix == 0, zero, half + shifted(half, 0, 1))
    xp = jnp.where(ix == nx - 1, zero, half + shifted(half, 0, -1))
    ym = jnp.where(iy == 0, zero, half + shifted(half, 1, 1))
    yp = jnp.where(iy == ny - 1, zero, half + shifted(half, 1, -1))
    up = half + 0.5 * above
    down = half + 0.5 * below
    total = up + down
    total = total + jnp.where(ix == 0, half, xm) + jnp.where(ix == nx - 1, half, xp)
    total = total + jnp.where(iy == 0, half, ym) + jnp.where(iy == ny - 1, half, yp)
    return xm, xp, ym, yp, down, up, total


def lateral(to_xm, to_xp, to_ym, to_yp):
    return (
        shifted(to_xm, 0, -1)
        + shifted(to_xp, 0, 1)
        + shifted(to_ym, 1, -1)
        + shifted(to_yp, 1, 1)
    )


def sum_kernel(n_blocks, coef_dev, entries, rows, slot_rows, scan, more, *refs):
    refs = list(refs)
    where = refs.pop(0) if scan else None
    given = None if scan else [refs.pop(0) for _ in range(3)]
    blocks = [refs.pop(0) for _ in range(n_blocks)]
    so_far = [refs.pop(0) for _ in range(2)] if more else [None] * 2
    own, other = refs.pop(0), refs.pop(0)
    lists, weights, counts = [refs.pop(0) for _ in range(3)] if scan else given
    outs = (own, other)
    targets = coef_dev * M

    def add(block, code, w, out):
        row, target = lax.div(code, targets), lax.rem(code, targets)
        at = pl.ds(pl.multiple_of(target * rows, rows), rows)
        src = block[pl.ds(pl.multiple_of(row * rows, rows), rows), :]
        out[at, :] = out[at, :] + w * src

    if scan:
        tables, sems = refs
        table_at = coef_dev * rows + slot_rows
        copies = [
            pltpu.make_async_copy(b.at[pl.ds(table_at, TABLE_ROWS)], tables.at[i], sems.at[i])
            for i, b in enumerate(blocks)
        ]
        for copy in copies:
            copy.start()
    for out, start in zip(outs, so_far):
        out[...] = start[...] if more else jnp.zeros_like(out)
    if scan:
        for copy in copies:
            copy.wait()
        names = [where[kind].astype(jnp.float32) for kind in range(2)]
    for i, b in enumerate(blocks):
        if scan:
            for kind in range(2):
                counts[2 * i + kind] = 0

            def look(e, carry, b=b, i=i):
                name = tables[i, 0, e]
                for kind, out in enumerate(outs):

                    @pl.when(name == names[kind])
                    def _(kind=kind, out=out):
                        slot = 2 * i + kind
                        code = tables[i, 1, e].astype(jnp.int32)
                        w = tables[i, 2, e]
                        at = counts[slot]
                        lists[slot * entries + at] = code
                        weights[slot * entries + at] = w
                        counts[slot] = at + 1
                        add(b, code, w, out)

                return carry

            lax.fori_loop(0, entries, look, 0)
            for k in range(M):

                @pl.when(where[2 + k] == where[2 + M + i])
                def _(b=b, k=k):
                    at = pl.ds(targets * rows + k * slot_rows, slot_rows)
                    slot = b[pl.ds(coef_dev * rows, slot_rows), :]
                    own[at, :] = own[at, :] + slot
                    other[at, :] = other[at, :] + slot

        else:
            for kind, out in enumerate(outs):
                slot = 2 * i + kind

                def listed(e, carry, b=b, out=out, slot=slot):
                    add(b, lists[slot * entries + e], weights[slot * entries + e], out)
                    return carry

                lax.fori_loop(0, counts[slot], listed, 0)


def sum_blocks(blocks, coef_dev, entries, rows, slot_rows, where, lists, so_far):
    scan, more, n = lists is None, so_far is not None, len(blocks)
    lanes = blocks[0].shape[1]
    size = coef_dev * M * rows + (M * slot_rows if scan else 0)
    total = jax.ShapeDtypeStruct((size, lanes), jnp.float32)
    out_shape, out_specs, scratch = [total, total], [VMEM, VMEM], []
    if scan:
        out_shape += [
            jax.ShapeDtypeStruct((2 * n * entries,), jnp.int32),
            jax.ShapeDtypeStruct((2 * n * entries,), jnp.float32),
            jax.ShapeDtypeStruct((2 * n,), jnp.int32),
        ]
        out_specs += [SMEM] * 3
        scratch = [
            pltpu.SMEM((n, TABLE_ROWS, lanes), jnp.float32),
            pltpu.SemaphoreType.DMA((n,)),
        ]
    small = [where] if scan else list(lists)
    operands = small + list(blocks) + (list(so_far) if more else [])
    got = pl.pallas_call(
        functools.partial(
            sum_kernel, n, coef_dev, entries, rows, slot_rows if scan else 0, scan, more
        ),
        out_shape=out_shape,
        in_specs=[SMEM] * len(small) + [VMEM] * (len(operands) - len(small)),
        out_specs=out_specs,
        scratch_shapes=scratch,
        compiler_params=pltpu.CompilerParams(vmem_limit_bytes=12 << 20),
        cost_estimate=cost(coef_dev * M, rows, lanes, 4),
    )(*operands)
    return got[:2], (lists if lists is not None else got[2:])


def exchange_pairs(count, inner, mask, keep=lambda o: True):
    return [
        (o * inner + i, (o ^ mask) * inner + i)
        for o in range(count)
        for i in range(inner)
        if keep(o)
    ]


def line_of_four(block, inner):
    middle = (1, 2)
    far = lax.ppermute(block, "chaos", exchange_pairs(4, inner, 2))
    near = lax.ppermute(block, "chaos", exchange_pairs(4, inner, 1))
    mid = lax.ppermute(block, "chaos", exchange_pairs(4, inner, 3, lambda o: o in middle))
    relay = lax.ppermute(far, "chaos", exchange_pairs(4, inner, 1, lambda o: o in middle))
    return near, far, mid, relay


def column_sums(coef_dev, entries, rows, slot_rows, wanted, owners):
    targets = coef_dev * M

    def sums(block, table, device):
        ids = table[:2, :entries].astype(jnp.int32)
        w = table[2, :entries]
        source_row, target = ids[1] // targets, ids[1] % targets
        picked = (source_row[:, None] == jnp.arange(coef_dev)[None, :]).astype(jnp.float32)
        found = []
        for who in wanted:
            mine = jnp.where(ids[0] == who + 1, w, 0.0)
            onehot = (jnp.arange(targets)[:, None] == target[None, :]).astype(jnp.float32)
            matrix = jnp.sum(
                (onehot * mine[None, :])[:, :, None] * picked[None, :, :], axis=1
            )
            data = block[: coef_dev * rows].reshape(coef_dev, -1)
            found.append(
                jnp.dot(matrix, data, precision=lax.Precision.HIGHEST).reshape(
                    targets * rows, -1
                )
            )
        if slot_rows:
            slot = block[coef_dev * rows : coef_dev * rows + slot_rows]
            part = jnp.concatenate(
                [jnp.where(owners[k] == device, slot, 0.0) for k in range(M)], axis=0
            )
            found = [jnp.concatenate([f, part], axis=0) for f in found]
        return found

    return sums


def grid_of(count):
    inner = 2 if count % 2 == 0 else 1
    return count // inner, inner


def chaos_sums(chunks, coef_dev, entries, rows_of, slot_rows, mode_owner):
    outer, inner = grid_of(lax.axis_size("chaos"))
    me = lax.axis_index("chaos")
    my_outer, my_inner = me // inner, me % inner
    neighbour = my_outer * inner + (inner - 1 - my_inner)
    found = []
    if outer == 4:
        where = jnp.stack(
            [me + 1, neighbour + 1]
            + [mode_owner[k] for k in range(M)]
            + [(my_outer ^ mask) * inner + my_inner for mask in (0, 1, 2, 3, 3)]
        ).astype(jnp.int32)
        head = 2 + M
        relay_where = jnp.concatenate([where[:head], where[head + 4 :]])
        lists = late_lists = None
        gathered = [line_of_four(c, inner) for c in chunks]
        for j, (chunk, (near, far, mid, relay)) in enumerate(zip(chunks, gathered)):
            args = (coef_dev, entries, rows_of[j], slot_rows)
            sums, lists = sum_blocks([chunk, near, far, mid], *args, where, lists, None)
            sums, late_lists = sum_blocks([relay], *args, relay_where, late_lists, sums)
            found.append(sums)
    else:
        ring = [
            (o * inner + i, ((o + 1) % outer) * inner + i)
            for o in range(outer)
            for i in range(inner)
        ]
        table_at = coef_dev * rows_of[0] + slot_rows

        def at_step(step, blocks):
            device = ((my_outer - step) % outer) * inner + my_inner
            table = blocks[0][table_at : table_at + TABLE_ROWS]
            return [
                tuple(
                    column_sums(
                        coef_dev,
                        entries,
                        rows_of[j],
                        slot_rows if j == 0 else 0,
                        (me, neighbour),
                        mode_owner,
                    )(block, table, device)
                )
                for j, block in enumerate(blocks)
            ]

        def body(step, carry):
            blocks, sums = carry
            blocks = [lax.ppermute(b, "chaos", ring) for b in blocks]
            return blocks, jax.tree.map(jnp.add, sums, at_step(step, blocks))

        _, found = lax.fori_loop(1, outer, body, (list(chunks), at_step(0, chunks)))
    if inner == 1:
        return [own for own, _ in found]
    across = [
        (o * inner + i, o * inner + inner - 1 - i) for o in range(outer) for i in range(inner)
    ]
    full = []
    for own, other in found:
        got = lax.ppermute(other, "chaos", across)
        full.append(own + got)
    return full


def depth_pair(values):
    count = lax.axis_size("space")
    first = [(i, i ^ 1) for i in range(count) if i ^ 1 < count]
    second = [
        (i, j)
        for i in range(count)
        for j in [i - 1 if i % 2 == 0 else i + 1]
        if 0 <= j < count
    ]
    other = lax.ppermute(values, "space", second)
    pair = lax.ppermute(values, "space", first)
    return other, pair


def base_kernel(coef_dev, depth, n_space, space_ref, coeffs, source, mean, *refs):
    other, pair, known, face, coef_ext, mean_ext = refs
    index = space_ref[0]
    even = lax.rem(index, 2) == 0
    pair_at = jnp.where(even, 2 * depth, 0)
    other_at = jnp.where(even, 0, 2 * depth)
    total_layers = 3 * depth
    planes = coef_dev * depth

    for at, part in ((pair_at, pair), (other_at, other)):
        for c in range(coef_dev):
            coef_ext[c, pl.ds(at, depth)] = part[c * depth : (c + 1) * depth]
        mean_ext[pl.ds(at, depth)] = part[2 * planes : 2 * planes + depth]
    for c in range(coef_dev):
        coef_ext[c, depth : 2 * depth] = coeffs[c]
    mean_ext[depth : 2 * depth] = mean[...]

    def layer(l, source_of):
        xm, xp, ym, yp, down, up, total = faces(mean_ext[l - 1], mean_ext[l], mean_ext[l + 1])
        diagonal = REACTION + total
        absolute = index * depth + l - depth
        inside = (absolute >= 0) & (absolute < n_space * depth)
        face[0, l], face[1, l], face[2, l], face[3, l] = xm, xp, ym, yp
        face[4, l], face[5, l] = down, up
        face[6, l] = jnp.where(inside, 1.0 / diagonal, 0.0)

        def coefficient(c, carry):
            v = coef_ext[c, l]
            spread = lateral(xm * v, xp * v, ym * v, yp * v)
            spread = spread + down * coef_ext[c, l - 1] + up * coef_ext[c, l + 1]
            known[c, l] = source_of(c) - (diagonal * v - spread)
            return carry

        for c in range(coef_dev):
            coefficient(c, 0)

    def from_part(part, at):
        def body(l, carry):
            layer(l, lambda c: part[planes + c * depth + l - at])
            return carry

        lax.fori_loop(jnp.maximum(at, 1), jnp.minimum(at + depth, total_layers - 1), body, 0)

    from_part(pair, pair_at)
    from_part(other, other_at)

    def body(l, carry):
        layer(l, lambda c: source[c, l - depth])
        return carry

    lax.fori_loop(depth, 2 * depth, body, 0)


def sweep_constants():
    midpoint = (BOUND_HIGH + BOUND_LOW) / 2.0
    halfwidth = (BOUND_HIGH - BOUND_LOW) / 2.0
    ratio = midpoint / halfwidth
    now = 1.0 / ratio
    steps = []
    for _ in range(ITERS - 1):
        following = 1.0 / (2.0 * ratio - now)
        steps.append((following * now, 2.0 * following / halfwidth))
        now = following
    return midpoint, steps


def sweep_kernel(coef_dev, depth, layer_counts, space_ref, known, face, *refs):
    n = len(layer_counts)
    parts = [refs[3 * j : 3 * j + 3] for j in range(n)]
    residual, correction, summed, mode_ext, mode_face, scaled, first, second = refs[3 * n :]
    nx, _ = known.shape[2:]
    targets = coef_dev * M
    even = lax.rem(space_ref[0], 2) == 0
    pair_at = jnp.where(even, 2 * depth, 0)
    other_at = jnp.where(even, 0, 2 * depth)
    last = 3 * depth - 1

    start = 0
    for j, (trio, layers) in enumerate(zip(parts, layer_counts)):
        for part, at in zip(trio, (depth, other_at, pair_at)):
            for t in range(targets):
                for l in range(layers):
                    row = (t * layers + l) * nx
                    summed[t, at + start + l] = part[row : row + nx]
            if j == 0:
                for k in range(M):
                    for l in range(depth):
                        row = (targets * layers + k * depth + l) * nx
                        mode_ext[k, at + l] = part[row : row + nx]
        start += layers

    def mode_faces(l, carry):
        for k in range(M):
            got = faces(mode_ext[k, l - 1], mode_ext[k, l], mode_ext[k, l + 1])
            for i, value in enumerate(got):
                mode_face[k, i, l] = value
        return carry

    lax.fori_loop(1, last, mode_faces, 0)
    midpoint, steps = sweep_constants()

    def coupled(l, own):
        for c in range(coef_dev):
            to = [None] * 4
            rest = known[c, l]
            for k in range(M):
                v = summed[c * M + k, l]
                for i in range(4):
                    term = mode_face[k, i, l] * v
                    to[i] = term if to[i] is None else to[i] + term
                rest = rest - mode_face[k, 6, l] * v
                rest = rest + mode_face[k, 4, l] * summed[c * M + k, l - 1]
                rest = rest + mode_face[k, 5, l] * summed[c * M + k, l + 1]
            rest = rest + lateral(*to)
            w = rest * face[6, l]
            d = w * (1.0 / midpoint)
            scaled[c, l] = w
            first[c, l] = d
            if own:
                residual[c, l - depth] = rest
                correction[c, l - depth] = d

    over_layers(coupled, depth, depth - 1)

    now, later = first, second
    for number, (keep, gain) in enumerate(steps):

        def swept(l, own, now=now, later=later, keep=keep, gain=gain, number=number):
            for c in range(coef_dev):
                v = now[c, l]
                spread = lateral(face[0, l] * v, face[1, l] * v, face[2, l] * v, face[3, l] * v)
                spread = spread + face[4, l] * now[c, l - 1] + face[5, l] * now[c, l + 1]
                w = scaled[c, l] - v + face[6, l] * spread
                d = keep * v + gain * w
                if number + 1 < len(steps):
                    scaled[c, l] = w
                    later[c, l] = d
                if own:
                    correction[c, l - depth] = correction[c, l - depth] + d

        over_layers(swept, depth, len(steps) - 1 - number)
        now, later = later, now


def over_layers(visit, depth, halo):
    def own(l, carry):
        visit(l, True)
        return carry

    def outside(i, carry):
        visit(jnp.where(i < halo, depth - halo + i, 2 * depth - halo + i), False)
        return carry

    lax.fori_loop(depth, 2 * depth, own, 0)
    if halo:
        lax.fori_loop(0, 2 * halo, outside, 0)


def residual_and_correction(coeffs, source, mean_field, mode_bank, mode_owner, links):
    coef_dev, depth, nx, ny = coeffs.shape
    n_space = lax.axis_size("space")
    entries = links.shape[1]
    slot_rows = depth * nx
    per_chunk = depth // CHUNKS
    layer_counts = [per_chunk] * CHUNKS
    index = lax.axis_index("space").astype(jnp.int32).reshape(1)

    s, p, k, level = (links[0, :, i] for i in range(4))
    table = jnp.stack(
        [
            jnp.where(level > 0, p // coef_dev + 1, 0).astype(jnp.float32),
            ((s * coef_dev + p % coef_dev) * M + k).astype(jnp.float32),
            jnp.sqrt(level.astype(jnp.float32)),
        ]
    )
    table = jnp.pad(table, ((0, TABLE_ROWS - 3), (0, ny - entries)))
    chunks, start = [], 0
    for j, layers in enumerate(layer_counts):
        piece = coeffs[:, start : start + layers].reshape(-1, ny)
        if j == 0:
            piece = jnp.concatenate([piece, mode_bank[0].reshape(-1, ny), table], axis=0)
        chunks.append(piece)
        start += layers

    sums = chaos_sums(
        chunks, coef_dev, entries, [layers * nx for layers in layer_counts], slot_rows, mode_owner
    )

    early = jnp.concatenate(
        [coeffs.reshape(-1, nx, ny), source.reshape(-1, nx, ny), mean_field], axis=0
    )
    other, pair = depth_pair(early)
    wide = (coef_dev, 3 * depth, nx, ny)
    known, face = pl.pallas_call(
        functools.partial(base_kernel, coef_dev, depth, n_space),
        out_shape=(
            jax.ShapeDtypeStruct(wide, jnp.float32),
            jax.ShapeDtypeStruct((7, 3 * depth, nx, ny), jnp.float32),
        ),
        in_specs=[SMEM] + [VMEM] * 5,
        out_specs=(VMEM, VMEM),
        scratch_shapes=[
            pltpu.VMEM(wide, jnp.float32),
            pltpu.VMEM((3 * depth, nx, ny), jnp.float32),
        ],
        cost_estimate=cost(3 * depth * coef_dev, nx, ny, 20),
        compiler_params=pltpu.CompilerParams(vmem_limit_bytes=16 << 20),
        name="base",
    )(index, coeffs, source, mean_field, other, pair)

    parts = []
    for own in sums:
        parts += [own, *depth_pair(own)]
    out = jax.ShapeDtypeStruct(coeffs.shape, jnp.float32)
    return pl.pallas_call(
        functools.partial(sweep_kernel, coef_dev, depth, layer_counts),
        out_shape=(out, out),
        in_specs=[SMEM] + [VMEM] * (2 + len(parts)),
        out_specs=(VMEM, VMEM),
        scratch_shapes=[
            pltpu.VMEM((coef_dev * M, 3 * depth, nx, ny), jnp.float32),
            pltpu.VMEM((M, 3 * depth, nx, ny), jnp.float32),
            pltpu.VMEM((M, 7, 3 * depth, nx, ny), jnp.float32),
            pltpu.VMEM(wide, jnp.float32),
            pltpu.VMEM(wide, jnp.float32),
            pltpu.VMEM(wide, jnp.float32),
        ],
        cost_estimate=cost(6 * depth * coef_dev, nx, ny, 40),
        compiler_params=pltpu.CompilerParams(vmem_limit_bytes=24 << 20),
        name="sweeps",
    )(index, known, face, *parts)


def solution(mesh):
    in_specs = (
        P("chaos", "space", None, None),
        P("chaos", "space", None, None),
        P("space", None, None),
        P("chaos", "space", None, None),
        P(),
        P("chaos", None, None),
    )
    out_specs = (P("chaos", "space", None, None), P("chaos", "space", None, None))
    return jax.shard_map(
        residual_and_correction, mesh=mesh, in_specs=in_specs, out_specs=out_specs, check_vma=False
    )
```

```python
import functools

import jax
import jax.numpy as jnp
from jax import lax
from jax.experimental import pallas as pl
from jax.experimental.pallas import tpu as pltpu
from jax.sharding import PartitionSpec as P


M = 2
ITERS = 4

REACTION = 0.5
BOUND_LOW = 0.04
BOUND_HIGH = 2.0

CHUNKS = 2
TABLE_ROWS = 8


VMEM = pl.BlockSpec(memory_space=pltpu.VMEM)
SMEM = pl.BlockSpec(memory_space=pltpu.SMEM)


def cost(planes, nx, ny, flops):
    return pl.CostEstimate(
        flops=flops * planes * nx * ny, bytes_accessed=8 * planes * nx * ny, transcendentals=0
    )


def shifted(values, axis, step):
    return pltpu.roll(values, step % values.shape[axis], axis)


def faces(below, own, above):
    nx, ny = own.shape
    ix = lax.broadcasted_iota(jnp.int32, (nx, ny), 0)
    iy = lax.broadcasted_iota(jnp.int32, (nx, ny), 1)
    half = 0.5 * own
    zero = jnp.zeros_like(own)
    xm = jnp.where(ix == 0, zero, half + shifted(half, 0, 1))
    xp = jnp.where(ix == nx - 1, zero, half + shifted(half, 0, -1))
    ym = jnp.where(iy == 0, zero, half + shifted(half, 1, 1))
    yp = jnp.where(iy == ny - 1, zero, half + shifted(half, 1, -1))
    up = half + 0.5 * above
    down = half + 0.5 * below
    total = up + down
    total = total + jnp.where(ix == 0, half, xm) + jnp.where(ix == nx - 1, half, xp)
    total = total + jnp.where(iy == 0, half, ym) + jnp.where(iy == ny - 1, half, yp)
    return xm, xp, ym, yp, down, up, total


def lateral(to_xm, to_xp, to_ym, to_yp):
    return (
        shifted(to_xm, 0, -1)
        + shifted(to_xp, 0, 1)
        + shifted(to_ym, 1, -1)
        + shifted(to_yp, 1, 1)
    )


def pack_kernel(coef_dev, rows, slot_rows, inner, links, coeffs, bank, block, sems):
    copies = [
        pltpu.make_async_copy(
            coeffs.at[c, pl.ds(0, rows)], block.at[pl.ds(c * rows, rows)], sems.at[c]
        )
        for c in range(coef_dev)
    ]
    copies.append(
        pltpu.make_async_copy(
            bank.at[0], block.at[pl.ds(coef_dev * rows, slot_rows)], sems.at[coef_dev]
        )
    )
    for copy in copies:
        copy.start()
    entries, lanes = links.shape[0], block.shape[1]
    listed = links[...].astype(jnp.float32)
    s, p, k, level = (listed[:, i : i + 1] for i in range(4))
    device = jnp.floor((p + 0.5) * (1.0 / coef_dev))
    outer = jnp.floor((device + 0.5) * (1.0 / inner))
    target = (p - device * coef_dev) * M + k
    columns = (
        jnp.where(level > 0.0, outer + 1.0, 0.0),
        ((device - outer * inner) * coef_dev + s) * (coef_dev * M) + target,
        jnp.sqrt(level),
    )
    place = lax.broadcasted_iota(jnp.int32, (entries, lanes), 0)
    at = lax.broadcasted_iota(jnp.int32, (entries, lanes), 1)
    table = [
        jnp.sum(jnp.where(place == at, column, 0.0), axis=0, keepdims=True)
        for column in columns
    ]
    table.append(jnp.zeros((TABLE_ROWS - len(columns), lanes), jnp.float32))
    block[pl.ds(coef_dev * rows + slot_rows, TABLE_ROWS), :] = jnp.concatenate(table, axis=0)
    for copy in copies:
        copy.wait()


def pack(coeffs, bank, links, rows, inner):
    coef_dev, lanes = coeffs.shape[0], coeffs.shape[3]
    whole_rows = coeffs.reshape(coef_dev, -1, lanes)
    slot = bank.reshape(1, -1, lanes)
    slot_rows = slot.shape[1]
    anywhere = pl.BlockSpec(memory_space=pl.ANY)
    return pl.pallas_call(
        functools.partial(pack_kernel, coef_dev, rows, slot_rows, inner),
        out_shape=jax.ShapeDtypeStruct(
            (coef_dev * rows + slot_rows + TABLE_ROWS, lanes), jnp.float32
        ),
        in_specs=[VMEM, anywhere, anywhere],
        out_specs=VMEM,
        scratch_shapes=[pltpu.SemaphoreType.DMA((coef_dev + 1,))],
        compiler_params=pltpu.CompilerParams(vmem_limit_bytes=4 << 20),
        cost_estimate=cost(coef_dev, rows, lanes, 1),
        name="pack",
    )(links, whole_rows, slot)


def sum_kernel(n_blocks, coef_dev, entries, rows, slot_rows, scan, more, *refs):
    refs = list(refs)
    where = refs.pop(0) if scan else None
    given = None if scan else [refs.pop(0) for _ in range(3)]
    blocks = [refs.pop(0) for _ in range(n_blocks)]
    so_far = [refs.pop(0) for _ in range(2)] if more else [None] * 2
    own, other = refs.pop(0), refs.pop(0)
    lists, weights, counts = [refs.pop(0) for _ in range(3)] if scan else given
    outs = (own, other)
    targets = coef_dev * M
    spaced = entries + 1
    if scan:
        tables, sems = refs
        table_at = coef_dev * rows + slot_rows
        copies = [
            pltpu.make_async_copy(b.at[pl.ds(table_at, TABLE_ROWS)], tables.at[i], sems.at[i])
            for i, b in enumerate(blocks)
        ]
        for copy in copies:
            copy.start()
    for out, start in zip(outs, so_far):
        out[...] = start[...] if more else jnp.zeros_like(out)
    if scan:
        name = where[0].astype(jnp.float32)
        split = jnp.float32(coef_dev * targets)
        first_is_own = where[1] == 0
    for i, b in enumerate(blocks):
        if scan:
            copies[i].wait()
            ends = [(2 * i + kind) * spaced for kind in range(2)]

            def look(e, ends, i=i):
                code, w = tables[i, 1, e], tables[i, 2, e]
                mine = tables[i, 0, e] == name
                low = code < split
                is_own = low == first_is_own
                short = jnp.where(low, code, code - split).astype(jnp.int32)
                for end in ends:
                    lists[end] = short
                    weights[end] = w
                hits = (mine & is_own, mine & jnp.logical_not(is_own))
                return tuple(end + hit.astype(jnp.int32) for end, hit in zip(ends, hits))

            ends = lax.fori_loop(0, entries, look, tuple(jnp.int32(e) for e in ends), unroll=8)
            for kind in range(2):
                counts[2 * i + kind] = ends[kind]
            for k in range(M):

                @pl.when(where[2 + k] == where[2 + M + i])
                def _(b=b, k=k):
                    at = pl.ds(targets * rows + k * slot_rows, slot_rows)
                    slot = b[pl.ds(coef_dev * rows, slot_rows), :]
                    own[at, :] = own[at, :] + slot
                    other[at, :] = other[at, :] + slot

        for kind, out in enumerate(outs):

            def listed(e, carry, b=b, out=out):
                code, w = lists[e], weights[e]
                row, target = lax.div(code, targets), lax.rem(code, targets)
                at = pl.ds(pl.multiple_of(target * rows, rows), rows)
                src = b[pl.ds(pl.multiple_of(row * rows, rows), rows), :]
                out[at, :] = out[at, :] + w * src
                return carry

            lax.fori_loop((2 * i + kind) * spaced, counts[2 * i + kind], listed, 0)


def sum_blocks(blocks, coef_dev, entries, rows, slot_rows, where, lists, so_far):
    scan, more, n = lists is None, so_far is not None, len(blocks)
    lanes = blocks[0].shape[1]
    size = coef_dev * M * rows + (M * slot_rows if scan else 0)
    total = jax.ShapeDtypeStruct((size, lanes), jnp.float32)
    out_shape, out_specs, scratch = [total, total], [VMEM, VMEM], []
    if scan:
        out_shape += [
            jax.ShapeDtypeStruct((2 * n * (entries + 1),), jnp.int32),
            jax.ShapeDtypeStruct((2 * n * (entries + 1),), jnp.float32),
            jax.ShapeDtypeStruct((2 * n,), jnp.int32),
        ]
        out_specs += [SMEM] * 3
        scratch = [
            pltpu.SMEM((n, TABLE_ROWS, lanes), jnp.float32),
            pltpu.SemaphoreType.DMA((n,)),
        ]
    small = [where] if scan else list(lists)
    operands = small + list(blocks) + (list(so_far) if more else [])
    got = pl.pallas_call(
        functools.partial(
            sum_kernel, n, coef_dev, entries, rows, slot_rows if scan else 0, scan, more
        ),
        out_shape=out_shape,
        in_specs=[SMEM] * len(small) + [VMEM] * (len(operands) - len(small)),
        out_specs=out_specs,
        scratch_shapes=scratch,
        compiler_params=pltpu.CompilerParams(vmem_limit_bytes=12 << 20),
        cost_estimate=cost(coef_dev * M, rows, lanes, 4),
    )(*operands)
    return got[:2], (lists if lists is not None else got[2:])


def exchange_pairs(count, inner, mask, keep=lambda o: True):
    return [
        (o * inner + i, (o ^ mask) * inner + i)
        for o in range(count)
        for i in range(inner)
        if keep(o)
    ]


def line_of_four(block, inner):
    middle = (1, 2)
    far = lax.ppermute(block, "chaos", exchange_pairs(4, inner, 2))
    near = lax.ppermute(block, "chaos", exchange_pairs(4, inner, 1))
    mid = lax.ppermute(block, "chaos", exchange_pairs(4, inner, 3, lambda o: o in middle))
    relay = lax.ppermute(far, "chaos", exchange_pairs(4, inner, 1, lambda o: o in middle))
    return near, far, mid, relay


def column_sums(coef_dev, entries, rows, slot_rows, wanted, owners):
    targets = coef_dev * M

    def sums(block, table, device):
        ids = table[:2, :entries].astype(jnp.int32)
        w = table[2, :entries]
        device_inner, source_row = ids[1] // (targets * coef_dev), ids[1] // targets % coef_dev
        target = ids[1] % targets
        picked = (source_row[:, None] == jnp.arange(coef_dev)[None, :]).astype(jnp.float32)
        found = []
        for who in wanted:
            mine = jnp.where((ids[0] == who[0] + 1) & (device_inner == who[1]), w, 0.0)
            onehot = (jnp.arange(targets)[:, None] == target[None, :]).astype(jnp.float32)
            matrix = jnp.sum(
                (onehot * mine[None, :])[:, :, None] * picked[None, :, :], axis=1
            )
            data = block[: coef_dev * rows].reshape(coef_dev, -1)
            found.append(
                jnp.dot(matrix, data, precision=lax.Precision.HIGHEST).reshape(
                    targets * rows, -1
                )
            )
        if slot_rows:
            slot = block[coef_dev * rows : coef_dev * rows + slot_rows]
            part = jnp.concatenate(
                [jnp.where(owners[k] == device, slot, 0.0) for k in range(M)], axis=0
            )
            found = [jnp.concatenate([f, part], axis=0) for f in found]
        return found

    return sums


def grid_of(count):
    inner = 2 if count % 2 == 0 else 1
    return count // inner, inner


def chaos_sums(chunks, coef_dev, entries, rows_of, slot_rows, mode_owner):
    outer, inner = grid_of(lax.axis_size("chaos"))
    me = lax.axis_index("chaos")
    my_outer, my_inner = me // inner, me % inner
    found = []
    if outer == 4:
        where = jnp.stack(
            [my_outer + 1, my_inner]
            + [mode_owner[k] for k in range(M)]
            + [(my_outer ^ mask) * inner + my_inner for mask in (0, 1, 2, 3, 3)]
        ).astype(jnp.int32)
        head = 2 + M
        relay_where = jnp.concatenate([where[:head], where[head + 4 :]])
        lists = late_lists = None
        gathered = [line_of_four(c, inner) for c in chunks]
        for j, (chunk, (near, far, mid, relay)) in enumerate(zip(chunks, gathered)):
            args = (coef_dev, entries, rows_of[j], slot_rows)
            sums, lists = sum_blocks([chunk, near, far, mid], *args, where, lists, None)
            sums, late_lists = sum_blocks([relay], *args, relay_where, late_lists, sums)
            found.append(sums)
    else:
        ring = [
            (o * inner + i, ((o + 1) % outer) * inner + i)
            for o in range(outer)
            for i in range(inner)
        ]
        table_at = coef_dev * rows_of[0] + slot_rows

        def at_step(step, blocks):
            device = ((my_outer - step) % outer) * inner + my_inner
            table = blocks[0][table_at : table_at + TABLE_ROWS]
            return [
                tuple(
                    column_sums(
                        coef_dev,
                        entries,
                        rows_of[j],
                        slot_rows if j == 0 else 0,
                        ((my_outer, my_inner), (my_outer, inner - 1 - my_inner)),
                        mode_owner,
                    )(block, table, device)
                )
                for j, block in enumerate(blocks)
            ]

        def body(step, carry):
            blocks, sums = carry
            blocks = [lax.ppermute(b, "chaos", ring) for b in blocks]
            return blocks, jax.tree.map(jnp.add, sums, at_step(step, blocks))

        _, found = lax.fori_loop(1, outer, body, (list(chunks), at_step(0, chunks)))
    if inner == 1:
        return [own for own, _ in found]
    across = [
        (o * inner + i, o * inner + inner - 1 - i) for o in range(outer) for i in range(inner)
    ]
    full = []
    for own, other in found:
        got = lax.ppermute(other, "chaos", across)
        full.append(own + got)
    return full


def depth_pair(values):
    count = lax.axis_size("space")
    first = [(i, i ^ 1) for i in range(count) if i ^ 1 < count]
    second = [
        (i, j)
        for i in range(count)
        for j in [i - 1 if i % 2 == 0 else i + 1]
        if 0 <= j < count
    ]
    other = lax.ppermute(values, "space", second)
    pair = lax.ppermute(values, "space", first)
    return other, pair


def base_kernel(coef_dev, depth, n_space, space_ref, coeffs, source, mean, *refs):
    other, pair, known, face, coef_ext, mean_ext = refs
    index = space_ref[0]
    even = lax.rem(index, 2) == 0
    pair_at = jnp.where(even, 2 * depth, 0)
    other_at = jnp.where(even, 0, 2 * depth)
    total_layers = 3 * depth
    planes = coef_dev * depth

    for at, part in ((pair_at, pair), (other_at, other)):
        for c in range(coef_dev):
            coef_ext[c, pl.ds(at, depth)] = part[c * depth : (c + 1) * depth]
        mean_ext[pl.ds(at, depth)] = part[2 * planes : 2 * planes + depth]
    for c in range(coef_dev):
        coef_ext[c, depth : 2 * depth] = coeffs[c]
    mean_ext[depth : 2 * depth] = mean[...]

    def layer(l, source_of):
        xm, xp, ym, yp, down, up, total = faces(mean_ext[l - 1], mean_ext[l], mean_ext[l + 1])
        diagonal = REACTION + total
        absolute = index * depth + l - depth
        inside = (absolute >= 0) & (absolute < n_space * depth)
        face[0, l], face[1, l], face[2, l], face[3, l] = xm, xp, ym, yp
        face[4, l], face[5, l] = down, up
        face[6, l] = jnp.where(inside, 1.0 / diagonal, 0.0)

        def coefficient(c, carry):
            v = coef_ext[c, l]
            spread = lateral(xm * v, xp * v, ym * v, yp * v)
            spread = spread + down * coef_ext[c, l - 1] + up * coef_ext[c, l + 1]
            known[c, l] = source_of(c) - (diagonal * v - spread)
            return carry

        for c in range(coef_dev):
            coefficient(c, 0)

    def from_part(part, at):
        def body(l, carry):
            layer(l, lambda c: part[planes + c * depth + l - at])
            return carry

        lax.fori_loop(jnp.maximum(at, 1), jnp.minimum(at + depth, total_layers - 1), body, 0)

    from_part(pair, pair_at)
    from_part(other, other_at)

    def body(l, carry):
        layer(l, lambda c: source[c, l - depth])
        return carry

    lax.fori_loop(depth, 2 * depth, body, 0)


def sweep_constants():
    midpoint = (BOUND_HIGH + BOUND_LOW) / 2.0
    halfwidth = (BOUND_HIGH - BOUND_LOW) / 2.0
    ratio = midpoint / halfwidth
    now = 1.0 / ratio
    steps = []
    for _ in range(ITERS - 1):
        following = 1.0 / (2.0 * ratio - now)
        steps.append((following * now, 2.0 * following / halfwidth))
        now = following
    return midpoint, steps


def sweep_kernel(coef_dev, depth, layer_counts, space_ref, known, face, *refs):
    n = len(layer_counts)
    parts = [refs[3 * j : 3 * j + 3] for j in range(n)]
    residual, correction, summed, mode_ext, mode_face, scaled, first, second = refs[3 * n :]
    nx, _ = known.shape[2:]
    targets = coef_dev * M
    even = lax.rem(space_ref[0], 2) == 0
    pair_at = jnp.where(even, 2 * depth, 0)
    other_at = jnp.where(even, 0, 2 * depth)
    last = 3 * depth - 1

    start = 0
    for j, (trio, layers) in enumerate(zip(parts, layer_counts)):
        for part, at in zip(trio, (depth, other_at, pair_at)):
            for t in range(targets):
                for l in range(layers):
                    row = (t * layers + l) * nx
                    summed[t, at + start + l] = part[row : row + nx]
            if j == 0:
                for k in range(M):
                    for l in range(depth):
                        row = (targets * layers + k * depth + l) * nx
                        mode_ext[k, at + l] = part[row : row + nx]
        start += layers

    def mode_faces(l, carry):
        for k in range(M):
            got = faces(mode_ext[k, l - 1], mode_ext[k, l], mode_ext[k, l + 1])
            for i, value in enumerate(got):
                mode_face[k, i, l] = value
        return carry

    lax.fori_loop(1, last, mode_faces, 0)
    midpoint, steps = sweep_constants()

    def coupled(l, own):
        for c in range(coef_dev):
            to = [None] * 4
            rest = known[c, l]
            for k in range(M):
                v = summed[c * M + k, l]
                for i in range(4):
                    term = mode_face[k, i, l] * v
                    to[i] = term if to[i] is None else to[i] + term
                rest = rest - mode_face[k, 6, l] * v
                rest = rest + mode_face[k, 4, l] * summed[c * M + k, l - 1]
                rest = rest + mode_face[k, 5, l] * summed[c * M + k, l + 1]
            rest = rest + lateral(*to)
            w = rest * face[6, l]
            d = w * (1.0 / midpoint)
            scaled[c, l] = w
            first[c, l] = d
            if own:
                residual[c, l - depth] = rest
                correction[c, l - depth] = d

    over_layers(coupled, depth, depth - 1)

    now, later = first, second
    for number, (keep, gain) in enumerate(steps):

        def swept(l, own, now=now, later=later, keep=keep, gain=gain, number=number):
            for c in range(coef_dev):
                v = now[c, l]
                spread = lateral(face[0, l] * v, face[1, l] * v, face[2, l] * v, face[3, l] * v)
                spread = spread + face[4, l] * now[c, l - 1] + face[5, l] * now[c, l + 1]
                w = scaled[c, l] - v + face[6, l] * spread
                d = keep * v + gain * w
                if number + 1 < len(steps):
                    scaled[c, l] = w
                    later[c, l] = d
                if own:
                    correction[c, l - depth] = correction[c, l - depth] + d

        over_layers(swept, depth, len(steps) - 1 - number)
        now, later = later, now


def over_layers(visit, depth, halo):
    def own(l, carry):
        visit(l, True)
        return carry

    def outside(i, carry):
        visit(jnp.where(i < halo, depth - halo + i, 2 * depth - halo + i), False)
        return carry

    lax.fori_loop(depth, 2 * depth, own, 0)
    if halo:
        lax.fori_loop(0, 2 * halo, outside, 0)


def residual_and_correction(coeffs, source, mean_field, mode_bank, mode_owner, links):
    coef_dev, depth, nx, ny = coeffs.shape
    n_space = lax.axis_size("space")
    entries = links.shape[1]
    slot_rows = depth * nx
    per_chunk = depth // CHUNKS
    layer_counts = [per_chunk] * CHUNKS
    index = lax.axis_index("space").astype(jnp.int32).reshape(1)

    rows_of = [layers * nx for layers in layer_counts]
    inner = grid_of(lax.axis_size("chaos"))[1]
    chunks = [pack(coeffs, mode_bank, links[0], rows_of[0], inner)]
    start = layer_counts[0]
    for layers in layer_counts[1:]:
        chunks.append(coeffs[:, start : start + layers].reshape(-1, ny))
        start += layers

    sums = chaos_sums(
        chunks, coef_dev, entries, rows_of, slot_rows, mode_owner
    )

    early = jnp.concatenate(
        [coeffs.reshape(-1, nx, ny), source.reshape(-1, nx, ny), mean_field], axis=0
    )
    other, pair = depth_pair(early)
    wide = (coef_dev, 3 * depth, nx, ny)
    known, face = pl.pallas_call(
        functools.partial(base_kernel, coef_dev, depth, n_space),
        out_shape=(
            jax.ShapeDtypeStruct(wide, jnp.float32),
            jax.ShapeDtypeStruct((7, 3 * depth, nx, ny), jnp.float32),
        ),
        in_specs=[SMEM] + [VMEM] * 5,
        out_specs=(VMEM, VMEM),
        scratch_shapes=[
            pltpu.VMEM(wide, jnp.float32),
            pltpu.VMEM((3 * depth, nx, ny), jnp.float32),
        ],
        cost_estimate=cost(3 * depth * coef_dev, nx, ny, 20),
        compiler_params=pltpu.CompilerParams(vmem_limit_bytes=16 << 20),
        name="base",
    )(index, coeffs, source, mean_field, other, pair)

    parts = []
    for own in sums:
        parts += [own, *depth_pair(own)]
    out = jax.ShapeDtypeStruct(coeffs.shape, jnp.float32)
    return pl.pallas_call(
        functools.partial(sweep_kernel, coef_dev, depth, layer_counts),
        out_shape=(out, out),
        in_specs=[SMEM] + [VMEM] * (2 + len(parts)),
        out_specs=(VMEM, VMEM),
        scratch_shapes=[
            pltpu.VMEM((coef_dev * M, 3 * depth, nx, ny), jnp.float32),
            pltpu.VMEM((M, 3 * depth, nx, ny), jnp.float32),
            pltpu.VMEM((M, 7, 3 * depth, nx, ny), jnp.float32),
            pltpu.VMEM(wide, jnp.float32),
            pltpu.VMEM(wide, jnp.float32),
            pltpu.VMEM(wide, jnp.float32),
        ],
        cost_estimate=cost(6 * depth * coef_dev, nx, ny, 40),
        compiler_params=pltpu.CompilerParams(vmem_limit_bytes=24 << 20),
        name="sweeps",
    )(index, known, face, *parts)


def solution(mesh):
    in_specs = (
        P("chaos", "space", None, None),
        P("chaos", "space", None, None),
        P("space", None, None),
        P("chaos", "space", None, None),
        P(),
        P("chaos", None, None),
    )
    out_specs = (P("chaos", "space", None, None), P("chaos", "space", None, None))
    return jax.shard_map(
        residual_and_correction, mesh=mesh, in_specs=in_specs, out_specs=out_specs, check_vma=False
    )
```

```python
import functools

import jax
import jax.numpy as jnp
from jax import lax
from jax.experimental import pallas as pl
from jax.experimental.pallas import tpu as pltpu
from jax.sharding import PartitionSpec as P


M = 2
ITERS = 4

REACTION = 0.5
BOUND_LOW = 0.04
BOUND_HIGH = 2.0

CHUNKS = 2
TABLE_ROWS = 8


VMEM = pl.BlockSpec(memory_space=pltpu.VMEM)
SMEM = pl.BlockSpec(memory_space=pltpu.SMEM)


def cost(planes, nx, ny, flops):
    return pl.CostEstimate(
        flops=flops * planes * nx * ny, bytes_accessed=8 * planes * nx * ny, transcendentals=0
    )


def shifted(values, axis, step):
    return pltpu.roll(values, step % values.shape[axis], axis)


def faces(below, own, above):
    nx, ny = own.shape
    ix = lax.broadcasted_iota(jnp.int32, (nx, ny), 0)
    iy = lax.broadcasted_iota(jnp.int32, (nx, ny), 1)
    half = 0.5 * own
    zero = jnp.zeros_like(own)
    xm = jnp.where(ix == 0, zero, half + shifted(half, 0, 1))
    xp = jnp.where(ix == nx - 1, zero, half + shifted(half, 0, -1))
    ym = jnp.where(iy == 0, zero, half + shifted(half, 1, 1))
    yp = jnp.where(iy == ny - 1, zero, half + shifted(half, 1, -1))
    up = half + 0.5 * above
    down = half + 0.5 * below
    total = up + down
    total = total + jnp.where(ix == 0, half, xm) + jnp.where(ix == nx - 1, half, xp)
    total = total + jnp.where(iy == 0, half, ym) + jnp.where(iy == ny - 1, half, yp)
    return xm, xp, ym, yp, down, up, total


def lateral(to_xm, to_xp, to_ym, to_yp):
    return (
        shifted(to_xm, 0, -1)
        + shifted(to_xp, 0, 1)
        + shifted(to_ym, 1, -1)
        + shifted(to_yp, 1, 1)
    )


def pack_kernel(coef_dev, capacity, rows_of, slot_rows, links, coeffs, bank, *refs):
    blocks, (sems,) = refs[: len(rows_of)], refs[len(rows_of) :]
    slot = blocks[0].at[pl.ds(coef_dev * rows_of[0], slot_rows)]
    copies = [pltpu.make_async_copy(bank.at[0], slot, sems.at[len(rows_of) * coef_dev])]
    start = 0
    for j, (block, rows) in enumerate(zip(blocks, rows_of)):
        for c in range(coef_dev):
            copies.append(
                pltpu.make_async_copy(
                    coeffs.at[c, pl.ds(start, rows)],
                    block.at[pl.ds(c * rows, rows)],
                    sems.at[j * coef_dev + c],
                )
            )
        start += rows
    for copy in copies:
        copy.start()
    entries, lanes = links.shape[1], blocks[0].shape[1]
    listed = links[...].astype(jnp.float32)
    s, p, k, level = (listed[i : i + 1] for i in range(4))
    device = jnp.floor((p + 0.5) * (1.0 / coef_dev))
    code = (s * coef_dev + p - device * coef_dev) * M + k
    square = (entries, entries)
    row = lax.broadcasted_iota(jnp.int32, square, 0)
    column = lax.broadcasted_iota(jnp.int32, square, 1)

    def upright(values):
        return jnp.sum(jnp.where(row == column, values, 0.0), axis=1, keepdims=True)

    device_up, level_up = upright(device), upright(level)
    earlier = (device == device_up) & (level > 0.0) & (column < row)
    rank = jnp.sum(jnp.where(earlier, 1.0, 0.0), axis=1, keepdims=True)
    place = jnp.where(level_up > 0.0, device_up * capacity + rank, -1.0)
    lane = lax.broadcasted_iota(jnp.int32, (entries, lanes), 1).astype(jnp.float32)
    table = [
        jnp.sum(jnp.where(place == lane, values, 0.0), axis=0, keepdims=True)
        for values in (upright(code), jnp.sqrt(level_up))
    ]
    table.append(jnp.zeros((TABLE_ROWS - len(table), lanes), jnp.float32))
    table = jnp.concatenate(table, axis=0)
    for block in blocks:
        block[pl.ds(block.shape[0] - TABLE_ROWS, TABLE_ROWS), :] = table
    for copy in copies:
        copy.wait()


def pack(coeffs, bank, links, capacity, rows_of):
    coef_dev, lanes = coeffs.shape[0], coeffs.shape[3]
    whole_rows = coeffs.reshape(coef_dev, -1, lanes)
    slot = bank.reshape(1, -1, lanes)
    slot_rows = slot.shape[1]
    hbm = pl.BlockSpec(memory_space=pltpu.HBM)
    sizes = [
        coef_dev * rows + (slot_rows if j == 0 else 0) + TABLE_ROWS
        for j, rows in enumerate(rows_of)
    ]
    return pl.pallas_call(
        functools.partial(pack_kernel, coef_dev, capacity, rows_of, slot_rows),
        out_shape=[jax.ShapeDtypeStruct((size, lanes), jnp.float32) for size in sizes],
        in_specs=[VMEM, hbm, hbm],
        out_specs=[VMEM] * len(sizes),
        scratch_shapes=[pltpu.SemaphoreType.DMA((len(sizes) * coef_dev + 1,))],
        cost_estimate=cost(coef_dev, sum(rows_of), lanes, 1),
        name="pack",
    )(links.T, whole_rows, slot)


def sum_kernel(n, coef_dev, capacity, rows, slot_rows, more, where, *refs):
    refs = list(refs)
    blocks = [refs.pop(0) for _ in range(n)]
    so_far = refs.pop(0) if more else None
    out, tables, sems = refs
    targets = coef_dev * M
    copies = [
        pltpu.make_async_copy(
            block.at[pl.ds(block.shape[0] - TABLE_ROWS, TABLE_ROWS)], tables.at[i], sems.at[i]
        )
        for i, block in enumerate(blocks)
    ]
    for copy in copies:
        copy.start()
    out[...] = so_far[...] if more else jnp.zeros_like(out)
    if slot_rows:
        for i, block in enumerate(blocks):
            for k in range(M):

                @pl.when(where[1 + k] == where[1 + M + i])
                def _(block=block, k=k):
                    at = pl.ds(targets * rows + k * slot_rows, slot_rows)
                    out[at, :] = block[pl.ds(coef_dev * rows, slot_rows), :]

    begin = where[0] * capacity
    for i, block in enumerate(blocks):
        copies[i].wait()

        def listed(e, carry, i=i, block=block):
            code, w = tables[i, 0, e].astype(jnp.int32), tables[i, 1, e]
            row, target = lax.div(code, targets), lax.rem(code, targets)
            at = pl.ds(pl.multiple_of(target * rows, rows), rows)
            src = block[pl.ds(pl.multiple_of(row * rows, rows), rows), :]
            out[at, :] = out[at, :] + w * src
            return carry

        lax.fori_loop(begin, begin + capacity, listed, 0)


def sum_blocks(blocks, devices, me, mode_owner, coef_dev, capacity, rows, slot_rows, so_far):
    n, lanes = len(blocks), blocks[0].shape[1]
    size = coef_dev * M * rows + M * slot_rows
    where = jnp.stack([me] + [mode_owner[k] for k in range(M)] + devices).astype(jnp.int32)
    more = so_far is not None
    return pl.pallas_call(
        functools.partial(
            sum_kernel, n, coef_dev, capacity, rows, slot_rows, more
        ),
        out_shape=jax.ShapeDtypeStruct((size, lanes), jnp.float32),
        in_specs=[SMEM] + [VMEM] * (n + more),
        out_specs=VMEM,
        scratch_shapes=[
            pltpu.SMEM((n, TABLE_ROWS, lanes), jnp.float32),
            pltpu.SemaphoreType.DMA((n,)),
        ],
        compiler_params=pltpu.CompilerParams(vmem_limit_bytes=12 << 20),
        cost_estimate=cost(coef_dev * M, rows, lanes, 4),
    )(where, *blocks, *([so_far] if more else []))


def plain_sums(block, table, mode_slot, device, me, mode_owner, coef_dev, capacity, rows):
    targets = coef_dev * M
    code = lax.dynamic_slice(table[0], (me * capacity,), (capacity,)).astype(jnp.int32)
    w = lax.dynamic_slice(table[1], (me * capacity,), (capacity,))
    row = (code[:, None] // targets == jnp.arange(coef_dev)[None, :]).astype(jnp.float32)
    target = (code[:, None] % targets == jnp.arange(targets)[None, :]).astype(jnp.float32)
    matrix = jnp.sum((target * w[:, None])[:, :, None] * row[:, None, :], axis=0)
    data = block[: coef_dev * rows].reshape(coef_dev, -1)
    found = jnp.dot(matrix, data, precision=lax.Precision.HIGHEST)
    found = found.reshape(targets * rows, -1)
    if mode_slot is None:
        return found
    modes = [jnp.where(mode_owner[k] == device, mode_slot, 0.0) for k in range(M)]
    return jnp.concatenate([found, *modes], axis=0)


def unrolled(count):
    return count % 2 == 0 and count <= 16


def ring_order(count):
    return list(range(0, count, 2)) + list(range(count - 1, 0, -2))


def ring_steps(count):
    half = count // 2
    return [
        (half, half - 1) if j == 0 else (half - 1, half) for j in range(CHUNKS)
    ]


def chaos_sums(chunks, coef_dev, capacity, rows_of, slot_rows, mode_owner):
    count = lax.axis_size("chaos")
    me = lax.axis_index("chaos")
    fixed = (me, mode_owner, coef_dev, capacity)
    if not unrolled(count):
        ring = [(i, (i + 1) % count) for i in range(count)]

        def at_step(step, blocks):
            device = (me - step) % count
            slot_at = coef_dev * rows_of[0]
            table, slot = blocks[0][-TABLE_ROWS:], blocks[0][slot_at : slot_at + slot_rows]
            return [
                plain_sums(b, table, slot if j == 0 else None, device, *fixed, rows_of[j])
                for j, b in enumerate(blocks)
            ]

        def body(step, carry):
            blocks, sums = carry
            blocks = [lax.ppermute(b, "chaos", ring) for b in blocks]
            return blocks, jax.tree.map(jnp.add, sums, at_step(step, blocks))

        return lax.fori_loop(1, count, body, (list(chunks), at_step(0, chunks)))[1]

    order = ring_order(count)
    there = [(order[i], order[(i + 1) % count]) for i in range(count)]
    back = [(b, a) for a, b in there]
    half = count // 2
    place = jnp.where(me % 2 == 0, me // 2, count - 1 - me // 2)

    def device_at(shift):
        q = (place + shift) % count
        return jnp.where(q < half, 2 * q, 2 * (count - 1 - q) + 1)

    gathered = []
    for chunk, steps in zip(chunks, ring_steps(count)):
        blocks = {0: chunk}
        for pairs, sign, n_steps in ((there, -1, steps[0]), (back, 1, steps[1])):
            block = chunk
            for step in range(1, n_steps + 1):
                block = lax.ppermute(block, "chaos", pairs)
                blocks[sign * step] = block
        gathered.append({shift % count: block for shift, block in blocks.items()})
    early = [0] + [s for step in range(1, half - 1) for s in (step, count - step)]
    late = [s for s in range(count) if s not in early]
    found = []
    for j, blocks in enumerate(gathered):
        sums = None
        for shifts in (early, late):
            sums = sum_blocks(
                [blocks[s] for s in shifts],
                [device_at(s) for s in shifts],
                *fixed,
                rows_of[j],
                slot_rows if j == 0 else 0,
                sums,
            )
        found.append(sums)
    return found


def depth_pair(values):
    count = lax.axis_size("space")
    first = [(i, i ^ 1) for i in range(count) if i ^ 1 < count]
    second = [
        (i, j)
        for i in range(count)
        for j in [i - 1 if i % 2 == 0 else i + 1]
        if 0 <= j < count
    ]
    other = lax.ppermute(values, "space", second)
    pair = lax.ppermute(values, "space", first)
    return other, pair


def base_kernel(coef_dev, depth, n_space, space_ref, coeffs, source, mean, *refs):
    other, pair, known, face, coef_ext, mean_ext = refs
    index = space_ref[0]
    even = lax.rem(index, 2) == 0
    pair_at = jnp.where(even, 2 * depth, 0)
    other_at = jnp.where(even, 0, 2 * depth)
    total_layers = 3 * depth
    planes = coef_dev * depth

    for at, part in ((pair_at, pair), (other_at, other)):
        for c in range(coef_dev):
            coef_ext[c, pl.ds(at, depth)] = part[c * depth : (c + 1) * depth]
        mean_ext[pl.ds(at, depth)] = part[2 * planes : 2 * planes + depth]
    for c in range(coef_dev):
        coef_ext[c, depth : 2 * depth] = coeffs[c]
    mean_ext[depth : 2 * depth] = mean[...]

    def layer(l, source_of):
        xm, xp, ym, yp, down, up, total = faces(mean_ext[l - 1], mean_ext[l], mean_ext[l + 1])
        diagonal = REACTION + total
        absolute = index * depth + l - depth
        inside = (absolute >= 0) & (absolute < n_space * depth)
        face[0, l], face[1, l], face[2, l], face[3, l] = xm, xp, ym, yp
        face[4, l], face[5, l] = down, up
        face[6, l] = jnp.where(inside, 1.0 / diagonal, 0.0)

        def coefficient(c, carry):
            v = coef_ext[c, l]
            spread = lateral(xm * v, xp * v, ym * v, yp * v)
            spread = spread + down * coef_ext[c, l - 1] + up * coef_ext[c, l + 1]
            known[c, l] = source_of(c) - (diagonal * v - spread)
            return carry

        for c in range(coef_dev):
            coefficient(c, 0)

    def from_part(part, at):
        def body(l, carry):
            layer(l, lambda c: part[planes + c * depth + l - at])
            return carry

        lax.fori_loop(jnp.maximum(at, 1), jnp.minimum(at + depth, total_layers - 1), body, 0)

    from_part(pair, pair_at)
    from_part(other, other_at)

    def body(l, carry):
        layer(l, lambda c: source[c, l - depth])
        return carry

    lax.fori_loop(depth, 2 * depth, body, 0)


def sweep_constants():
    midpoint = (BOUND_HIGH + BOUND_LOW) / 2.0
    halfwidth = (BOUND_HIGH - BOUND_LOW) / 2.0
    ratio = midpoint / halfwidth
    now = 1.0 / ratio
    steps = []
    for _ in range(ITERS - 1):
        following = 1.0 / (2.0 * ratio - now)
        steps.append((following * now, 2.0 * following / halfwidth))
        now = following
    return midpoint, steps


def order_parts(trio, even, n, layers, summed, nx):
    for part, slab in zip(trio, (1, jnp.where(even, 0, 2), jnp.where(even, 2, 0))):
        for t in range(n):
            at = t * layers * nx
            summed[slab, t] = part[at : at + layers * nx].reshape(layers, nx, -1)


def coupled(l, depth, start, layers, coef_dev, summed, mode_face, visit):
    slab, at = divmod(l, depth)
    near = {}
    for offset in (-1, 0, 1):
        s, i = divmod(l + offset, depth)
        if 0 <= s < 3 and start <= i < start + layers:
            near[offset] = (s, i - start)
    if not near:
        return False
    for c in range(coef_dev):
        to, rest = [None] * 4, None

        def add(total, term):
            return term if total is None else total + term

        for k in range(M):
            if 0 in near:
                s, i = near[0]
                v = summed[s, c * M + k, i]
                for q in range(4):
                    to[q] = add(to[q], mode_face[k, q, l] * v)
                rest = add(rest, -(mode_face[k, 6, l] * v))
            for offset, which in ((-1, 4), (1, 5)):
                if offset in near:
                    s, i = near[offset]
                    rest = add(rest, mode_face[k, which, l] * summed[s, c * M + k, i])
        visit(c, rest + lateral(*to) if 0 in near else rest)
    return True


def begin_kernel(coef_dev, depth, layers, space_ref, known, own, other, pair, *refs):
    rest, mode_face, summed, mode_ext = refs
    nx = known.shape[2]
    targets = coef_dev * M
    even = lax.rem(space_ref[0], 2) == 0
    order_parts((own, other, pair), even, targets, layers, summed, nx)
    for part, slab in zip(
        (own, other, pair), (1, jnp.where(even, 0, 2), jnp.where(even, 2, 0))
    ):
        for k in range(M):
            at = (targets * layers + k * depth) * nx
            mode_ext[k, pl.ds(slab * depth, depth)] = part[at : at + depth * nx].reshape(
                depth, nx, -1
            )
    last = 3 * depth - 1

    def mode_faces(l, carry):
        for k in range(M):
            got = faces(mode_ext[k, l - 1], mode_ext[k, l], mode_ext[k, l + 1])
            for i, value in enumerate(got):
                mode_face[k, i, l] = value
        return carry

    lax.fori_loop(1, last, mode_faces, 0)
    for l in range(1, last):

        def visit(c, value, l=l):
            rest[c, l] = known[c, l] + value

        if not coupled(l, depth, 0, layers, coef_dev, summed, mode_face, visit):
            for c in range(coef_dev):
                rest[c, l] = known[c, l]


def sweep_kernel(coef_dev, depth, start, layers, space_ref, rest, mode_face, face, *refs):
    own, other, pair, residual, correction, summed, scaled, first, second = refs
    nx = rest.shape[2]
    even = lax.rem(space_ref[0], 2) == 0
    order_parts((own, other, pair), even, coef_dev * M, layers, summed, nx)
    last = 3 * depth - 1
    midpoint, steps = sweep_constants()
    for l in range(1, last):

        def visit(c, value, l=l):
            total = rest[c, l] if value is None else rest[c, l] + value
            w = total * face[6, l]
            d = w * (1.0 / midpoint)
            scaled[c, l] = w
            first[c, l] = d
            if depth <= l < 2 * depth:
                residual[c, l - depth] = total
                correction[c, l - depth] = d

        if not coupled(l, depth, start, layers, coef_dev, summed, mode_face, visit):
            for c in range(coef_dev):
                visit(c, None)

    now, later = first, second
    for number, (keep, gain) in enumerate(steps):

        def swept(l, own, now=now, later=later, keep=keep, gain=gain, number=number):
            for c in range(coef_dev):
                v = now[c, l]
                spread = lateral(face[0, l] * v, face[1, l] * v, face[2, l] * v, face[3, l] * v)
                spread = spread + face[4, l] * now[c, l - 1] + face[5, l] * now[c, l + 1]
                w = scaled[c, l] - v + face[6, l] * spread
                d = keep * v + gain * w
                if number + 1 < len(steps):
                    scaled[c, l] = w
                    later[c, l] = d
                if own:
                    correction[c, l - depth] = correction[c, l - depth] + d

        over_layers(swept, depth, len(steps) - 1 - number)
        now, later = later, now


def over_layers(visit, depth, halo):
    def own(l, carry):
        visit(l, True)
        return carry

    def outside(i, carry):
        visit(jnp.where(i < halo, depth - halo + i, 2 * depth - halo + i), False)
        return carry

    lax.fori_loop(depth, 2 * depth, own, 0)
    if halo:
        lax.fori_loop(0, 2 * halo, outside, 0)


def residual_and_correction(coeffs, source, mean_field, mode_bank, mode_owner, links):
    coef_dev, depth, nx, ny = coeffs.shape
    n_space = lax.axis_size("space")
    slot_rows = depth * nx
    per_chunk = depth // CHUNKS
    layer_counts = [per_chunk] * CHUNKS
    index = lax.axis_index("space").astype(jnp.int32).reshape(1)

    rows_of = [layers * nx for layers in layer_counts]
    count = lax.axis_size("chaos")
    shifts = count // 2 - 1
    capacity = max(2, (M * coef_dev - 1 + shifts - 1) // shifts)
    assert count * capacity <= ny
    chunks = pack(coeffs, mode_bank, links[0], capacity, rows_of)

    sums = chaos_sums(
        chunks, coef_dev, capacity, rows_of, slot_rows, mode_owner
    )

    early = jnp.concatenate(
        [coeffs.reshape(-1, nx, ny), source.reshape(-1, nx, ny), mean_field], axis=0
    )
    other, pair = depth_pair(early)
    wide = (coef_dev, 3 * depth, nx, ny)
    known, face = pl.pallas_call(
        functools.partial(base_kernel, coef_dev, depth, n_space),
        out_shape=(
            jax.ShapeDtypeStruct(wide, jnp.float32),
            jax.ShapeDtypeStruct((7, 3 * depth, nx, ny), jnp.float32),
        ),
        in_specs=[SMEM] + [VMEM] * 5,
        out_specs=(VMEM, VMEM),
        scratch_shapes=[
            pltpu.VMEM(wide, jnp.float32),
            pltpu.VMEM((3 * depth, nx, ny), jnp.float32),
        ],
        cost_estimate=cost(3 * depth * coef_dev, nx, ny, 20),
        compiler_params=pltpu.CompilerParams(vmem_limit_bytes=16 << 20),
        name="base",
    )(index, coeffs, source, mean_field, other, pair)

    parts = [[own, *depth_pair(own)] for own in sums]
    layers = layer_counts[0]
    ordered = pltpu.VMEM((3, coef_dev * M, layers, nx, ny), jnp.float32)
    mode_faces = (M, 7, 3 * depth, nx, ny)
    rest, mode_face = pl.pallas_call(
        functools.partial(begin_kernel, coef_dev, depth, layers),
        out_shape=(
            jax.ShapeDtypeStruct(wide, jnp.float32),
            jax.ShapeDtypeStruct(mode_faces, jnp.float32),
        ),
        in_specs=[SMEM] + [VMEM] * 4,
        out_specs=(VMEM, VMEM),
        scratch_shapes=[ordered, pltpu.VMEM((M, 3 * depth, nx, ny), jnp.float32)],
        compiler_params=pltpu.CompilerParams(vmem_limit_bytes=16 << 20),
        cost_estimate=cost(3 * depth * coef_dev, nx, ny, 40),
        name="begin",
    )(index, known, *parts[0])
    out = jax.ShapeDtypeStruct(coeffs.shape, jnp.float32)
    return pl.pallas_call(
        functools.partial(sweep_kernel, coef_dev, depth, depth - layers, layers),
        out_shape=(out, out),
        in_specs=[SMEM] + [VMEM] * 6,
        out_specs=(VMEM, VMEM),
        scratch_shapes=[ordered] + [pltpu.VMEM(wide, jnp.float32)] * 3,
        compiler_params=pltpu.CompilerParams(vmem_limit_bytes=20 << 20),
        cost_estimate=cost(6 * depth * coef_dev, nx, ny, 40),
        name="sweeps",
    )(index, rest, mode_face, face, *parts[1])


def solution(mesh):
    in_specs = (
        P("chaos", "space", None, None),
        P("chaos", "space", None, None),
        P("space", None, None),
        P("chaos", "space", None, None),
        P(),
        P("chaos", None, None),
    )
    out_specs = (P("chaos", "space", None, None), P("chaos", "space", None, None))
    return jax.shard_map(
        residual_and_correction, mesh=mesh, in_specs=in_specs, out_specs=out_specs, check_vma=False
    )
```

```python
import functools

import jax
import jax.numpy as jnp
from jax import lax
from jax.experimental import pallas as pl
from jax.experimental.pallas import tpu as pltpu
from jax.sharding import PartitionSpec as P


M = 2
ITERS = 4

REACTION = 0.5
BOUND_LOW = 0.04
BOUND_HIGH = 2.0

CHUNKS = 2
TABLE_ROWS = 8


VMEM = pl.BlockSpec(memory_space=pltpu.VMEM)
SMEM = pl.BlockSpec(memory_space=pltpu.SMEM)


def cost(planes, nx, ny, flops):
    return pl.CostEstimate(
        flops=flops * planes * nx * ny, bytes_accessed=8 * planes * nx * ny, transcendentals=0
    )


def shifted(values, axis, step):
    return pltpu.roll(values, step % values.shape[axis], axis)


def faces(below, own, above):
    nx, ny = own.shape
    ix = lax.broadcasted_iota(jnp.int32, (nx, ny), 0)
    iy = lax.broadcasted_iota(jnp.int32, (nx, ny), 1)
    half = 0.5 * own
    zero = jnp.zeros_like(own)
    xm = jnp.where(ix == 0, zero, half + shifted(half, 0, 1))
    xp = jnp.where(ix == nx - 1, zero, half + shifted(half, 0, -1))
    ym = jnp.where(iy == 0, zero, half + shifted(half, 1, 1))
    yp = jnp.where(iy == ny - 1, zero, half + shifted(half, 1, -1))
    up = half + 0.5 * above
    down = half + 0.5 * below
    total = up + down
    total = total + jnp.where(ix == 0, half, xm) + jnp.where(ix == nx - 1, half, xp)
    total = total + jnp.where(iy == 0, half, ym) + jnp.where(iy == ny - 1, half, yp)
    return xm, xp, ym, yp, down, up, total


def lateral(to_xm, to_xp, to_ym, to_yp):
    return (
        shifted(to_xm, 0, -1)
        + shifted(to_xp, 0, 1)
        + shifted(to_ym, 1, -1)
        + shifted(to_yp, 1, 1)
    )


def pack_kernel(coef_dev, capacity, rows_of, slot_rows, links, coeffs, bank, *refs):
    blocks, (sems,) = refs[: len(rows_of)], refs[len(rows_of) :]
    slot = blocks[0].at[pl.ds(coef_dev * rows_of[0], slot_rows)]
    copies = [pltpu.make_async_copy(bank.at[0], slot, sems.at[len(rows_of) * coef_dev])]
    start = 0
    for j, (block, rows) in enumerate(zip(blocks, rows_of)):
        for c in range(coef_dev):
            copies.append(
                pltpu.make_async_copy(
                    coeffs.at[c, pl.ds(start, rows)],
                    block.at[pl.ds(c * rows, rows)],
                    sems.at[j * coef_dev + c],
                )
            )
        start += rows
    for copy in copies:
        copy.start()
    entries, lanes = links.shape[1], blocks[0].shape[1]
    listed = links[...].astype(jnp.float32)
    s, p, k, level = (listed[i : i + 1] for i in range(4))
    device = jnp.floor((p + 0.5) * (1.0 / coef_dev))
    code = (s * coef_dev + p - device * coef_dev) * M + k
    square = (entries, entries)
    row = lax.broadcasted_iota(jnp.int32, square, 0)
    column = lax.broadcasted_iota(jnp.int32, square, 1)

    def upright(values):
        return jnp.sum(jnp.where(row == column, values, 0.0), axis=1, keepdims=True)

    device_up, level_up = upright(device), upright(level)
    earlier = (device == device_up) & (level > 0.0) & (column < row)
    rank = jnp.sum(jnp.where(earlier, 1.0, 0.0), axis=1, keepdims=True)
    place = jnp.where(level_up > 0.0, device_up * capacity + rank, -1.0)
    lane = lax.broadcasted_iota(jnp.int32, (entries, lanes), 1).astype(jnp.float32)
    table = [
        jnp.sum(jnp.where(place == lane, values, 0.0), axis=0, keepdims=True)
        for values in (upright(code), jnp.sqrt(level_up))
    ]
    table.append(jnp.zeros((TABLE_ROWS - len(table), lanes), jnp.float32))
    table = jnp.concatenate(table, axis=0)
    for block in blocks:
        block[pl.ds(block.shape[0] - TABLE_ROWS, TABLE_ROWS), :] = table
    for copy in copies:
        copy.wait()


def pack(coeffs, bank, links, capacity, rows_of):
    coef_dev, lanes = coeffs.shape[0], coeffs.shape[3]
    whole_rows = coeffs.reshape(coef_dev, -1, lanes)
    slot = bank.reshape(1, -1, lanes)
    slot_rows = slot.shape[1]
    hbm = pl.BlockSpec(memory_space=pltpu.HBM)
    sizes = [
        coef_dev * rows + (slot_rows if j == 0 else 0) + TABLE_ROWS
        for j, rows in enumerate(rows_of)
    ]
    return pl.pallas_call(
        functools.partial(pack_kernel, coef_dev, capacity, rows_of, slot_rows),
        out_shape=[jax.ShapeDtypeStruct((size, lanes), jnp.float32) for size in sizes],
        in_specs=[VMEM, hbm, hbm],
        out_specs=[VMEM] * len(sizes),
        scratch_shapes=[pltpu.SemaphoreType.DMA((len(sizes) * coef_dev + 1,))],
        cost_estimate=cost(coef_dev, sum(rows_of), lanes, 1),
        name="pack",
    )(links.T, whole_rows, slot)


def start_tables(blocks, tables, sems):
    copies = []
    for i, block in enumerate(blocks):
        at = pl.ds(block.shape[0] - TABLE_ROWS, TABLE_ROWS)
        copies.append(pltpu.make_async_copy(block.at[at], tables.at[i], sems.at[i]))
        copies[-1].start()
    return copies


def table_scratch(n, lanes):
    return [pltpu.SMEM((n, TABLE_ROWS, lanes), jnp.float32), pltpu.SemaphoreType.DMA((n,))]


def pick_kernel(coef_dev, capacity, rows, begin, block, out, tables, sems):
    (copy,) = start_tables([block], tables, sems)
    out[capacity * rows :, :] = block[coef_dev * rows :, :]
    copy.wait()
    for e in range(capacity):
        row = lax.div(tables[0, 0, begin[0] + e].astype(jnp.int32), coef_dev * M)
        out[e * rows : (e + 1) * rows, :] = block[
            pl.ds(pl.multiple_of(row * rows, rows), rows), :
        ]


def pick(block, device, coef_dev, capacity, rows):
    size, lanes = block.shape
    return pl.pallas_call(
        functools.partial(pick_kernel, coef_dev, capacity, rows),
        out_shape=jax.ShapeDtypeStruct((size - (coef_dev - capacity) * rows, lanes), jnp.float32),
        in_specs=[SMEM, VMEM],
        out_specs=VMEM,
        scratch_shapes=table_scratch(1, lanes),
        compiler_params=pltpu.CompilerParams(vmem_limit_bytes=8 << 20),
        cost_estimate=cost(capacity, rows, lanes, 1),
        name="pick",
    )((device * capacity).astype(jnp.int32).reshape(1), block)


def sum_kernel(picked, coef_dev, capacity, rows, slot_rows, more, where, *refs):
    refs = list(refs)
    blocks = [refs.pop(0) for _ in picked]
    so_far = refs.pop(0) if more else None
    out, tables, sems = refs
    targets = coef_dev * M
    copies = start_tables(blocks, tables, sems)
    out[...] = so_far[...] if more else jnp.zeros_like(out)
    if slot_rows:
        for i, (block, few) in enumerate(zip(blocks, picked)):
            for k in range(M):

                @pl.when(where[1 + k] == where[1 + M + i])
                def _(block=block, k=k, few=few):
                    at = pl.ds(targets * rows + k * slot_rows, slot_rows)
                    out[at, :] = block[pl.ds((capacity if few else coef_dev) * rows, slot_rows), :]

    begin = where[0] * capacity
    for i, (block, few) in enumerate(zip(blocks, picked)):
        copies[i].wait()
        for e in range(capacity):
            code, w = tables[i, 0, begin + e].astype(jnp.int32), tables[i, 1, begin + e]
            row, target = e if few else lax.div(code, targets), lax.rem(code, targets)
            at = pl.ds(pl.multiple_of(target * rows, rows), rows)
            src = block[pl.ds(pl.multiple_of(row * rows, rows), rows), :]
            out[at, :] = out[at, :] + w * src


def sum_blocks(
    blocks, picked, devices, me, mode_owner, coef_dev, capacity, rows, slot_rows, so_far
):
    n, lanes = len(blocks), blocks[0].shape[1]
    size = coef_dev * M * rows + M * slot_rows
    where = jnp.stack([me] + [mode_owner[k] for k in range(M)] + devices).astype(jnp.int32)
    more = so_far is not None
    return pl.pallas_call(
        functools.partial(sum_kernel, picked, coef_dev, capacity, rows, slot_rows, more),
        out_shape=jax.ShapeDtypeStruct((size, lanes), jnp.float32),
        in_specs=[SMEM] + [VMEM] * (n + more),
        out_specs=VMEM,
        scratch_shapes=table_scratch(n, lanes),
        compiler_params=pltpu.CompilerParams(vmem_limit_bytes=12 << 20),
        cost_estimate=cost(coef_dev * M, rows, lanes, 4),
    )(where, *blocks, *([so_far] if more else []))


def plain_sums(block, table, mode_slot, device, me, mode_owner, coef_dev, capacity, rows):
    targets = coef_dev * M
    code = lax.dynamic_slice(table[0], (me * capacity,), (capacity,)).astype(jnp.int32)
    w = lax.dynamic_slice(table[1], (me * capacity,), (capacity,))
    row = (code[:, None] // targets == jnp.arange(coef_dev)[None, :]).astype(jnp.float32)
    target = (code[:, None] % targets == jnp.arange(targets)[None, :]).astype(jnp.float32)
    matrix = jnp.sum((target * w[:, None])[:, :, None] * row[:, None, :], axis=0)
    data = block[: coef_dev * rows].reshape(coef_dev, -1)
    found = jnp.dot(matrix, data, precision=lax.Precision.HIGHEST)
    found = found.reshape(targets * rows, -1)
    if mode_slot is None:
        return found
    modes = [jnp.where(mode_owner[k] == device, mode_slot, 0.0) for k in range(M)]
    return jnp.concatenate([found, *modes], axis=0)


def unrolled(count):
    return count % 2 == 0 and 6 <= count <= 16


def ring_order(count):
    return list(range(0, count, 2)) + list(range(count - 1, 0, -2))


def ring_steps(count):
    half = count // 2
    return [
        (half, half - 1) if j == 0 else (half - 1, half) for j in range(CHUNKS)
    ]


def sum_parts(count, chunk):
    half = count // 2
    middle = list(range(2, half - 1))
    if chunk == 0:
        return {"a": [0, 1], "b": middle + [half - 1]}
    return {"a": [0, 1], "b": middle, "c": [half - 1, half]}


def chaos_sums(chunks, coef_dev, capacity, rows_of, slot_rows, mode_owner):
    count = lax.axis_size("chaos")
    me = lax.axis_index("chaos")
    fixed = (me, mode_owner, coef_dev, capacity)
    if not unrolled(count):
        ring = [(i, (i + 1) % count) for i in range(count)]

        def at_step(step, blocks):
            device = (me - step) % count
            slot_at = coef_dev * rows_of[0]
            table, slot = blocks[0][-TABLE_ROWS:], blocks[0][slot_at : slot_at + slot_rows]
            return [
                plain_sums(b, table, slot if j == 0 else None, device, *fixed, rows_of[j])
                for j, b in enumerate(blocks)
            ]

        def body(step, carry):
            blocks, sums = carry
            blocks = [lax.ppermute(b, "chaos", ring) for b in blocks]
            return blocks, jax.tree.map(jnp.add, sums, at_step(step, blocks))

        found = lax.fori_loop(1, count, body, (list(chunks), at_step(0, chunks)))[1]
        return found, None, jnp.int32(-1)

    order = ring_order(count)
    there = [(order[i], order[(i + 1) % count]) for i in range(count)]
    back = [(b, a) for a, b in there]
    half = count // 2
    place = jnp.where(me % 2 == 0, me // 2, count - 1 - me // 2)

    def device_at(shift):
        q = (place + shift) % count
        return jnp.where(q < half, 2 * q, 2 * (count - 1 - q) + 1)

    found, opposite = [], None
    for j, (chunk, steps) in enumerate(zip(chunks, ring_steps(count))):
        blocks = {0: (chunk, False)}
        for pairs, sign, n_steps in ((there, -1, steps[0]), (back, 1, steps[1])):
            block = chunk
            for step in range(1, n_steps + 1):
                if step == n_steps:
                    block = pick(block, device_at(-sign), coef_dev, capacity, rows_of[j])
                block = lax.ppermute(block, "chaos", pairs)
                blocks[sign * step % count] = (block, step == n_steps)
        sums = None
        for distances in sum_parts(count, j).values():
            shifts = sorted({s * d % count for d in distances for s in (1, -1)})
            sums = sum_blocks(
                [blocks[s][0] for s in shifts],
                [blocks[s][1] for s in shifts],
                [device_at(s) for s in shifts],
                *fixed,
                rows_of[j],
                slot_rows if j == 0 else 0,
                sums,
            )
        found.append(sums)
        if j == 0:
            opposite = blocks[half][0]
    return found, opposite, device_at(half)


def depth_pair(values):
    count = lax.axis_size("space")
    first = [(i, i ^ 1) for i in range(count) if i ^ 1 < count]
    second = [
        (i, j)
        for i in range(count)
        for j in [i - 1 if i % 2 == 0 else i + 1]
        if 0 <= j < count
    ]
    other = lax.ppermute(values, "space", second)
    pair = lax.ppermute(values, "space", first)
    return other, pair


def base_kernel(coef_dev, depth, n_space, space_ref, coeffs, source, mean, *refs):
    other, pair, known, face, coef_ext, mean_ext = refs
    index = space_ref[0]
    even = lax.rem(index, 2) == 0
    pair_at = jnp.where(even, 2 * depth, 0)
    other_at = jnp.where(even, 0, 2 * depth)
    total_layers = 3 * depth
    planes = coef_dev * depth

    for at, part in ((pair_at, pair), (other_at, other)):
        for c in range(coef_dev):
            coef_ext[c, pl.ds(at, depth)] = part[c * depth : (c + 1) * depth]
        mean_ext[pl.ds(at, depth)] = part[2 * planes : 2 * planes + depth]
    for c in range(coef_dev):
        coef_ext[c, depth : 2 * depth] = coeffs[c]
    mean_ext[depth : 2 * depth] = mean[...]

    def layer(l, source_of):
        xm, xp, ym, yp, down, up, total = faces(mean_ext[l - 1], mean_ext[l], mean_ext[l + 1])
        diagonal = REACTION + total
        absolute = index * depth + l - depth
        inside = (absolute >= 0) & (absolute < n_space * depth)
        face[0, l], face[1, l], face[2, l], face[3, l] = xm, xp, ym, yp
        face[4, l], face[5, l] = down, up
        face[6, l] = jnp.where(inside, 1.0 / diagonal, 0.0)

        def coefficient(c, carry):
            v = coef_ext[c, l]
            spread = lateral(xm * v, xp * v, ym * v, yp * v)
            spread = spread + down * coef_ext[c, l - 1] + up * coef_ext[c, l + 1]
            known[c, l] = source_of(c) - (diagonal * v - spread)
            return carry

        for c in range(coef_dev):
            coefficient(c, 0)

    def from_part(part, at):
        def body(l, carry):
            layer(l, lambda c: part[planes + c * depth + l - at])
            return carry

        lax.fori_loop(jnp.maximum(at, 1), jnp.minimum(at + depth, total_layers - 1), body, 0)

    from_part(pair, pair_at)
    from_part(other, other_at)

    def body(l, carry):
        layer(l, lambda c: source[c, l - depth])
        return carry

    lax.fori_loop(depth, 2 * depth, body, 0)


def sweep_constants():
    midpoint = (BOUND_HIGH + BOUND_LOW) / 2.0
    halfwidth = (BOUND_HIGH - BOUND_LOW) / 2.0
    ratio = midpoint / halfwidth
    now = 1.0 / ratio
    steps = []
    for _ in range(ITERS - 1):
        following = 1.0 / (2.0 * ratio - now)
        steps.append((following * now, 2.0 * following / halfwidth))
        now = following
    return midpoint, steps


def order_parts(trio, even, n, layers, summed, nx):
    slabs = (1, jnp.where(even, 0, 2), jnp.where(even, 2, 0))
    for part, slab in zip(trio, slabs):
        for t in range(n):
            at = t * layers * nx
            summed[slab, t] = part[at : at + layers * nx].reshape(layers, nx, -1)
    return slabs


def add_picked(trio, slabs, begin, capacity, targets, layers, summed, table, nx):
    rows = layers * nx
    for e in range(capacity):
        target = lax.rem(table[0, begin + e].astype(jnp.int32), targets)
        w = table[1, begin + e]
        for part, slab in zip(trio, slabs):
            src = part[e * rows : (e + 1) * rows].reshape(layers, nx, -1)
            summed[slab, target] = summed[slab, target] + w * src


def coupled(l, depth, start, layers, coef_dev, summed, mode_face, visit):
    slab, at = divmod(l, depth)
    near = {}
    for offset in (-1, 0, 1):
        s, i = divmod(l + offset, depth)
        if 0 <= s < 3 and start <= i < start + layers:
            near[offset] = (s, i - start)
    if not near:
        return False
    for c in range(coef_dev):
        to, rest = [None] * 4, None

        def add(total, term):
            return term if total is None else total + term

        for k in range(M):
            if 0 in near:
                s, i = near[0]
                v = summed[s, c * M + k, i]
                for q in range(4):
                    to[q] = add(to[q], mode_face[k, q, l] * v)
                rest = add(rest, -(mode_face[k, 6, l] * v))
            for offset, which in ((-1, 4), (1, 5)):
                if offset in near:
                    s, i = near[offset]
                    rest = add(rest, mode_face[k, which, l] * summed[s, c * M + k, i])
        visit(c, rest + lateral(*to) if 0 in near else rest)
    return True


def begin_kernel(coef_dev, depth, layers, capacity, n_picked, where, known, own, other, pair, *refs):
    picked = refs[:n_picked]
    rest, mode_face, summed, mode_ext, tables, sems = refs[n_picked:]
    nx = known.shape[2]
    targets = coef_dev * M
    copies = start_tables(picked[:1], tables, sems)
    even = lax.rem(where[0], 2) == 0
    slabs = order_parts((own, other, pair), even, targets, layers, summed, nx)
    for part, slab in zip((own, other, pair), slabs):
        for k in range(M):
            at = (targets * layers + k * depth) * nx
            mode_ext[k, pl.ds(slab * depth, depth)] = part[at : at + depth * nx].reshape(
                depth, nx, -1
            )
    if picked:
        at = capacity * layers * nx
        for k in range(M):

            @pl.when(where[2 + k] == where[2 + M])
            def _(k=k):
                for part, slab in zip(picked, slabs):
                    mode_ext[k, pl.ds(slab * depth, depth)] = part[at : at + depth * nx].reshape(
                        depth, nx, -1
                    )

        copies[0].wait()
        begin = where[1] * capacity
        add_picked(picked, slabs, begin, capacity, targets, layers, summed, tables.at[0], nx)
    last = 3 * depth - 1

    def mode_faces(l, carry):
        for k in range(M):
            got = faces(mode_ext[k, l - 1], mode_ext[k, l], mode_ext[k, l + 1])
            for i, value in enumerate(got):
                mode_face[k, i, l] = value
        return carry

    lax.fori_loop(1, last, mode_faces, 0)
    for l in range(1, last):

        def visit(c, value, l=l):
            rest[c, l] = known[c, l] + value

        if not coupled(l, depth, 0, layers, coef_dev, summed, mode_face, visit):
            for c in range(coef_dev):
                rest[c, l] = known[c, l]


def sweep_kernel(coef_dev, depth, start, layers, space_ref, rest, mode_face, face, *refs):
    own, other, pair, residual, correction, summed, scaled, first, second = refs
    nx = rest.shape[2]
    even = lax.rem(space_ref[0], 2) == 0
    order_parts((own, other, pair), even, coef_dev * M, layers, summed, nx)
    last = 3 * depth - 1
    midpoint, steps = sweep_constants()
    for l in range(1, last):

        def visit(c, value, l=l):
            total = rest[c, l] if value is None else rest[c, l] + value
            w = total * face[6, l]
            d = w * (1.0 / midpoint)
            scaled[c, l] = w
            first[c, l] = d
            if depth <= l < 2 * depth:
                residual[c, l - depth] = total
                correction[c, l - depth] = d

        if not coupled(l, depth, start, layers, coef_dev, summed, mode_face, visit):
            for c in range(coef_dev):
                visit(c, None)

    now, later = first, second
    for number, (keep, gain) in enumerate(steps):

        def swept(l, own, now=now, later=later, keep=keep, gain=gain, number=number):
            for c in range(coef_dev):
                v = now[c, l]
                spread = lateral(face[0, l] * v, face[1, l] * v, face[2, l] * v, face[3, l] * v)
                spread = spread + face[4, l] * now[c, l - 1] + face[5, l] * now[c, l + 1]
                w = scaled[c, l] - v + face[6, l] * spread
                d = keep * v + gain * w
                if number + 1 < len(steps):
                    scaled[c, l] = w
                    later[c, l] = d
                if own:
                    correction[c, l - depth] = correction[c, l - depth] + d

        over_layers(swept, depth, len(steps) - 1 - number)
        now, later = later, now


def over_layers(visit, depth, halo):
    def own(l, carry):
        visit(l, True)
        return carry

    def outside(i, carry):
        visit(jnp.where(i < halo, depth - halo + i, 2 * depth - halo + i), False)
        return carry

    lax.fori_loop(depth, 2 * depth, own, 0)
    if halo:
        lax.fori_loop(0, 2 * halo, outside, 0)


def residual_and_correction(coeffs, source, mean_field, mode_bank, mode_owner, links):
    coef_dev, depth, nx, ny = coeffs.shape
    n_space = lax.axis_size("space")
    slot_rows = depth * nx
    per_chunk = depth // CHUNKS
    layer_counts = [per_chunk] * CHUNKS
    index = lax.axis_index("space").astype(jnp.int32).reshape(1)

    rows_of = [layers * nx for layers in layer_counts]
    count = lax.axis_size("chaos")
    shifts = count // 2 - 1
    capacity = max(2, (M * coef_dev - 1 + shifts - 1) // shifts)
    assert count * capacity <= ny
    chunks = pack(coeffs, mode_bank, links[0], capacity, rows_of)

    sums, opposite, opposite_device = chaos_sums(
        chunks, coef_dev, capacity, rows_of, slot_rows, mode_owner
    )

    early = jnp.concatenate(
        [coeffs.reshape(-1, nx, ny), source.reshape(-1, nx, ny), mean_field], axis=0
    )
    other, pair = depth_pair(early)
    wide = (coef_dev, 3 * depth, nx, ny)
    known, face = pl.pallas_call(
        functools.partial(base_kernel, coef_dev, depth, n_space),
        out_shape=(
            jax.ShapeDtypeStruct(wide, jnp.float32),
            jax.ShapeDtypeStruct((7, 3 * depth, nx, ny), jnp.float32),
        ),
        in_specs=[SMEM] + [VMEM] * 5,
        out_specs=(VMEM, VMEM),
        scratch_shapes=[
            pltpu.VMEM(wide, jnp.float32),
            pltpu.VMEM((3 * depth, nx, ny), jnp.float32),
        ],
        cost_estimate=cost(3 * depth * coef_dev, nx, ny, 20),
        compiler_params=pltpu.CompilerParams(vmem_limit_bytes=16 << 20),
        name="base",
    )(index, coeffs, source, mean_field, other, pair)

    parts = [[own, *depth_pair(own)] for own in sums]
    picked = [] if opposite is None else [opposite, *depth_pair(opposite)]
    where = jnp.stack(
        [index[0], lax.axis_index("chaos"), *(mode_owner[k] for k in range(M)), opposite_device]
    ).astype(jnp.int32)
    layers = layer_counts[0]
    ordered = pltpu.VMEM((3, coef_dev * M, layers, nx, ny), jnp.float32)
    mode_faces = (M, 7, 3 * depth, nx, ny)
    rest, mode_face = pl.pallas_call(
        functools.partial(begin_kernel, coef_dev, depth, layers, capacity, len(picked)),
        out_shape=(
            jax.ShapeDtypeStruct(wide, jnp.float32),
            jax.ShapeDtypeStruct(mode_faces, jnp.float32),
        ),
        in_specs=[SMEM] + [VMEM] * (4 + len(picked)),
        out_specs=(VMEM, VMEM),
        scratch_shapes=[
            ordered,
            pltpu.VMEM((M, 3 * depth, nx, ny), jnp.float32),
            *table_scratch(1, ny),
        ],
        compiler_params=pltpu.CompilerParams(vmem_limit_bytes=16 << 20),
        cost_estimate=cost(3 * depth * coef_dev, nx, ny, 40),
        name="begin",
    )(where, known, *parts[0], *picked)
    out = jax.ShapeDtypeStruct(coeffs.shape, jnp.float32)
    return pl.pallas_call(
        functools.partial(sweep_kernel, coef_dev, depth, depth - layers, layers),
        out_shape=(out, out),
        in_specs=[SMEM] + [VMEM] * 6,
        out_specs=(VMEM, VMEM),
        scratch_shapes=[ordered] + [pltpu.VMEM(wide, jnp.float32)] * 3,
        compiler_params=pltpu.CompilerParams(vmem_limit_bytes=20 << 20),
        cost_estimate=cost(6 * depth * coef_dev, nx, ny, 40),
        name="sweeps",
    )(index, rest, mode_face, face, *parts[1])


def solution(mesh):
    in_specs = (
        P("chaos", "space", None, None),
        P("chaos", "space", None, None),
        P("space", None, None),
        P("chaos", "space", None, None),
        P(),
        P("chaos", None, None),
    )
    out_specs = (P("chaos", "space", None, None), P("chaos", "space", None, None))
    step = jax.shard_map(
        residual_and_correction, mesh=mesh, in_specs=in_specs, out_specs=out_specs, check_vma=False
    )
    if not unrolled(mesh.shape["chaos"]):
        return step
    return step
```

```python
import functools

import jax
import jax.numpy as jnp
from jax import lax
from jax.experimental import pallas as pl
from jax.experimental.pallas import tpu as pltpu
from jax.sharding import PartitionSpec as P


M = 2
ITERS = 4

REACTION = 0.5
BOUND_LOW = 0.04
BOUND_HIGH = 2.0

CHUNKS = 2
TABLE_ROWS = 8


VMEM = pl.BlockSpec(memory_space=pltpu.VMEM)
SMEM = pl.BlockSpec(memory_space=pltpu.SMEM)


def cost(planes, nx, ny, flops):
    return pl.CostEstimate(
        flops=flops * planes * nx * ny, bytes_accessed=8 * planes * nx * ny, transcendentals=0
    )


def shifted(values, axis, step):
    return pltpu.roll(values, step % values.shape[axis], axis)


def faces(below, own, above):
    nx, ny = own.shape
    ix = lax.broadcasted_iota(jnp.int32, (nx, ny), 0)
    iy = lax.broadcasted_iota(jnp.int32, (nx, ny), 1)
    half = 0.5 * own
    zero = jnp.zeros_like(own)
    xm = jnp.where(ix == 0, zero, half + shifted(half, 0, 1))
    xp = jnp.where(ix == nx - 1, zero, half + shifted(half, 0, -1))
    ym = jnp.where(iy == 0, zero, half + shifted(half, 1, 1))
    yp = jnp.where(iy == ny - 1, zero, half + shifted(half, 1, -1))
    up = half + 0.5 * above
    down = half + 0.5 * below
    total = up + down
    total = total + jnp.where(ix == 0, half, xm) + jnp.where(ix == nx - 1, half, xp)
    total = total + jnp.where(iy == 0, half, ym) + jnp.where(iy == ny - 1, half, yp)
    return xm, xp, ym, yp, down, up, total


def lateral(to_xm, to_xp, to_ym, to_yp):
    return (
        shifted(to_xm, 0, -1)
        + shifted(to_xp, 0, 1)
        + shifted(to_ym, 1, -1)
        + shifted(to_yp, 1, 1)
    )


def pack_kernel(coef_dev, capacity, rows_of, slot_rows, links, coeffs, bank, *refs):
    blocks, (sems,) = refs[: len(rows_of)], refs[len(rows_of) :]
    slot = blocks[0].at[pl.ds(coef_dev * rows_of[0], slot_rows)]
    copies = [pltpu.make_async_copy(bank.at[0], slot, sems.at[len(rows_of) * coef_dev])]
    start = 0
    for j, (block, rows) in enumerate(zip(blocks, rows_of)):
        for c in range(coef_dev):
            copies.append(
                pltpu.make_async_copy(
                    coeffs.at[c, pl.ds(start, rows)],
                    block.at[pl.ds(c * rows, rows)],
                    sems.at[j * coef_dev + c],
                )
            )
        start += rows
    for copy in copies:
        copy.start()
    entries, lanes = links.shape[1], blocks[0].shape[1]
    listed = links[...].astype(jnp.float32)
    s, p, k, level = (listed[i : i + 1] for i in range(4))
    device = jnp.floor((p + 0.5) * (1.0 / coef_dev))
    code = (s * coef_dev + p - device * coef_dev) * M + k
    square = (entries, entries)
    row = lax.broadcasted_iota(jnp.int32, square, 0)
    column = lax.broadcasted_iota(jnp.int32, square, 1)

    def upright(values):
        return jnp.sum(jnp.where(row == column, values, 0.0), axis=1, keepdims=True)

    device_up, level_up = upright(device), upright(level)
    earlier = (device == device_up) & (level > 0.0) & (column < row)
    rank = jnp.sum(jnp.where(earlier, 1.0, 0.0), axis=1, keepdims=True)
    place = jnp.where(level_up > 0.0, device_up * capacity + rank, -1.0)
    lane = lax.broadcasted_iota(jnp.int32, (entries, lanes), 1).astype(jnp.float32)
    table = [
        jnp.sum(jnp.where(place == lane, values, 0.0), axis=0, keepdims=True)
        for values in (upright(code), jnp.sqrt(level_up))
    ]
    table.append(jnp.zeros((TABLE_ROWS - len(table), lanes), jnp.float32))
    table = jnp.concatenate(table, axis=0)
    for block in blocks:
        block[pl.ds(block.shape[0] - TABLE_ROWS, TABLE_ROWS), :] = table
    for copy in copies:
        copy.wait()


def pack(coeffs, bank, links, capacity, rows_of):
    coef_dev, lanes = coeffs.shape[0], coeffs.shape[3]
    whole_rows = coeffs.reshape(coef_dev, -1, lanes)
    slot = bank.reshape(1, -1, lanes)
    slot_rows = slot.shape[1]
    hbm = pl.BlockSpec(memory_space=pltpu.HBM)
    sizes = [
        coef_dev * rows + (slot_rows if j == 0 else 0) + TABLE_ROWS
        for j, rows in enumerate(rows_of)
    ]
    return pl.pallas_call(
        functools.partial(pack_kernel, coef_dev, capacity, rows_of, slot_rows),
        out_shape=[jax.ShapeDtypeStruct((size, lanes), jnp.float32) for size in sizes],
        in_specs=[VMEM, hbm, hbm],
        out_specs=[VMEM] * len(sizes),
        scratch_shapes=[pltpu.SemaphoreType.DMA((len(sizes) * coef_dev + 1,))],
        cost_estimate=cost(coef_dev, sum(rows_of), lanes, 1),
        name="pack",
    )(links.T, whole_rows, slot)


def start_tables(blocks, tables, sems):
    copies = []
    for i, block in enumerate(blocks):
        at = pl.ds(block.shape[0] - TABLE_ROWS, TABLE_ROWS)
        copies.append(pltpu.make_async_copy(block.at[at], tables.at[i], sems.at[i]))
        copies[-1].start()
    return copies


def table_scratch(n, lanes):
    return [pltpu.SMEM((n, TABLE_ROWS, lanes), jnp.float32), pltpu.SemaphoreType.DMA((n,))]


def pick_kernel(coef_dev, capacity, rows, begin, block, out, tables, sems):
    (copy,) = start_tables([block], tables, sems)
    out[capacity * rows :, :] = block[coef_dev * rows :, :]
    copy.wait()
    for e in range(capacity):
        row = lax.div(tables[0, 0, begin[0] + e].astype(jnp.int32), coef_dev * M)
        out[e * rows : (e + 1) * rows, :] = block[
            pl.ds(pl.multiple_of(row * rows, rows), rows), :
        ]


def pick(block, device, coef_dev, capacity, rows):
    size, lanes = block.shape
    return pl.pallas_call(
        functools.partial(pick_kernel, coef_dev, capacity, rows),
        out_shape=jax.ShapeDtypeStruct((size - (coef_dev - capacity) * rows, lanes), jnp.float32),
        in_specs=[SMEM, VMEM],
        out_specs=VMEM,
        scratch_shapes=table_scratch(1, lanes),
        compiler_params=pltpu.CompilerParams(vmem_limit_bytes=2 << 20),
        cost_estimate=cost(capacity, rows, lanes, 1),
        name="pick",
    )((device * capacity).astype(jnp.int32).reshape(1), block)


def sum_kernel(picked, coef_dev, capacity, rows, slot_rows, more, where, *refs):
    refs = list(refs)
    blocks = [refs.pop(0) for _ in picked]
    so_far = refs.pop(0) if more else None
    out, tables, sems = refs
    targets = coef_dev * M
    copies = start_tables(blocks, tables, sems)
    out[...] = so_far[...] if more else jnp.zeros_like(out)
    if slot_rows:
        for i, (block, few) in enumerate(zip(blocks, picked)):
            for k in range(M):

                @pl.when(where[1 + k] == where[1 + M + i])
                def _(block=block, k=k, few=few):
                    at = pl.ds(targets * rows + k * slot_rows, slot_rows)
                    out[at, :] = block[pl.ds((capacity if few else coef_dev) * rows, slot_rows), :]

    begin = where[0] * capacity
    for i, (block, few) in enumerate(zip(blocks, picked)):
        copies[i].wait()
        for e in range(capacity):
            code, w = tables[i, 0, begin + e].astype(jnp.int32), tables[i, 1, begin + e]
            row, target = e if few else lax.div(code, targets), lax.rem(code, targets)
            at = pl.ds(pl.multiple_of(target * rows, rows), rows)
            src = block[pl.ds(pl.multiple_of(row * rows, rows), rows), :]
            out[at, :] = out[at, :] + w * src


def sum_blocks(
    blocks, picked, devices, me, mode_owner, coef_dev, capacity, rows, slot_rows, so_far
):
    n, lanes = len(blocks), blocks[0].shape[1]
    size = coef_dev * M * rows + M * slot_rows
    where = jnp.stack([me] + [mode_owner[k] for k in range(M)] + devices).astype(jnp.int32)
    more = so_far is not None
    return pl.pallas_call(
        functools.partial(sum_kernel, picked, coef_dev, capacity, rows, slot_rows, more),
        out_shape=jax.ShapeDtypeStruct((size, lanes), jnp.float32),
        in_specs=[SMEM] + [VMEM] * (n + more),
        out_specs=VMEM,
        scratch_shapes=table_scratch(n, lanes),
        compiler_params=pltpu.CompilerParams(vmem_limit_bytes=5 << 20),
        cost_estimate=cost(coef_dev * M, rows, lanes, 4),
    )(where, *blocks, *([so_far] if more else []))


def plain_sums(block, table, mode_slot, device, me, mode_owner, coef_dev, capacity, rows):
    targets = coef_dev * M
    code = lax.dynamic_slice(table[0], (me * capacity,), (capacity,)).astype(jnp.int32)
    w = lax.dynamic_slice(table[1], (me * capacity,), (capacity,))
    row = (code[:, None] // targets == jnp.arange(coef_dev)[None, :]).astype(jnp.float32)
    target = (code[:, None] % targets == jnp.arange(targets)[None, :]).astype(jnp.float32)
    matrix = jnp.sum((target * w[:, None])[:, :, None] * row[:, None, :], axis=0)
    data = block[: coef_dev * rows].reshape(coef_dev, -1)
    found = jnp.dot(matrix, data, precision=lax.Precision.HIGHEST)
    found = found.reshape(targets * rows, -1)
    if mode_slot is None:
        return found
    modes = [jnp.where(mode_owner[k] == device, mode_slot, 0.0) for k in range(M)]
    return jnp.concatenate([found, *modes], axis=0)


def unrolled(count):
    return count % 2 == 0 and 6 <= count <= 16


def ring_order(count):
    return list(range(0, count, 2)) + list(range(count - 1, 0, -2))


def ring_steps(count):
    half = count // 2
    return [
        (half, half - 1) if j == 0 else (half - 1, half) for j in range(CHUNKS)
    ]


def sum_parts(count, chunk):
    half = count // 2
    middle, last = list(range(2, half - 1)), [half - 1, half]
    if chunk == 0:
        return {"a": [0, 1], "c": middle + last}
    return {"a": [0, 1], "b": middle, "c": last}


def chaos_sums(chunks, coef_dev, capacity, rows_of, slot_rows, mode_owner):
    count = lax.axis_size("chaos")
    me = lax.axis_index("chaos")
    fixed = (me, mode_owner, coef_dev, capacity)
    if not unrolled(count):
        ring = [(i, (i + 1) % count) for i in range(count)]

        def at_step(step, blocks):
            device = (me - step) % count
            slot_at = coef_dev * rows_of[0]
            table, slot = blocks[0][-TABLE_ROWS:], blocks[0][slot_at : slot_at + slot_rows]
            return [
                plain_sums(b, table, slot if j == 0 else None, device, *fixed, rows_of[j])
                for j, b in enumerate(blocks)
            ]

        def body(step, carry):
            blocks, sums = carry
            blocks = [lax.ppermute(b, "chaos", ring) for b in blocks]
            return blocks, jax.tree.map(jnp.add, sums, at_step(step, blocks))

        return lax.fori_loop(1, count, body, (list(chunks), at_step(0, chunks)))[1]

    order = ring_order(count)
    there = [(order[i], order[(i + 1) % count]) for i in range(count)]
    back = [(b, a) for a, b in there]
    half = count // 2
    place = jnp.where(me % 2 == 0, me // 2, count - 1 - me // 2)

    def device_at(shift):
        q = (place + shift) % count
        return jnp.where(q < half, 2 * q, 2 * (count - 1 - q) + 1)

    found = []
    for j, (chunk, steps) in enumerate(zip(chunks, ring_steps(count))):
        blocks = {0: (chunk, False)}
        for pairs, sign, n_steps in ((there, -1, steps[0]), (back, 1, steps[1])):
            block = chunk
            for step in range(1, n_steps + 1):
                if step == n_steps:
                    block = pick(block, device_at(-sign), coef_dev, capacity, rows_of[j])
                block = lax.ppermute(block, "chaos", pairs)
                blocks[sign * step % count] = (block, step == n_steps)
        sums = None
        for distances in sum_parts(count, j).values():
            shifts = sorted({s * d % count for d in distances for s in (1, -1)})
            sums = sum_blocks(
                [blocks[s][0] for s in shifts],
                [blocks[s][1] for s in shifts],
                [device_at(s) for s in shifts],
                *fixed,
                rows_of[j],
                slot_rows if j == 0 else 0,
                sums,
            )
        found.append(sums)
    return found


def depth_pair(to_other, to_pair):
    count = lax.axis_size("space")
    first = [(i, i ^ 1) for i in range(count) if i ^ 1 < count]
    second = [
        (i, j)
        for i in range(count)
        for j in [i - 1 if i % 2 == 0 else i + 1]
        if 0 <= j < count
    ]
    other = lax.ppermute(to_other, "space", second)
    pair = lax.ppermute(to_pair, "space", first)
    return other, pair


def base_kernel(coef_dev, depth, n_space, space_ref, coeffs, source, mean, *refs):
    other, pair, known, face, coef_ext, mean_ext = refs
    index = space_ref[0]
    even = lax.rem(index, 2) == 0
    for part, below in ((pair, jnp.logical_not(even)), (other, even)):
        at = jnp.where(below, 0, 2 * depth)
        edge = jnp.where(below, 1, 0)
        for c in range(coef_dev):
            coef_ext[c, jnp.where(below, 0, depth + 1)] = part[2 * c + edge]
        mean_ext[pl.ds(at, depth)] = part[2 * coef_dev : 2 * coef_dev + depth]
    for c in range(coef_dev):
        coef_ext[c, 1 : depth + 1] = coeffs[c]
    mean_ext[depth : 2 * depth] = mean[...]

    def layer(l, own):
        xm, xp, ym, yp, down, up, total = faces(mean_ext[l - 1], mean_ext[l], mean_ext[l + 1])
        diagonal = REACTION + total
        absolute = index * depth + l - depth
        inside = (absolute >= 0) & (absolute < n_space * depth)
        inverse = jnp.where(inside, 1.0 / diagonal, 0.0)
        for i, value in enumerate((xm, xp, ym, yp, down, up)):
            face[i, l] = value * inverse
        face[6, l] = inverse
        if own:
            at = l - depth
            for c in range(coef_dev):
                v = coef_ext[c, at + 1]
                spread = lateral(xm * v, xp * v, ym * v, yp * v)
                spread = spread + down * coef_ext[c, at] + up * coef_ext[c, at + 2]
                known[c, at] = source[c, at] - (diagonal * v - spread)

    over_layers(layer, depth, ITERS - 1)


def sweep_constants():
    midpoint = (BOUND_HIGH + BOUND_LOW) / 2.0
    halfwidth = (BOUND_HIGH - BOUND_LOW) / 2.0
    ratio = midpoint / halfwidth
    now = 1.0 / ratio
    steps = []
    for _ in range(ITERS - 1):
        following = 1.0 / (2.0 * ratio - now)
        steps.append((following * now, 2.0 * following / halfwidth))
        now = following
    return midpoint, steps


def plane(sums, layers, nx, target, l):
    at = (target * layers + l % layers) * nx
    return sums[l // layers][at : at + nx, :]


def mode_plane(sums, layers, depth, nx, targets, k, l):
    at = (targets * layers + k * depth + l) * nx
    return sums[0][at : at + nx, :]


def coupled(l, inside, coef_dev, read, mode_face, visit):
    for c in range(coef_dev):
        to, rest = [None] * 4, None

        def add(total, term):
            return term if total is None else total + term

        for k in range(M):
            target = c * M + k
            if l in inside:
                v = read(target, l)
                for q in range(4):
                    to[q] = add(to[q], mode_face[k, q, l] * v)
                rest = add(rest, mode_face[k, 6, l] * v)
            for near, which in ((l - 1, 4), (l + 1, 5)):
                if near in inside:
                    rest = add(rest, mode_face[k, which, l] * read(target, near))
        if rest is not None:
            visit(c, rest + lateral(*to) if l in inside else rest)


def begin_kernel(coef_dev, depth, layers, sums, rest, mode_face):
    nx = rest.shape[2]
    targets = coef_dev * M
    for k in range(M):
        own = [mode_plane([sums], layers, depth, nx, targets, k, l) for l in range(depth)]
        for l in range(depth):
            below = own[l - 1] if l > 0 else -own[l]
            above = own[l + 1] if l + 1 < depth else -own[l]
            *got, total = faces(below, own[l], above)
            for i, value in enumerate((*got, -total)):
                mode_face[k, i, l] = value
    for l in range(depth):
        if l > layers:
            for c in range(coef_dev):
                rest[c, l] = jnp.zeros_like(rest[c, l])

        def visit(c, value, l=l):
            rest[c, l] = value

        coupled(
            l, range(layers), coef_dev,
            lambda target, at: plane([sums], layers, nx, target, at), mode_face, visit,
        )


def couple_kernel(coef_dev, depth, layers, space_ref, known, part, mode_face, *refs):
    sums, (rest, to_other, to_pair) = refs[: depth // layers], refs[depth // layers :]
    nx = part.shape[2]
    targets = coef_dev * M
    halo = ITERS - 1

    def read(target, l):
        return plane(sums, layers, nx, target, l)

    for l in range(depth):

        def visit(c, value, l=l):
            rest[c, l] = known[c, l] + part[c, l] + value

        late = range(layers, depth)
        if not {l - 1, l, l + 1} & set(late):
            for c in range(coef_dev):
                rest[c, l] = known[c, l] + part[c, l]
        coupled(l, late, coef_dev, read, mode_face, visit)

    even = lax.rem(space_ref[0], 2) == 0

    def fill(message, first, edge):
        for c in range(coef_dev):
            message[c * halo : (c + 1) * halo] = rest[c, first : first + halo]
        for t in range(targets):
            message[coef_dev * halo + t] = read(t, edge)
        for k in range(M):
            message[coef_dev * halo + targets + k] = mode_plane(
                sums, layers, depth, nx, targets, k, edge
            )

    @pl.when(even)
    def _():
        fill(to_pair, depth - halo, depth - 1)
        fill(to_other, 0, 0)

    @pl.when(jnp.logical_not(even))
    def _():
        fill(to_pair, 0, 0)
        fill(to_other, depth - halo, depth - 1)


def sweep_kernel(coef_dev, depth, layers, space_ref, rest, face, other, pair, *refs):
    sums = refs[: depth // layers]
    residual, correction, edges, scaled, first, second = refs[depth // layers :]
    nx = rest.shape[2]
    targets = coef_dev * M
    halo = ITERS - 1
    even = lax.rem(space_ref[0], 2) == 0

    def rows(c, l):
        return pl.ds(pl.multiple_of((c * 3 * depth + l) * nx, nx), nx)

    for part, below in ((pair, jnp.logical_not(even)), (other, even)):
        at = jnp.where(below, depth - halo, 2 * depth)
        for c in range(coef_dev):
            for i in range(halo):
                scaled[rows(c, at + i), :] = part[c * halo + i]
        edges[jnp.where(below, 0, 1)] = part[coef_dev * halo :]
    half_modes = [
        [
            0.5 * (mode_plane(sums, layers, depth, nx, targets, k, l) + edges[side, targets + k])
            for k in range(M)
        ]
        for side, l in ((0, 0), (1, depth - 1))
    ]
    for c in range(coef_dev):
        for l in range(depth):
            total = rest[c, l]
            for side, edge, beyond in ((0, 0, depth - 1), (1, depth - 1, 2 * depth)):
                if l != edge:
                    continue
                flux = None
                for k in range(M):
                    target = c * M + k
                    drop = plane(sums, layers, nx, target, l) - edges[side, target]
                    term = half_modes[side][k] * drop
                    flux = term if flux is None else flux + term
                total = total - flux
                scaled[rows(c, beyond), :] = scaled[rows(c, beyond), :] + flux
            residual[c, l] = total
            scaled[rows(c, depth + l), :] = total

    midpoint, steps = sweep_constants()

    def start(l, own):
        for c in range(coef_dev):
            w = scaled[rows(c, l), :] * face[6, l]
            d = w * (1.0 / midpoint)
            scaled[rows(c, l), :] = w
            first[rows(c, l), :] = d
            if own:
                correction[c, l - depth] = d

    over_layers(start, depth, halo)

    now, later = first, second
    for number, (keep, gain) in enumerate(steps):

        def swept(l, own, now=now, later=later, keep=keep, gain=gain, number=number):
            for c in range(coef_dev):
                at = pl.multiple_of((c * 3 * depth + l) * nx, nx)
                here = pl.ds(at, nx)
                v = now[here, :]
                w = scaled[here, :] - v
                w = w + face[0, l] * now[pl.ds(at - 1, nx), :]
                w = w + face[1, l] * now[pl.ds(at + 1, nx), :]
                w = w + face[2, l] * shifted(v, 1, 1) + face[3, l] * shifted(v, 1, -1)
                w = w + face[4, l] * now[pl.ds(at - nx, nx), :]
                w = w + face[5, l] * now[pl.ds(at + nx, nx), :]
                d = keep * v + gain * w
                if number + 1 < len(steps):
                    scaled[here, :] = w
                    later[here, :] = d
                if own:
                    correction[c, l - depth] = correction[c, l - depth] + d

        over_layers(swept, depth, len(steps) - 1 - number)
        now, later = later, now


def over_layers(visit, depth, halo):
    def own(l, carry):
        visit(l, True)
        return carry

    def outside(i, carry):
        visit(jnp.where(i < halo, depth - halo + i, 2 * depth - halo + i), False)
        return carry

    lax.fori_loop(depth, 2 * depth, own, 0)
    if halo:
        lax.fori_loop(0, 2 * halo, outside, 0)


def residual_and_correction(coeffs, source, mean_field, mode_bank, mode_owner, links):
    coef_dev, depth, nx, ny = coeffs.shape
    n_space = lax.axis_size("space")
    slot_rows = depth * nx
    per_chunk = depth // CHUNKS
    layer_counts = [per_chunk] * CHUNKS
    index = lax.axis_index("space").astype(jnp.int32).reshape(1)

    rows_of = [layers * nx for layers in layer_counts]
    count = lax.axis_size("chaos")
    shifts = count // 2 - 1
    capacity = max(2, (M * coef_dev - 1 + shifts - 1) // shifts)
    assert count * capacity <= ny
    chunks = pack(coeffs, mode_bank, links[0], capacity, rows_of)

    sums = chaos_sums(
        chunks, coef_dev, capacity, rows_of, slot_rows, mode_owner
    )

    halo = ITERS - 1
    assert halo < depth and depth == CHUNKS * per_chunk
    ends = coeffs[:, :: depth - 1].reshape(-1, nx, ny)
    early = jnp.concatenate([ends, mean_field], axis=0)
    other, pair = depth_pair(early, early)
    ext = (7, 3 * depth, nx, ny)
    own = jax.ShapeDtypeStruct(coeffs.shape, jnp.float32)
    known, face = pl.pallas_call(
        functools.partial(base_kernel, coef_dev, depth, n_space),
        out_shape=(own, jax.ShapeDtypeStruct(ext, jnp.float32)),
        in_specs=[SMEM] + [VMEM] * 5,
        out_specs=(VMEM, VMEM),
        scratch_shapes=[
            pltpu.VMEM((coef_dev, depth + 2, nx, ny), jnp.float32),
            pltpu.VMEM((3 * depth, nx, ny), jnp.float32),
        ],
        compiler_params=pltpu.CompilerParams(vmem_limit_bytes=8 << 20),
        cost_estimate=cost(depth * coef_dev, nx, ny, 20),
        name="base",
    )(index, coeffs, source, mean_field, other, pair)

    layers = per_chunk
    part, mode_face = pl.pallas_call(
        functools.partial(begin_kernel, coef_dev, depth, layers),
        out_shape=(own, jax.ShapeDtypeStruct((M, 7, depth, nx, ny), jnp.float32)),
        in_specs=[VMEM],
        out_specs=(VMEM, VMEM),
        compiler_params=pltpu.CompilerParams(vmem_limit_bytes=8 << 20),
        cost_estimate=cost(depth * coef_dev, nx, ny, 20),
        name="begin",
    )(sums[0])
    message = jax.ShapeDtypeStruct((coef_dev * (halo + M) + M, nx, ny), jnp.float32)
    rest, to_other, to_pair = pl.pallas_call(
        functools.partial(couple_kernel, coef_dev, depth, layers),
        out_shape=(own, message, message),
        in_specs=[SMEM] + [VMEM] * (3 + len(sums)),
        out_specs=(VMEM, VMEM, VMEM),
        compiler_params=pltpu.CompilerParams(vmem_limit_bytes=8 << 20),
        cost_estimate=cost(depth * coef_dev, nx, ny, 20),
        name="couple",
    )(index, known, part, mode_face, *sums)
    other, pair = depth_pair(to_other, to_pair)
    return pl.pallas_call(
        functools.partial(sweep_kernel, coef_dev, depth, layers),
        out_shape=(own, own),
        in_specs=[SMEM] + [VMEM] * (4 + len(sums)),
        out_specs=(VMEM, VMEM),
        scratch_shapes=[pltpu.VMEM((2, coef_dev * M + M, nx, ny), jnp.float32)]
        + [pltpu.VMEM((coef_dev * 3 * depth * nx, ny), jnp.float32)] * 3,
        compiler_params=pltpu.CompilerParams(vmem_limit_bytes=12 << 20),
        cost_estimate=cost(6 * depth * coef_dev, nx, ny, 40),
        name="sweeps",
    )(index, rest, face, other, pair, *sums)


def solution(mesh):
    in_specs = (
        P("chaos", "space", None, None),
        P("chaos", "space", None, None),
        P("space", None, None),
        P("chaos", "space", None, None),
        P(),
        P("chaos", None, None),
    )
    out_specs = (P("chaos", "space", None, None), P("chaos", "space", None, None))
    step = jax.shard_map(
        residual_and_correction, mesh=mesh, in_specs=in_specs, out_specs=out_specs, check_vma=False
    )
    if not unrolled(mesh.shape["chaos"]):
        return step
    return step
```

```python
import functools

import jax
import jax.numpy as jnp
from jax import lax
from jax.experimental import pallas as pl
from jax.experimental.pallas import tpu as pltpu
from jax.sharding import PartitionSpec as P


M = 2
ITERS = 4

REACTION = 0.5
BOUND_LOW = 0.04
BOUND_HIGH = 2.0

CHUNKS = 2
PARTS = 2
TABLE_ROWS = 8


VMEM = pl.BlockSpec(memory_space=pltpu.VMEM)
SMEM = pl.BlockSpec(memory_space=pltpu.SMEM)


def cost(planes, nx, ny, flops):
    return pl.CostEstimate(
        flops=flops * planes * nx * ny, bytes_accessed=8 * planes * nx * ny, transcendentals=0
    )


def shifted(values, axis, step):
    return pltpu.roll(values, step % values.shape[axis], axis)


def faces(below, own, above):
    nx, ny = own.shape
    ix = lax.broadcasted_iota(jnp.int32, (nx, ny), 0)
    iy = lax.broadcasted_iota(jnp.int32, (nx, ny), 1)
    half = 0.5 * own
    zero = jnp.zeros_like(own)
    xm = jnp.where(ix == 0, zero, half + shifted(half, 0, 1))
    xp = jnp.where(ix == nx - 1, zero, half + shifted(half, 0, -1))
    ym = jnp.where(iy == 0, zero, half + shifted(half, 1, 1))
    yp = jnp.where(iy == ny - 1, zero, half + shifted(half, 1, -1))
    up = half + 0.5 * above
    down = half + 0.5 * below
    total = up + down
    total = total + jnp.where(ix == 0, half, xm) + jnp.where(ix == nx - 1, half, xp)
    total = total + jnp.where(iy == 0, half, ym) + jnp.where(iy == ny - 1, half, yp)
    return xm, xp, ym, yp, down, up, total


def lateral(to_xm, to_xp, to_ym, to_yp):
    return (
        shifted(to_xm, 0, -1)
        + shifted(to_xp, 0, 1)
        + shifted(to_ym, 1, -1)
        + shifted(to_yp, 1, 1)
    )


def pack_kernel(coef_dev, capacity, rows_of, slot_rows, links, coeffs, bank, *refs):
    blocks, (sems,) = refs[: len(rows_of)], refs[len(rows_of) :]
    slot = blocks[0].at[pl.ds(coef_dev * rows_of[0], slot_rows)]
    copies = [pltpu.make_async_copy(bank.at[0], slot, sems.at[len(rows_of) * coef_dev])]
    start = 0
    for j, (block, rows) in enumerate(zip(blocks, rows_of)):
        for c in range(coef_dev):
            copies.append(
                pltpu.make_async_copy(
                    coeffs.at[c, pl.ds(start, rows)],
                    block.at[pl.ds(c * rows, rows)],
                    sems.at[j * coef_dev + c],
                )
            )
        start += rows
    for copy in copies:
        copy.start()
    entries, lanes = links.shape[1], blocks[0].shape[1]
    listed = links[...].astype(jnp.float32)
    s, p, k, level = (listed[i : i + 1] for i in range(4))
    device = jnp.floor((p + 0.5) * (1.0 / coef_dev))
    code = (s * coef_dev + p - device * coef_dev) * M + k
    square = (entries, entries)
    row = lax.broadcasted_iota(jnp.int32, square, 0)
    column = lax.broadcasted_iota(jnp.int32, square, 1)

    def upright(values):
        return jnp.sum(jnp.where(row == column, values, 0.0), axis=1, keepdims=True)

    device_up, level_up = upright(device), upright(level)
    earlier = (device == device_up) & (level > 0.0) & (column < row)
    rank = jnp.sum(jnp.where(earlier, 1.0, 0.0), axis=1, keepdims=True)
    place = jnp.where(level_up > 0.0, device_up * capacity + rank, -1.0)
    lane = lax.broadcasted_iota(jnp.int32, (entries, lanes), 1).astype(jnp.float32)
    table = [
        jnp.sum(jnp.where(place == lane, values, 0.0), axis=0, keepdims=True)
        for values in (upright(code), jnp.sqrt(level_up))
    ]
    table.append(jnp.zeros((TABLE_ROWS - len(table), lanes), jnp.float32))
    table = jnp.concatenate(table, axis=0)
    for block in blocks:
        block[pl.ds(block.shape[0] - TABLE_ROWS, TABLE_ROWS), :] = table
    for copy in copies:
        copy.wait()


def pack(coeffs, bank, links, capacity, rows_of):
    coef_dev, lanes = coeffs.shape[0], coeffs.shape[3]
    whole_rows = coeffs.reshape(coef_dev, -1, lanes)
    slot = bank.reshape(1, -1, lanes)
    slot_rows = slot.shape[1]
    hbm = pl.BlockSpec(memory_space=pltpu.HBM)
    sizes = [
        coef_dev * rows + (slot_rows if j == 0 else 0) + TABLE_ROWS
        for j, rows in enumerate(rows_of)
    ]
    return pl.pallas_call(
        functools.partial(pack_kernel, coef_dev, capacity, rows_of, slot_rows),
        out_shape=[jax.ShapeDtypeStruct((size, lanes), jnp.float32) for size in sizes],
        in_specs=[VMEM, hbm, hbm],
        out_specs=[VMEM] * len(sizes),
        scratch_shapes=[pltpu.SemaphoreType.DMA((len(sizes) * coef_dev + 1,))],
        cost_estimate=cost(coef_dev, sum(rows_of), lanes, 1),
        name="pack",
    )(links.T, whole_rows, slot)


def start_tables(blocks, tables, sems):
    copies = []
    for i, block in enumerate(blocks):
        at = pl.ds(block.shape[0] - TABLE_ROWS, TABLE_ROWS)
        copies.append(pltpu.make_async_copy(block.at[at], tables.at[i], sems.at[i]))
        copies[-1].start()
    return copies


def device_at(me, shift, count):
    half = count // 2
    up = lax.div(me, 2)
    place = jnp.where(lax.rem(me, 2) == 0, up, count - 1 - up)
    q = lax.rem(place + shift % count, count)
    return jnp.where(q < half, 2 * q, 2 * (count - 1 - q) + 1)


def table_scratch(n, lanes):
    return [pltpu.SMEM((n, TABLE_ROWS, lanes), jnp.float32), pltpu.SemaphoreType.DMA((n,))]


def pick_kernel(coef_dev, capacity, rows, shift, count, me, block, out, tables, sems):
    (copy,) = start_tables([block], tables, sems)
    out[capacity * rows :, :] = block[coef_dev * rows :, :]
    begin = device_at(me[0], shift, count) * capacity
    copy.wait()
    for e in range(capacity):
        row = lax.div(tables[0, 0, begin + e].astype(jnp.int32), coef_dev * M)
        out[e * rows : (e + 1) * rows, :] = block[
            pl.ds(pl.multiple_of(row * rows, rows), rows), :
        ]


def pick(block, shift, count, me, coef_dev, capacity, rows):
    size, lanes = block.shape
    return pl.pallas_call(
        functools.partial(pick_kernel, coef_dev, capacity, rows, shift, count),
        out_shape=jax.ShapeDtypeStruct((size - (coef_dev - capacity) * rows, lanes), jnp.float32),
        in_specs=[SMEM, VMEM],
        out_specs=VMEM,
        scratch_shapes=table_scratch(1, lanes),
        compiler_params=pltpu.CompilerParams(vmem_limit_bytes=2 << 20),
        cost_estimate=cost(capacity, rows, lanes, 1),
        name="pick",
    )(me, block)


def sum_kernel(
    picked, shifts, count, coef_dev, capacity, rows, slot_rows, more, me_ref, owner_ref, *refs
):
    refs = list(refs)
    blocks = [refs.pop(0) for _ in picked]
    so_far = refs.pop(0) if more else None
    out, tables, sems = refs
    targets = coef_dev * M
    copies = start_tables(blocks, tables, sems)
    out[...] = so_far[...] if more else jnp.zeros_like(out)
    me = me_ref[0]
    if slot_rows:
        for i, (block, few) in enumerate(zip(blocks, picked)):
            for k in range(M):

                @pl.when(owner_ref[k] == device_at(me, shifts[i], count))
                def _(block=block, k=k, few=few):
                    at = pl.ds(targets * rows + k * slot_rows, slot_rows)
                    out[at, :] = block[pl.ds((capacity if few else coef_dev) * rows, slot_rows), :]

    begin = me * capacity
    for i, (block, few) in enumerate(zip(blocks, picked)):
        copies[i].wait()
        for e in range(capacity):
            code, w = tables[i, 0, begin + e].astype(jnp.int32), tables[i, 1, begin + e]
            row, target = e if few else lax.div(code, targets), lax.rem(code, targets)
            at = pl.ds(pl.multiple_of(target * rows, rows), rows)
            src = block[pl.ds(pl.multiple_of(row * rows, rows), rows), :]
            out[at, :] = out[at, :] + w * src


def sum_blocks(
    blocks, picked, shifts, count, me, owner, coef_dev, capacity, rows, slot_rows, so_far
):
    n, lanes = len(blocks), blocks[0].shape[1]
    size = coef_dev * M * rows + M * slot_rows
    more = so_far is not None
    return pl.pallas_call(
        functools.partial(
            sum_kernel, picked, shifts, count, coef_dev, capacity, rows, slot_rows, more
        ),
        out_shape=jax.ShapeDtypeStruct((size, lanes), jnp.float32),
        in_specs=[SMEM, SMEM] + [VMEM] * (n + more),
        out_specs=VMEM,
        scratch_shapes=table_scratch(n, lanes),
        compiler_params=pltpu.CompilerParams(vmem_limit_bytes=5 << 20),
        cost_estimate=cost(coef_dev * M, rows, lanes, 4),
    )(me, owner, *blocks, *([so_far] if more else []))


def plain_sums(block, table, mode_slot, device, me, mode_owner, coef_dev, capacity, rows):
    targets = coef_dev * M
    code = lax.dynamic_slice(table[0], (me * capacity,), (capacity,)).astype(jnp.int32)
    w = lax.dynamic_slice(table[1], (me * capacity,), (capacity,))
    row = (code[:, None] // targets == jnp.arange(coef_dev)[None, :]).astype(jnp.float32)
    target = (code[:, None] % targets == jnp.arange(targets)[None, :]).astype(jnp.float32)
    matrix = jnp.sum((target * w[:, None])[:, :, None] * row[:, None, :], axis=0)
    data = block[: coef_dev * rows].reshape(coef_dev, -1)
    found = jnp.dot(matrix, data, precision=lax.Precision.HIGHEST)
    found = found.reshape(targets * rows, -1)
    if mode_slot is None:
        return found
    modes = [jnp.where(mode_owner[k] == device, mode_slot, 0.0) for k in range(M)]
    return jnp.concatenate([found, *modes], axis=0)


def unrolled(count):
    return count % 2 == 0 and 6 <= count <= 16


def ring_order(count):
    return list(range(0, count, 2)) + list(range(count - 1, 0, -2))


def ring_steps(count):
    half = count // 2
    return [
        (half, half - 1) if j == 0 else (half - 1, half) for j in range(CHUNKS)
    ]


def sum_parts(count, chunk):
    half = count // 2
    middle, last = list(range(2, half - 1)), [half - 1, half]
    if chunk == 0:
        return {"a": [0, 1], "c": middle + last}
    return {"a": [0, 1], "b": middle, "c": last}


def chaos_sums(chunks, coef_dev, capacity, rows_of, slot_rows, mode_owner):
    count = lax.axis_size("chaos")
    me = lax.axis_index("chaos")
    fixed = (me, mode_owner, coef_dev, capacity)
    if not unrolled(count):
        ring = [(i, (i + 1) % count) for i in range(count)]

        def at_step(step, blocks):
            device = (me - step) % count
            slot_at = coef_dev * rows_of[0]
            table, slot = blocks[0][-TABLE_ROWS:], blocks[0][slot_at : slot_at + slot_rows]
            return [
                plain_sums(b, table, slot if j == 0 else None, device, *fixed, rows_of[j])
                for j, b in enumerate(blocks)
            ]

        def body(step, carry):
            blocks, sums = carry
            blocks = [lax.ppermute(b, "chaos", ring) for b in blocks]
            return blocks, jax.tree.map(jnp.add, sums, at_step(step, blocks))

        return lax.fori_loop(1, count, body, (list(chunks), at_step(0, chunks)))[1]

    order = ring_order(count)
    there = [(order[i], order[(i + 1) % count]) for i in range(count)]
    back = [(b, a) for a, b in there]
    me = me.astype(jnp.int32).reshape(1)
    found = []
    for j, (chunk, steps) in enumerate(zip(chunks, ring_steps(count))):
        blocks = {0: (chunk, False)}
        for pairs, sign, n_steps in ((there, -1, steps[0]), (back, 1, steps[1])):
            block = chunk
            for step in range(1, n_steps + 1):
                if step == n_steps:
                    block = pick(block, -sign, count, me, coef_dev, capacity, rows_of[j])
                block = lax.ppermute(block, "chaos", pairs)
                blocks[sign * step % count] = (block, step == n_steps)
        sums = None
        for distances in sum_parts(count, j).values():
            shifts = sorted({s * d % count for d in distances for s in (1, -1)})
            sums = sum_blocks(
                [blocks[s][0] for s in shifts],
                [blocks[s][1] for s in shifts],
                shifts,
                count,
                me,
                mode_owner,
                coef_dev,
                capacity,
                rows_of[j],
                slot_rows if j == 0 else 0,
                sums,
            )
        found.append(sums)
    return found


def depth_pair(to_other, to_pair):
    count = lax.axis_size("space")
    first = [(i, i ^ 1) for i in range(count) if i ^ 1 < count]
    second = [
        (i, j)
        for i in range(count)
        for j in [i - 1 if i % 2 == 0 else i + 1]
        if 0 <= j < count
    ]
    other = lax.ppermute(to_other, "space", second)
    pair = lax.ppermute(to_pair, "space", first)
    return other, pair


def base_kernel(coef_dev, depth, n_space, space_ref, coeffs, source, mean, *refs):
    other, pair, known, face, coef_ext, mean_ext = refs
    index = space_ref[0]
    even = lax.rem(index, 2) == 0
    for part, below in ((pair, jnp.logical_not(even)), (other, even)):
        at = jnp.where(below, 0, 2 * depth)
        edge = jnp.where(below, 1, 0)
        for c in range(coef_dev):
            coef_ext[c, jnp.where(below, 0, depth + 1)] = part[2 * c + edge]
        mean_ext[pl.ds(at, depth)] = part[2 * coef_dev : 2 * coef_dev + depth]
    for c in range(coef_dev):
        coef_ext[c, 1 : depth + 1] = coeffs[c]
    mean_ext[depth : 2 * depth] = mean[...]

    def layer(l, own):
        xm, xp, ym, yp, down, up, total = faces(mean_ext[l - 1], mean_ext[l], mean_ext[l + 1])
        diagonal = REACTION + total
        absolute = index * depth + l - depth
        inside = (absolute >= 0) & (absolute < n_space * depth)
        inverse = jnp.where(inside, 1.0 / diagonal, 0.0)
        for i, value in enumerate((xm, xp, ym, yp, down, up)):
            face[i, l] = value * inverse
        face[6, l] = inverse
        if own:
            at = l - depth
            for c in range(coef_dev):
                v = coef_ext[c, at + 1]
                spread = lateral(xm * v, xp * v, ym * v, yp * v)
                spread = spread + down * coef_ext[c, at] + up * coef_ext[c, at + 2]
                known[c, at] = source[c, at] - (diagonal * v - spread)

    over_layers(layer, depth, ITERS - 1)


def sweep_constants():
    midpoint = (BOUND_HIGH + BOUND_LOW) / 2.0
    halfwidth = (BOUND_HIGH - BOUND_LOW) / 2.0
    ratio = midpoint / halfwidth
    now = 1.0 / ratio
    steps = []
    for _ in range(ITERS - 1):
        following = 1.0 / (2.0 * ratio - now)
        steps.append((following * now, 2.0 * following / halfwidth))
        now = following
    return midpoint, steps


def plane(sums, layers, nx, target, l):
    at = (target * layers + l % layers) * nx
    return sums[l // layers][at : at + nx, :]


def mode_plane(sums, layers, depth, nx, targets, k, l):
    at = (targets * layers + k * depth + l) * nx
    return sums[0][at : at + nx, :]


def coupled(l, inside, coef_dev, read, mode_face, visit):
    for c in range(coef_dev):
        to, rest = [None] * 4, None

        def add(total, term):
            return term if total is None else total + term

        for k in range(M):
            target = c * M + k
            if l in inside:
                v = read(target, l)
                for q in range(4):
                    to[q] = add(to[q], mode_face[k, q, l] * v)
                rest = add(rest, mode_face[k, 6, l] * v)
            for near, which in ((l - 1, 4), (l + 1, 5)):
                if near in inside:
                    rest = add(rest, mode_face[k, which, l] * read(target, near))
        if rest is not None:
            visit(c, rest + lateral(*to) if l in inside else rest)


def begin_kernel(coef_dev, depth, layers, sums, rest, mode_face):
    nx = rest.shape[2]
    targets = coef_dev * M
    for k in range(M):
        own = [mode_plane([sums], layers, depth, nx, targets, k, l) for l in range(depth)]
        for l in range(depth):
            below = own[l - 1] if l > 0 else -own[l]
            above = own[l + 1] if l + 1 < depth else -own[l]
            *got, total = faces(below, own[l], above)
            for i, value in enumerate((*got, -total)):
                mode_face[k, i, l] = value
    for l in range(depth):
        if l > layers:
            for c in range(coef_dev):
                rest[c, l] = jnp.zeros_like(rest[c, l])

        def visit(c, value, l=l):
            rest[c, l] = value

        coupled(
            l, range(layers), coef_dev,
            lambda target, at: plane([sums], layers, nx, target, at), mode_face, visit,
        )


def couple_kernel(coef_dev, depth, layers, space_ref, known, part, mode_face, *refs):
    sums, (rest, *messages) = refs[: depth // layers], refs[depth // layers :]
    nx = part.shape[2]
    targets = coef_dev * M
    halo = ITERS - 1

    def read(target, l):
        return plane(sums, layers, nx, target, l)

    for l in range(depth):

        def visit(c, value, l=l):
            rest[c, l] = known[c, l] + part[c, l] + value

        late = range(layers, depth)
        if not {l - 1, l, l + 1} & set(late):
            for c in range(coef_dev):
                rest[c, l] = known[c, l] + part[c, l]
        coupled(l, late, coef_dev, read, mode_face, visit)

    even = lax.rem(space_ref[0], 2) == 0

    few = coef_dev // PARTS

    def fill(messages, first, edge):
        for part, message in enumerate(messages):
            for c in range(few):
                message[c * halo : (c + 1) * halo] = rest[part * few + c, first : first + halo]
            for t in range(few * M):
                message[few * halo + t] = read(part * few * M + t, edge)
            for k in range(M):
                message[few * (halo + M) + k] = mode_plane(
                    sums, layers, depth, nx, targets, k, edge
                )

    to_other, to_pair = messages[:PARTS], messages[PARTS:]

    @pl.when(even)
    def _():
        fill(to_pair, depth - halo, depth - 1)
        fill(to_other, 0, 0)

    @pl.when(jnp.logical_not(even))
    def _():
        fill(to_pair, 0, 0)
        fill(to_other, depth - halo, depth - 1)


def sweep_kernel(part, coef_dev, depth, layers, space_ref, rest, face, other, pair, *refs):
    sums = refs[: depth // layers]
    residual, correction, edges, scaled, first, second = refs[-6:]
    nx = rest.shape[2]
    targets = coef_dev * M
    halo = ITERS - 1
    few = coef_dev // PARTS
    even = lax.rem(space_ref[0], 2) == 0

    def rows(c, l):
        return pl.ds(pl.multiple_of((c * 3 * depth + l) * nx, nx), nx)

    for message, below in ((pair, jnp.logical_not(even)), (other, even)):
        at = jnp.where(below, depth - halo, 2 * depth)
        for c in range(few):
            for i in range(halo):
                scaled[rows(c, at + i), :] = message[c * halo + i]
        edges[jnp.where(below, 0, 1)] = message[few * halo :]
    half_modes = [
        [
            0.5 * (mode_plane(sums, layers, depth, nx, targets, k, l) + edges[side, few * M + k])
            for k in range(M)
        ]
        for side, l in ((0, 0), (1, depth - 1))
    ]
    for c in range(few):
        for l in range(depth):
            total = rest[part * few + c, l]
            for side, edge, beyond in ((0, 0, depth - 1), (1, depth - 1, 2 * depth)):
                if l != edge:
                    continue
                flux = None
                for k in range(M):
                    own = plane(sums, layers, nx, (part * few + c) * M + k, l)
                    term = half_modes[side][k] * (own - edges[side, c * M + k])
                    flux = term if flux is None else flux + term
                total = total - flux
                scaled[rows(c, beyond), :] = scaled[rows(c, beyond), :] + flux
            residual[c, l] = total
            scaled[rows(c, depth + l), :] = total

    midpoint, steps = sweep_constants()

    def start(l, own):
        for c in range(few):
            w = scaled[rows(c, l), :] * face[6, l]
            d = w * (1.0 / midpoint)
            scaled[rows(c, l), :] = w
            first[rows(c, l), :] = d
            if own:
                correction[c, l - depth] = d

    over_layers(start, depth, halo)

    now, later = first, second
    for number, (keep, gain) in enumerate(steps):

        def swept(l, own, now=now, later=later, keep=keep, gain=gain, number=number):
            for c in range(few):
                at = pl.multiple_of((c * 3 * depth + l) * nx, nx)
                here = pl.ds(at, nx)
                v = now[here, :]
                w = scaled[here, :] - v
                w = w + face[0, l] * now[pl.ds(at - 1, nx), :]
                w = w + face[1, l] * now[pl.ds(at + 1, nx), :]
                w = w + face[2, l] * shifted(v, 1, 1) + face[3, l] * shifted(v, 1, -1)
                w = w + face[4, l] * now[pl.ds(at - nx, nx), :]
                w = w + face[5, l] * now[pl.ds(at + nx, nx), :]
                d = keep * v + gain * w
                if number + 1 < len(steps):
                    scaled[here, :] = w
                    later[here, :] = d
                if own:
                    correction[c, l - depth] = correction[c, l - depth] + d

        over_layers(swept, depth, len(steps) - 1 - number)
        now, later = later, now


def over_layers(visit, depth, halo):
    def own(i, carry):
        for l in range(2):
            visit(depth + 2 * i + l, True)
        return carry

    def outside(i, carry):
        visit(depth - halo + i, False)
        visit(2 * depth + i, False)
        return carry

    assert depth % 2 == 0
    lax.fori_loop(0, depth // 2, own, 0)
    if halo:
        lax.fori_loop(0, halo, outside, 0)


def residual_and_correction(coeffs, source, mean_field, mode_bank, mode_owner, links):
    coef_dev, depth, nx, ny = coeffs.shape
    n_space = lax.axis_size("space")
    slot_rows = depth * nx
    per_chunk = depth // CHUNKS
    layer_counts = [per_chunk] * CHUNKS
    index = lax.axis_index("space").astype(jnp.int32).reshape(1)

    rows_of = [layers * nx for layers in layer_counts]
    count = lax.axis_size("chaos")
    shifts = count // 2 - 1
    capacity = max(2, (M * coef_dev - 1 + shifts - 1) // shifts)
    assert count * capacity <= ny
    chunks = pack(coeffs, mode_bank, links[0], capacity, rows_of)

    sums = chaos_sums(
        chunks, coef_dev, capacity, rows_of, slot_rows, mode_owner
    )

    halo = ITERS - 1
    assert halo < depth and depth == CHUNKS * per_chunk
    ends = coeffs[:, :: depth - 1].reshape(-1, nx, ny)
    early = jnp.concatenate([ends, mean_field], axis=0)
    other, pair = depth_pair(early, early)
    ext = (7, 3 * depth, nx, ny)
    own = jax.ShapeDtypeStruct(coeffs.shape, jnp.float32)
    known, face = pl.pallas_call(
        functools.partial(base_kernel, coef_dev, depth, n_space),
        out_shape=(own, jax.ShapeDtypeStruct(ext, jnp.float32)),
        in_specs=[SMEM] + [VMEM] * 5,
        out_specs=(VMEM, VMEM),
        scratch_shapes=[
            pltpu.VMEM((coef_dev, depth + 2, nx, ny), jnp.float32),
            pltpu.VMEM((3 * depth, nx, ny), jnp.float32),
        ],
        compiler_params=pltpu.CompilerParams(vmem_limit_bytes=8 << 20),
        cost_estimate=cost(depth * coef_dev, nx, ny, 20),
        name="base",
    )(index, coeffs, source, mean_field, other, pair)

    layers = per_chunk
    part, mode_face = pl.pallas_call(
        functools.partial(begin_kernel, coef_dev, depth, layers),
        out_shape=(own, jax.ShapeDtypeStruct((M, 7, depth, nx, ny), jnp.float32)),
        in_specs=[VMEM],
        out_specs=(VMEM, VMEM),
        compiler_params=pltpu.CompilerParams(vmem_limit_bytes=8 << 20),
        cost_estimate=cost(depth * coef_dev, nx, ny, 20),
        name="begin",
    )(sums[0])
    few = coef_dev // PARTS
    message = jax.ShapeDtypeStruct((few * (halo + M) + M, nx, ny), jnp.float32)
    rest, *messages = pl.pallas_call(
        functools.partial(couple_kernel, coef_dev, depth, layers),
        out_shape=[own] + [message] * (2 * PARTS),
        in_specs=[SMEM] + [VMEM] * (3 + len(sums)),
        out_specs=[VMEM] * (1 + 2 * PARTS),
        compiler_params=pltpu.CompilerParams(vmem_limit_bytes=8 << 20),
        cost_estimate=cost(depth * coef_dev, nx, ny, 20),
        name="couple",
    )(index, known, part, mode_face, *sums)
    found = []
    for h in range(PARTS):
        other, pair = depth_pair(messages[h], messages[PARTS + h])
        first = 5 + len(sums)
        found = pl.pallas_call(
            functools.partial(sweep_kernel, h, coef_dev, depth, layers),
            grid=(1,),
            out_shape=(own, own),
            in_specs=[SMEM]
            + [VMEM] * (first - 1)
            + [pl.BlockSpec(memory_space=pl.ANY)] * len(found),
            out_specs=[pl.BlockSpec((few, depth, nx, ny), lambda i, h=h: (h, 0, 0, 0))] * 2,
            scratch_shapes=[pltpu.VMEM((2, few * M + M, nx, ny), jnp.float32)]
            + [pltpu.VMEM((few * 3 * depth * nx, ny), jnp.float32)] * 3,
            input_output_aliases={first + i: i for i in range(len(found))},
            compiler_params=pltpu.CompilerParams(vmem_limit_bytes=12 << 20),
            cost_estimate=cost(3 * depth * coef_dev, nx, ny, 40),
        )(index, rest, face, other, pair, *sums, *found)
    return tuple(found)


def solution(mesh):
    in_specs = (
        P("chaos", "space", None, None),
        P("chaos", "space", None, None),
        P("space", None, None),
        P("chaos", "space", None, None),
        P(),
        P("chaos", None, None),
    )
    out_specs = (P("chaos", "space", None, None), P("chaos", "space", None, None))
    step = jax.shard_map(
        residual_and_correction, mesh=mesh, in_specs=in_specs, out_specs=out_specs, check_vma=False
    )
    if not unrolled(mesh.shape["chaos"]):
        return step
    return step
```

```python
import functools

import jax
import jax.numpy as jnp
from jax import lax
from jax.experimental import pallas as pl
from jax.experimental.pallas import tpu as pltpu
from jax.sharding import PartitionSpec as P


M = 2
ITERS = 4

REACTION = 0.5
BOUND_LOW = 0.04
BOUND_HIGH = 2.0

CHUNKS = 2
PARTS = 2
TABLE_ROWS = 8


VMEM = pl.BlockSpec(memory_space=pltpu.VMEM)
SMEM = pl.BlockSpec(memory_space=pltpu.SMEM)


def cost(planes, nx, ny, flops):
    return pl.CostEstimate(
        flops=flops * planes * nx * ny, bytes_accessed=8 * planes * nx * ny, transcendentals=0
    )


def shifted(values, axis, step):
    return pltpu.roll(values, step % values.shape[axis], axis)


def faces(below, own, above):
    nx, ny = own.shape
    ix = lax.broadcasted_iota(jnp.int32, (nx, ny), 0)
    iy = lax.broadcasted_iota(jnp.int32, (nx, ny), 1)
    half = 0.5 * own
    zero = jnp.zeros_like(own)
    xm = jnp.where(ix == 0, zero, half + shifted(half, 0, 1))
    xp = jnp.where(ix == nx - 1, zero, half + shifted(half, 0, -1))
    ym = jnp.where(iy == 0, zero, half + shifted(half, 1, 1))
    yp = jnp.where(iy == ny - 1, zero, half + shifted(half, 1, -1))
    up = half + 0.5 * above
    down = half + 0.5 * below
    total = up + down
    total = total + jnp.where(ix == 0, half, xm) + jnp.where(ix == nx - 1, half, xp)
    total = total + jnp.where(iy == 0, half, ym) + jnp.where(iy == ny - 1, half, yp)
    return xm, xp, ym, yp, down, up, total


def lateral(to_xm, to_xp, to_ym, to_yp):
    return (
        shifted(to_xm, 0, -1)
        + shifted(to_xp, 0, 1)
        + shifted(to_ym, 1, -1)
        + shifted(to_yp, 1, 1)
    )


def pack_kernel(coef_dev, capacity, rows_of, slot_rows, links, coeffs, bank, *refs):
    blocks, (listed, sems, link_sem) = refs[: len(rows_of)], refs[len(rows_of) :]
    link_copy = pltpu.make_async_copy(links, listed, link_sem)
    link_copy.start()
    slot = blocks[0].at[pl.ds(coef_dev * rows_of[0], slot_rows)]
    copies = [pltpu.make_async_copy(bank.at[0], slot, sems.at[len(rows_of) * coef_dev])]
    start = 0
    for j, (block, rows) in enumerate(zip(blocks, rows_of)):
        for c in range(coef_dev):
            copies.append(
                pltpu.make_async_copy(
                    coeffs.at[c, pl.ds(start, rows)],
                    block.at[pl.ds(c * rows, rows)],
                    sems.at[j * coef_dev + c],
                )
            )
        start += rows
    for copy in copies:
        copy.start()
    entries, lanes = links.shape[1], blocks[0].shape[1]
    link_copy.wait()
    values = listed[...].astype(jnp.float32)
    s, p, k, level = (values[i : i + 1] for i in range(4))
    device = jnp.floor((p + 0.5) * (1.0 / coef_dev))
    code = (s * coef_dev + p - device * coef_dev) * M + k
    square = (entries, entries)
    row = lax.broadcasted_iota(jnp.int32, square, 0)
    column = lax.broadcasted_iota(jnp.int32, square, 1)

    def upright(values):
        return jnp.sum(jnp.where(row == column, values, 0.0), axis=1, keepdims=True)

    device_up, level_up = upright(device), upright(level)
    earlier = (device == device_up) & (level > 0.0) & (column < row)
    rank = jnp.sum(jnp.where(earlier, 1.0, 0.0), axis=1, keepdims=True)
    place = jnp.where(level_up > 0.0, device_up * capacity + rank, -1.0)
    lane = lax.broadcasted_iota(jnp.int32, (entries, lanes), 1).astype(jnp.float32)
    table = [
        jnp.sum(jnp.where(place == lane, values, 0.0), axis=0, keepdims=True)
        for values in (upright(code), jnp.sqrt(level_up))
    ]
    table.append(jnp.zeros((TABLE_ROWS - len(table), lanes), jnp.float32))
    table = jnp.concatenate(table, axis=0)
    for block in blocks:
        block[pl.ds(block.shape[0] - TABLE_ROWS, TABLE_ROWS), :] = table
    for copy in copies:
        copy.wait()


def pack(coeffs, bank, links, capacity, rows_of):
    coef_dev, lanes = coeffs.shape[0], coeffs.shape[3]
    whole_rows = coeffs.reshape(coef_dev, -1, lanes)
    slot = bank.reshape(1, -1, lanes)
    slot_rows = slot.shape[1]
    hbm = pl.BlockSpec(memory_space=pltpu.HBM)
    sizes = [
        coef_dev * rows + (slot_rows if j == 0 else 0) + TABLE_ROWS
        for j, rows in enumerate(rows_of)
    ]
    return pl.pallas_call(
        functools.partial(pack_kernel, coef_dev, capacity, rows_of, slot_rows),
        out_shape=[jax.ShapeDtypeStruct((size, lanes), jnp.float32) for size in sizes],
        in_specs=[hbm, hbm, hbm],
        out_specs=[VMEM] * len(sizes),
        scratch_shapes=[
            pltpu.VMEM((links.shape[1], links.shape[0]), jnp.int32),
            pltpu.SemaphoreType.DMA((len(sizes) * coef_dev + 1,)),
            pltpu.SemaphoreType.DMA(()),
        ],
        cost_estimate=cost(coef_dev, sum(rows_of), lanes, 1),
        name="pack",
    )(links.T, whole_rows, slot)


def start_tables(blocks, tables, sems):
    copies = []
    for i, block in enumerate(blocks):
        at = pl.ds(block.shape[0] - TABLE_ROWS, TABLE_ROWS)
        copies.append(pltpu.make_async_copy(block.at[at], tables.at[i], sems.at[i]))
        copies[-1].start()
    return copies


def device_at(me, shift, count):
    half = count // 2
    up = lax.div(me, 2)
    place = jnp.where(lax.rem(me, 2) == 0, up, count - 1 - up)
    q = lax.rem(place + shift % count, count)
    return jnp.where(q < half, 2 * q, 2 * (count - 1 - q) + 1)


def table_scratch(n, lanes):
    return [pltpu.SMEM((n, TABLE_ROWS, lanes), jnp.float32), pltpu.SemaphoreType.DMA((n,))]


def pick_kernel(coef_dev, capacity, rows, shift, count, me, block, out, tables, sems):
    (copy,) = start_tables([block], tables, sems)
    out[capacity * rows :, :] = block[coef_dev * rows :, :]
    begin = device_at(me[0], shift, count) * capacity
    copy.wait()
    for e in range(capacity):
        row = lax.div(tables[0, 0, begin + e].astype(jnp.int32), coef_dev * M)
        out[e * rows : (e + 1) * rows, :] = block[
            pl.ds(pl.multiple_of(row * rows, rows), rows), :
        ]


def pick(block, shift, count, me, coef_dev, capacity, rows):
    size, lanes = block.shape
    return pl.pallas_call(
        functools.partial(pick_kernel, coef_dev, capacity, rows, shift, count),
        out_shape=jax.ShapeDtypeStruct((size - (coef_dev - capacity) * rows, lanes), jnp.float32),
        in_specs=[SMEM, VMEM],
        out_specs=VMEM,
        scratch_shapes=table_scratch(1, lanes),
        compiler_params=pltpu.CompilerParams(vmem_limit_bytes=2 << 20),
        cost_estimate=cost(capacity, rows, lanes, 1),
        name="pick",
    )(me, block)


def sum_kernel(
    picked, shifts, count, coef_dev, capacity, rows, slot_rows, more, me_ref, owner_ref, *refs
):
    refs = list(refs)
    blocks = [refs.pop(0) for _ in picked]
    so_far = refs.pop(0) if more else None
    out, tables, sems = refs
    targets = coef_dev * M
    copies = start_tables(blocks, tables, sems)
    out[...] = so_far[...] if more else jnp.zeros_like(out)
    me = me_ref[0]
    if slot_rows:
        for i, (block, few) in enumerate(zip(blocks, picked)):
            for k in range(M):

                @pl.when(owner_ref[k] == device_at(me, shifts[i], count))
                def _(block=block, k=k, few=few):
                    at = pl.ds(targets * rows + k * slot_rows, slot_rows)
                    out[at, :] = block[pl.ds((capacity if few else coef_dev) * rows, slot_rows), :]

    begin = me * capacity
    for i, (block, few) in enumerate(zip(blocks, picked)):
        copies[i].wait()
        for e in range(capacity):
            code, w = tables[i, 0, begin + e].astype(jnp.int32), tables[i, 1, begin + e]
            row, target = e if few else lax.div(code, targets), lax.rem(code, targets)
            at = pl.ds(pl.multiple_of(target * rows, rows), rows)
            src = block[pl.ds(pl.multiple_of(row * rows, rows), rows), :]
            out[at, :] = out[at, :] + w * src


def sum_blocks(
    blocks, picked, shifts, count, me, owner, coef_dev, capacity, rows, slot_rows, so_far
):
    n, lanes = len(blocks), blocks[0].shape[1]
    size = coef_dev * M * rows + M * slot_rows
    more = so_far is not None
    return pl.pallas_call(
        functools.partial(
            sum_kernel, picked, shifts, count, coef_dev, capacity, rows, slot_rows, more
        ),
        out_shape=jax.ShapeDtypeStruct((size, lanes), jnp.float32),
        in_specs=[SMEM, SMEM] + [VMEM] * (n + more),
        out_specs=VMEM,
        scratch_shapes=table_scratch(n, lanes),
        compiler_params=pltpu.CompilerParams(vmem_limit_bytes=5 << 20),
        cost_estimate=cost(coef_dev * M, rows, lanes, 4),
    )(me, owner, *blocks, *([so_far] if more else []))


def plain_sums(block, table, mode_slot, device, me, mode_owner, coef_dev, capacity, rows):
    targets = coef_dev * M
    code = lax.dynamic_slice(table[0], (me * capacity,), (capacity,)).astype(jnp.int32)
    w = lax.dynamic_slice(table[1], (me * capacity,), (capacity,))
    row = (code[:, None] // targets == jnp.arange(coef_dev)[None, :]).astype(jnp.float32)
    target = (code[:, None] % targets == jnp.arange(targets)[None, :]).astype(jnp.float32)
    matrix = jnp.sum((target * w[:, None])[:, :, None] * row[:, None, :], axis=0)
    data = block[: coef_dev * rows].reshape(coef_dev, -1)
    found = jnp.dot(matrix, data, precision=lax.Precision.HIGHEST)
    found = found.reshape(targets * rows, -1)
    if mode_slot is None:
        return found
    modes = [jnp.where(mode_owner[k] == device, mode_slot, 0.0) for k in range(M)]
    return jnp.concatenate([found, *modes], axis=0)


def unrolled(count):
    return count % 2 == 0 and 6 <= count <= 16


def ring_order(count):
    return list(range(0, count, 2)) + list(range(count - 1, 0, -2))


def ring_steps(count):
    half = count // 2
    return [
        (half, half - 1) if j == 0 else (half - 1, half) for j in range(CHUNKS)
    ]


def sum_parts(count, chunk):
    half = count // 2
    middle, last = list(range(2, half - 1)), [half - 1, half]
    if chunk == 0:
        return {"a": [0, 1], "b": middle, "c": last}
    return {"a": [0, 1], "b": middle + last[:1], "c": last[1:]}


def chaos_sums(chunks, coef_dev, capacity, rows_of, slot_rows, mode_owner):
    count = lax.axis_size("chaos")
    me = lax.axis_index("chaos")
    fixed = (me, mode_owner, coef_dev, capacity)
    if not unrolled(count):
        ring = [(i, (i + 1) % count) for i in range(count)]

        def at_step(step, blocks):
            device = (me - step) % count
            slot_at = coef_dev * rows_of[0]
            table, slot = blocks[0][-TABLE_ROWS:], blocks[0][slot_at : slot_at + slot_rows]
            return [
                plain_sums(b, table, slot if j == 0 else None, device, *fixed, rows_of[j])
                for j, b in enumerate(blocks)
            ]

        def body(step, carry):
            blocks, sums = carry
            blocks = [lax.ppermute(b, "chaos", ring) for b in blocks]
            return blocks, jax.tree.map(jnp.add, sums, at_step(step, blocks))

        return lax.fori_loop(1, count, body, (list(chunks), at_step(0, chunks)))[1]

    order = ring_order(count)
    there = [(order[i], order[(i + 1) % count]) for i in range(count)]
    back = [(b, a) for a, b in there]
    me = me.astype(jnp.int32).reshape(1)
    found = []
    for j, (chunk, steps) in enumerate(zip(chunks, ring_steps(count))):
        blocks = {0: (chunk, False)}
        for pairs, sign, n_steps in ((there, -1, steps[0]), (back, 1, steps[1])):
            block = chunk
            for step in range(1, n_steps + 1):
                if step == n_steps:
                    block = pick(block, -sign, count, me, coef_dev, capacity, rows_of[j])
                block = lax.ppermute(block, "chaos", pairs)
                blocks[sign * step % count] = (block, step == n_steps)
        sums = None
        for distances in sum_parts(count, j).values():
            shifts = sorted({s * d % count for d in distances for s in (1, -1)})
            sums = sum_blocks(
                [blocks[s][0] for s in shifts],
                [blocks[s][1] for s in shifts],
                shifts,
                count,
                me,
                mode_owner,
                coef_dev,
                capacity,
                rows_of[j],
                slot_rows if j == 0 else 0,
                sums,
            )
        found.append(sums)
    return found


def depth_pair(to_other, to_pair):
    count = lax.axis_size("space")
    first = [(i, i ^ 1) for i in range(count) if i ^ 1 < count]
    second = [
        (i, j)
        for i in range(count)
        for j in [i - 1 if i % 2 == 0 else i + 1]
        if 0 <= j < count
    ]
    other = lax.ppermute(to_other, "space", second)
    pair = lax.ppermute(to_pair, "space", first)
    return other, pair


def base_kernel(coef_dev, depth, n_space, space_ref, coeffs, source, mean, *refs):
    other, pair, known, face, coef_ext, mean_ext = refs
    index = space_ref[0]
    even = lax.rem(index, 2) == 0
    for part, below in ((pair, jnp.logical_not(even)), (other, even)):
        at = jnp.where(below, 0, 2 * depth)
        edge = jnp.where(below, 1, 0)
        for c in range(coef_dev):
            coef_ext[c, jnp.where(below, 0, depth + 1)] = part[2 * c + edge]
        mean_ext[pl.ds(at, depth)] = part[2 * coef_dev : 2 * coef_dev + depth]
    for c in range(coef_dev):
        coef_ext[c, 1 : depth + 1] = coeffs[c]
    mean_ext[depth : 2 * depth] = mean[...]

    def layer(l, own):
        xm, xp, ym, yp, down, up, total = faces(mean_ext[l - 1], mean_ext[l], mean_ext[l + 1])
        diagonal = REACTION + total
        absolute = index * depth + l - depth
        inside = (absolute >= 0) & (absolute < n_space * depth)
        inverse = jnp.where(inside, 1.0 / diagonal, 0.0)
        for i, value in enumerate((xm, xp, ym, yp, down, up)):
            face[i, l] = value * inverse
        face[6, l] = inverse
        if own:
            at = l - depth
            for c in range(coef_dev):
                v = coef_ext[c, at + 1]
                spread = lateral(xm * v, xp * v, ym * v, yp * v)
                spread = spread + down * coef_ext[c, at] + up * coef_ext[c, at + 2]
                known[c, at] = source[c, at] - (diagonal * v - spread)

    over_layers(layer, depth, ITERS - 1)


def sweep_constants():
    midpoint = (BOUND_HIGH + BOUND_LOW) / 2.0
    halfwidth = (BOUND_HIGH - BOUND_LOW) / 2.0
    ratio = midpoint / halfwidth
    now = 1.0 / ratio
    steps = []
    for _ in range(ITERS - 1):
        following = 1.0 / (2.0 * ratio - now)
        steps.append((following * now, 2.0 * following / halfwidth))
        now = following
    return midpoint, steps


def plane(sums, layers, nx, target, l):
    at = (target * layers + l % layers) * nx
    return sums[l // layers][at : at + nx, :]


def mode_plane(sums, layers, depth, nx, targets, k, l):
    at = (targets * layers + k * depth + l) * nx
    return sums[0][at : at + nx, :]


def coupled(l, inside, coef_dev, read, mode_face, visit):
    for c in range(coef_dev):
        to, rest = [None] * 4, None

        def add(total, term):
            return term if total is None else total + term

        for k in range(M):
            target = c * M + k
            if l in inside:
                v = read(target, l)
                for q in range(4):
                    to[q] = add(to[q], mode_face[k, q, l] * v)
                rest = add(rest, mode_face[k, 6, l] * v)
            for near, which in ((l - 1, 4), (l + 1, 5)):
                if near in inside:
                    rest = add(rest, mode_face[k, which, l] * read(target, near))
        if rest is not None:
            visit(c, rest + lateral(*to) if l in inside else rest)


def begin_kernel(coef_dev, depth, layers, sums, rest, mode_face):
    nx = rest.shape[2]
    targets = coef_dev * M
    for k in range(M):
        own = [mode_plane([sums], layers, depth, nx, targets, k, l) for l in range(depth)]
        for l in range(depth):
            below = own[l - 1] if l > 0 else -own[l]
            above = own[l + 1] if l + 1 < depth else -own[l]
            *got, total = faces(below, own[l], above)
            for i, value in enumerate((*got, -total)):
                mode_face[k, i, l] = value
    for l in range(depth):
        if l > layers:
            for c in range(coef_dev):
                rest[c, l] = jnp.zeros_like(rest[c, l])

        def visit(c, value, l=l):
            rest[c, l] = value

        coupled(
            l, range(layers), coef_dev,
            lambda target, at: plane([sums], layers, nx, target, at), mode_face, visit,
        )


def couple_kernel(coef_dev, depth, layers, space_ref, known, part, mode_face, *refs):
    sums, (rest, *messages) = refs[: depth // layers], refs[depth // layers :]
    nx = part.shape[2]
    targets = coef_dev * M
    halo = ITERS - 1

    def read(target, l):
        return plane(sums, layers, nx, target, l)

    for l in range(depth):

        def visit(c, value, l=l):
            rest[c, l] = known[c, l] + part[c, l] + value

        late = range(layers, depth)
        if not {l - 1, l, l + 1} & set(late):
            for c in range(coef_dev):
                rest[c, l] = known[c, l] + part[c, l]
        coupled(l, late, coef_dev, read, mode_face, visit)

    even = lax.rem(space_ref[0], 2) == 0

    few = coef_dev // PARTS

    def fill(messages, first, edge):
        for part, message in enumerate(messages):
            for c in range(few):
                message[c * halo : (c + 1) * halo] = rest[part * few + c, first : first + halo]
            for t in range(few * M):
                message[few * halo + t] = read(part * few * M + t, edge)
            if part == 0:
                for k in range(M):
                    message[few * (halo + M) + k] = mode_plane(
                        sums, layers, depth, nx, targets, k, edge
                    )

    to_other, to_pair = messages[:PARTS], messages[PARTS:]

    @pl.when(even)
    def _():
        fill(to_pair, depth - halo, depth - 1)
        fill(to_other, 0, 0)

    @pl.when(jnp.logical_not(even))
    def _():
        fill(to_pair, 0, 0)
        fill(to_other, depth - halo, depth - 1)


def sweep_kernel(part, coef_dev, depth, layers, space_ref, rest, face, other, pair, *refs):
    first_other, first_pair, *sums = refs[: 2 + depth // layers]
    residual, correction, edges, scaled, first, second = refs[-6:]
    nx = rest.shape[2]
    targets = coef_dev * M
    halo = ITERS - 1
    few = coef_dev // PARTS
    even = lax.rem(space_ref[0], 2) == 0

    def rows(c, l):
        return pl.ds(pl.multiple_of((c * 3 * depth + l) * nx, nx), nx)

    for message, modes, below in (
        (pair, first_pair, jnp.logical_not(even)),
        (other, first_other, even),
    ):
        at = jnp.where(below, depth - halo, 2 * depth)
        for c in range(few):
            for i in range(halo):
                scaled[rows(c, at + i), :] = message[c * halo + i]
        side = jnp.where(below, 0, 1)
        edges[side, : few * M] = message[few * halo : few * (halo + M)]
        edges[side, few * M :] = modes[few * (halo + M) :]
    half_modes = [
        [
            0.5 * (mode_plane(sums, layers, depth, nx, targets, k, l) + edges[side, few * M + k])
            for k in range(M)
        ]
        for side, l in ((0, 0), (1, depth - 1))
    ]
    for c in range(few):
        for l in range(depth):
            total = rest[part * few + c, l]
            for side, edge, beyond in ((0, 0, depth - 1), (1, depth - 1, 2 * depth)):
                if l != edge:
                    continue
                flux = None
                for k in range(M):
                    own = plane(sums, layers, nx, (part * few + c) * M + k, l)
                    term = half_modes[side][k] * (own - edges[side, c * M + k])
                    flux = term if flux is None else flux + term
                total = total - flux
                scaled[rows(c, beyond), :] = scaled[rows(c, beyond), :] + flux
            residual[c, l] = total
            scaled[rows(c, depth + l), :] = total

    midpoint, steps = sweep_constants()

    def start(l, own):
        for c in range(few):
            w = scaled[rows(c, l), :] * face[6, l]
            d = w * (1.0 / midpoint)
            scaled[rows(c, l), :] = w
            first[rows(c, l), :] = d
            if own:
                correction[c, l - depth] = d

    over_layers(start, depth, halo)

    now, later = first, second
    for number, (keep, gain) in enumerate(steps):

        def swept(l, own, now=now, later=later, keep=keep, gain=gain, number=number):
            for c in range(few):
                at = pl.multiple_of((c * 3 * depth + l) * nx, nx)
                here = pl.ds(at, nx)
                v = now[here, :]
                w = scaled[here, :] - v
                w = w + face[0, l] * now[pl.ds(at - 1, nx), :]
                w = w + face[1, l] * now[pl.ds(at + 1, nx), :]
                w = w + face[2, l] * shifted(v, 1, 1) + face[3, l] * shifted(v, 1, -1)
                w = w + face[4, l] * now[pl.ds(at - nx, nx), :]
                w = w + face[5, l] * now[pl.ds(at + nx, nx), :]
                d = keep * v + gain * w
                if number + 1 < len(steps):
                    scaled[here, :] = w
                    later[here, :] = d
                if own:
                    correction[c, l - depth] = correction[c, l - depth] + d

        over_layers(swept, depth, len(steps) - 1 - number)
        now, later = later, now


def over_layers(visit, depth, halo):
    def own(i, carry):
        for l in range(2):
            visit(depth + 2 * i + l, True)
        return carry

    def outside(i, carry):
        visit(depth - halo + i, False)
        visit(2 * depth + i, False)
        return carry

    assert depth % 2 == 0
    lax.fori_loop(0, depth // 2, own, 0)
    if halo:
        lax.fori_loop(0, halo, outside, 0)


def residual_and_correction(coeffs, source, mean_field, mode_bank, mode_owner, links):
    coef_dev, depth, nx, ny = coeffs.shape
    n_space = lax.axis_size("space")
    slot_rows = depth * nx
    per_chunk = depth // CHUNKS
    layer_counts = [per_chunk] * CHUNKS
    index = lax.axis_index("space").astype(jnp.int32).reshape(1)

    rows_of = [layers * nx for layers in layer_counts]
    count = lax.axis_size("chaos")
    shifts = count // 2 - 1
    capacity = max(2, (M * coef_dev - 1 + shifts - 1) // shifts)
    assert count * capacity <= ny
    chunks = pack(coeffs, mode_bank, links[0], capacity, rows_of)

    sums = chaos_sums(
        chunks, coef_dev, capacity, rows_of, slot_rows, mode_owner
    )

    halo = ITERS - 1
    assert halo < depth and depth == CHUNKS * per_chunk
    ends = coeffs[:, :: depth - 1].reshape(-1, nx, ny)
    early = jnp.concatenate([ends, mean_field], axis=0)
    other, pair = depth_pair(early, early)
    ext = (7, 3 * depth, nx, ny)
    own = jax.ShapeDtypeStruct(coeffs.shape, jnp.float32)
    known, face = pl.pallas_call(
        functools.partial(base_kernel, coef_dev, depth, n_space),
        out_shape=(own, jax.ShapeDtypeStruct(ext, jnp.float32)),
        in_specs=[SMEM] + [VMEM] * 5,
        out_specs=(VMEM, VMEM),
        scratch_shapes=[
            pltpu.VMEM((coef_dev, depth + 2, nx, ny), jnp.float32),
            pltpu.VMEM((3 * depth, nx, ny), jnp.float32),
        ],
        compiler_params=pltpu.CompilerParams(vmem_limit_bytes=8 << 20),
        cost_estimate=cost(depth * coef_dev, nx, ny, 20),
        name="base",
    )(index, coeffs, source, mean_field, other, pair)

    layers = per_chunk
    part, mode_face = pl.pallas_call(
        functools.partial(begin_kernel, coef_dev, depth, layers),
        out_shape=(own, jax.ShapeDtypeStruct((M, 7, depth, nx, ny), jnp.float32)),
        in_specs=[VMEM],
        out_specs=(VMEM, VMEM),
        compiler_params=pltpu.CompilerParams(vmem_limit_bytes=8 << 20),
        cost_estimate=cost(depth * coef_dev, nx, ny, 20),
        name="begin",
    )(sums[0])
    few = coef_dev // PARTS
    message = [
        jax.ShapeDtypeStruct((few * (halo + M) + (M if h == 0 else 0), nx, ny), jnp.float32)
        for h in range(PARTS)
    ]
    rest, *messages = pl.pallas_call(
        functools.partial(couple_kernel, coef_dev, depth, layers),
        out_shape=[own] + message * 2,
        in_specs=[SMEM] + [VMEM] * (3 + len(sums)),
        out_specs=[VMEM] * (1 + 2 * PARTS),
        compiler_params=pltpu.CompilerParams(vmem_limit_bytes=8 << 20),
        cost_estimate=cost(depth * coef_dev, nx, ny, 20),
        name="couple",
    )(index, known, part, mode_face, *sums)
    found = []
    for h in range(PARTS):
        other, pair = depth_pair(messages[h], messages[PARTS + h])
        if h == 0:
            modes = (other, pair)
        first = 7 + len(sums)
        found = pl.pallas_call(
            functools.partial(sweep_kernel, h, coef_dev, depth, layers),
            grid=(1,),
            out_shape=(own, own),
            in_specs=[SMEM]
            + [VMEM] * (first - 1)
            + [pl.BlockSpec(memory_space=pl.ANY)] * len(found),
            out_specs=[pl.BlockSpec((few, depth, nx, ny), lambda i, h=h: (h, 0, 0, 0))] * 2,
            scratch_shapes=[pltpu.VMEM((2, few * M + M, nx, ny), jnp.float32)]
            + [pltpu.VMEM((few * 3 * depth * nx, ny), jnp.float32)] * 3,
            input_output_aliases={first + i: i for i in range(len(found))},
            compiler_params=pltpu.CompilerParams(vmem_limit_bytes=12 << 20),
            cost_estimate=cost(3 * depth * coef_dev, nx, ny, 40),
        )(index, rest, face, other, pair, *modes, *sums, *found)
    return tuple(found)


def solution(mesh):
    in_specs = (
        P("chaos", "space", None, None),
        P("chaos", "space", None, None),
        P("space", None, None),
        P("chaos", "space", None, None),
        P(),
        P("chaos", None, None),
    )
    out_specs = (P("chaos", "space", None, None), P("chaos", "space", None, None))
    step = jax.shard_map(
        residual_and_correction, mesh=mesh, in_specs=in_specs, out_specs=out_specs, check_vma=False
    )
    if not unrolled(mesh.shape["chaos"]):
        return step
    return step
```
